128 devices in a mesh: level: 2 (over z_lo), subj: 8 (over y, core), gz: 8 (over z_hi, x).
Axes of the slice: x: 4, y: 4, z: 4 (z_hi: 2, z_lo: 2; z = z_hi * 2 + z_lo), core: 2. Of those that a mesh axis runs over, the one named last changes fastest.
Arguments:
- images: bfloat16 [16, 192, 192, 192], P('subj', 'gz'), may hold values from -6 to 6
- momenta: float32 [16, 96, 3, 96, 96], P('subj', 'gz'), may hold values from -18 to 18
- assign: int32 [16], replicated, may hold values from 0 to 15, as said below
Outputs:
- template: float32 [192, 192, 192], P('gz')
The draws below stay inside these ranges and needn't reach their ends.
Inputs may be any that keep to these rules, and one draw needn't show every extreme that they name: assign is a permutation of 0 to 15 with assign[i] % 2 == i % 2 for every i.
All inputs are finite; a program needn't handle non-finite values.
Results may differ from the reference program's by a relative error of at most 0.00069.
Values may be sent and summed in bfloat16 or wider, within the bound.
No kernel may reach another device: no remote copies, remote signals or barrier semaphores. Data moves between devices by JAX's collectives and lax.ppermute only.
A program may use at most 128 MiB of HBM per device.

```python
import jax
import jax.numpy as jnp
from jax import lax

NF = 192
NC = 96
SUBJ_DEV = 2
SWEEPS = 2
SUBJECTS = 16


def draw_assign(key, part):
    groups = SUBJECTS // SUBJ_DEV
    keys = jax.random.split(jax.random.fold_in(key, 7), SUBJ_DEV)
    orders = jax.vmap(lambda single: jax.random.permutation(single, groups))(keys)
    slots = jnp.arange(SUBJ_DEV, dtype=jnp.int32)
    table = orders.T.astype(jnp.int32) * SUBJ_DEV + slots[None, :]
    return table.reshape(SUBJECTS)


def block_levels(stream_key, dims, cuts, smallest, largest):
    level, own = 1.0, jax.random.fold_in(stream_key, 6)
    for position, parts in cuts:
        draws = jnp.exp(jax.random.uniform(jax.random.fold_in(own, position), (parts,), jnp.float32, smallest / len(cuts), largest / len(cuts)))
        level = level * jnp.repeat(draws, dims[position] // parts).reshape([-1 if axis == position else 1 for axis in range(len(dims))])
    return level


def bell_draw(stream_key, extent, deviation, limit, cuts=(), kind=jnp.bfloat16):
    entries = jax.random.normal(stream_key, extent, jnp.float32) * deviation
    if len(cuts) > 0:
        entries = block_levels(stream_key, extent, cuts, -0.22, 0.18) * entries
    return jnp.clip(entries, min=-limit, max=limit).astype(kind)


def setup_inputs(seed: int = 0) -> dict:
    key_of = jax.random.split(jax.random.key(seed), 4)
    return {
        "images": bell_draw(key_of[0], (SUBJECTS, NF, NF, NF), 1.0, 6.0, ((0, 8), (1, 8))),
        "momenta": bell_draw(key_of[1], (SUBJECTS, NC, 3, NC, NC), 3.0, 18.0, ((0, 8), (1, 8)), jnp.float32),
        "assign": draw_assign(jax.random.fold_in(key_of[3], 71), 0),
    }


def band(padded, count, axis):
    def take(offset):
        return lax.slice_in_dim(padded, offset, offset + count, axis=axis)
    return (take(0) + take(4)) * 0.0625 + (take(1) + take(3)) * 0.25 + take(2) * 0.375


def blur_plane(field, axis):
    widths = [(2, 2) if dimension == axis else (0, 0) for dimension in range(field.ndim)]
    return band(jnp.pad(field, widths), field.shape[axis], axis)


def upsample_table(finest, coarse, offset):
    rows_fine = jnp.arange(finest, dtype=jnp.int32)[:, None]
    columns = jnp.arange(coarse, dtype=jnp.int32)[None, :]
    nearest = rows_fine // 2 + offset
    farther = nearest + 2 * (rows_fine % 2) - 1
    return 0.75 * (columns == nearest).astype(jnp.float32) + 0.25 * (columns == farther).astype(jnp.float32)


def warp_slab(extended, upsampled):
    center = extended[1:-1]
    grad_z = (extended[2:] - extended[:-2]) * 0.5
    padded_y = jnp.pad(center, ((0, 0), (1, 1), (0, 0)))
    grad_y = (padded_y[:, 2:] - padded_y[:, :-2]) * 0.5
    padded_x = jnp.pad(center, ((0, 0), (0, 0), (1, 1)))
    grad_x = (padded_x[:, :, 2:] - padded_x[:, :, :-2]) * 0.5
    return center - (upsampled[:, 0] * grad_x + upsampled[:, 1] * grad_y + upsampled[:, 2] * grad_z)


def relax(extended):
    center = extended[1:-1]
    padded_y = jnp.pad(center, ((0, 0), (1, 1), (0, 0)))
    padded_x = jnp.pad(center, ((0, 0), (0, 0), (1, 1)))
    neighbours = extended[2:] + extended[:-2] + padded_y[:, 2:] + padded_y[:, :-2] + padded_x[:, :, 2:] + padded_x[:, :, :-2]
    return center + 0.15 * (neighbours - 6.0 * center)


def reference(images, momenta, assign):
    table = upsample_table(NF, NC, 0)
    highest = lax.Precision.HIGHEST

    def per_subject(total, element):
        image, source = element
        moment = lax.dynamic_index_in_dim(momenta, source, 0, keepdims=False)
        smooth = blur_plane(blur_plane(blur_plane(moment, 3), 2), 0)
        coarse_field = smooth.astype(jnp.bfloat16).astype(jnp.float32)
        section_x = jnp.einsum('zcyx,Xx->zcyX', coarse_field, table, precision=highest)
        section_y = jnp.einsum('zcyX,Yy->zcYX', section_x, table, precision=highest)
        upsampled = jnp.einsum('zcYX,Zz->ZcYX', section_y, table, precision=highest)
        extended = jnp.pad(image.astype(jnp.float32), ((1, 1), (0, 0), (0, 0)))
        return total + warp_slab(extended, upsampled), None

    start_total = jnp.zeros((NF, NF, NF), jnp.float32)
    total, _ = lax.scan(per_subject, start_total, (images, assign))
    mean = total / SUBJECTS
    for repeat in range(SWEEPS):
        mean = relax(jnp.pad(mean, ((1, 1), (0, 0), (0, 0))))
    return mean
```

```python
import jax
import jax.numpy as jnp
import numpy as np
from jax import lax
from jax.experimental import pallas as pl
from jax.experimental.pallas import tpu as pltpu
from jax.sharding import PartitionSpec as P


SWEEPS = 2
F32 = jnp.float32
BF16 = jnp.bfloat16
HZ = 12
CY = 24
CZ = HZ // 2 + 2
CW = CY // 2 + 2
VR = CZ * CW
VROWS = 6 * VR
PROWS = 80
SCALE = 128.0


def lerp_table(fine):
    table = np.zeros((fine, fine // 2 + 2), np.float32)
    for row in range(fine):
        near = row // 2 + 1
        table[row, near] += 0.75
        table[row, near + 2 * (row % 2) - 1] += 0.25
    return table


def zy_table():
    return np.kron(lerp_table(HZ), lerp_table(CY))


def x_table(fine, slot):
    inner = lerp_table(fine)[:, 1:-1].T
    coarse = fine // 2
    table = np.zeros((256, 256), np.float32)
    for base in (0, 128):
        table[base : base + coarse, :128] = inner[:, :128]
        table[base : base + coarse, 128 + 64 * slot : 192 + 64 * slot] = inner[:, 128:]
    return table


def pack_plane(plane, put):
    count = plane.shape[1] // CY
    low = [plane[0][:, :128], plane[1][:, :128]]
    both = jnp.concatenate([plane[0][:, 128:], plane[1][:, 128:]], axis=1)
    parts = low + [both]
    row = lax.broadcasted_iota(jnp.int32, (8, 128), 0)
    for peer in range(count):
        start = CY * peer
        halo = jnp.zeros((8, 128), F32)
        for index, part in enumerate(parts):
            if peer > 0:
                halo = jnp.where(row == 2 * index, part[start - 1 : start], halo)
            if peer < count - 1:
                halo = jnp.where(row == 2 * index + 1, part[start + CY : start + CY + 1], halo)
        blocks = [part[start : start + CY] for part in parts] + [halo]
        put(peer, jnp.concatenate(blocks, axis=0))


def pack_kernel(info, image, *rest):
    outs, stage = rest[:-1], rest[-1]

    def put(peer, value):
        stage[peer] = value.astype(BF16)

    pack_plane(image[:, 0].astype(F32), put)
    for k, out in enumerate(outs):
        out[0] = stage[info[1] ^ k]


def pack_images(info, images):
    grid = pltpu.PrefetchScalarGridSpec(
        num_scalar_prefetch=1,
        grid=(HZ + 1,),
        in_specs=[
            pl.BlockSpec((2, 1, 192, 192), lambda z, info: (0, (HZ - 1) * info[0] + z, 0, 0))
        ],
        out_specs=[pl.BlockSpec((1, PROWS, 128), lambda z, info: (z, 0, 0))] * 8,
        scratch_shapes=[pltpu.VMEM((8, PROWS, 128), BF16)],
    )
    return pl.pallas_call(
        pack_kernel,
        grid_spec=grid,
        out_shape=[jax.ShapeDtypeStruct((HZ + 1, PROWS, 128), BF16)] * 8,
        name="pack_images",
    )(info, images)


def blur_kernel(info, momenta, halo, image_halo, *rest):
    outs = rest[:8]
    held, stage, tall, wide, piece, sems = rest[8:]
    level, me = info[0], info[1]
    half = info[2] * 2 + level
    own = pltpu.make_async_copy(
        momenta.at[:, pl.ds(3 * level, 9)], held.at[:, pl.ds(3 - 3 * level, 9)], sems.at[0]
    )
    side = pltpu.make_async_copy(halo, held.at[:, pl.ds(9 * level, 3)], sems.at[1])
    own.start()
    side.start()

    def put(peer, value):
        stage[peer, VROWS:] = value.astype(BF16)

    pack_plane(image_halo[...].astype(F32), put)
    tall[:8] = jnp.zeros((8, 128), F32)
    tall[104:] = jnp.zeros((8, 128), F32)
    wide[:, :8] = jnp.zeros((CZ, 8, 128), F32)
    wide[:, 104:] = jnp.zeros((CZ, 8, 128), F32)
    own.wait()
    side.wait()
    first = (half > 0).astype(F32)
    last = (half < 15).astype(F32)
    spare = jnp.zeros((96, 32), F32)
    for block in range(6):
        subject, component = block // 3, block % 3

        def row(r, carry, subject=subject, component=component):
            def m(t):
                return held[subject, r + t, component]

            z = (m(0) + m(4)) * 0.0625 + (m(1) + m(3)) * 0.25 + m(2) * 0.375
            z = z * jnp.where(r == 0, first, jnp.where(r == CZ - 1, last, 1.0))
            z = jnp.concatenate([z, spare], axis=1)

            def lane(k):
                return pltpu.roll(z, k % 128, 1)

            x = (lane(2) + lane(-2)) * 0.0625 + (lane(1) + lane(-1)) * 0.25 + z * 0.375
            tall[8:104] = x
            y = (tall[6:102] + tall[10:106]) * 0.0625 + (tall[7:103] + tall[9:105]) * 0.25
            wide[r, 8:104] = y + x * 0.375
            return carry

        lax.fori_loop(0, CZ, row, 0)
        for peer in range(8):
            start = 8 + (CY // 2) * peer - 1
            for r in range(CZ):
                piece[CW * r : CW * (r + 1)] = wide[r, start : start + CW]
            stage[peer, VR * block : VR * (block + 1)] = piece[...].astype(BF16)
    for k, out in enumerate(outs):
        out[...] = stage[me ^ k]


def blur(info, momenta, halo, image_halo):
    rows = VROWS + PROWS
    return pl.pallas_call(
        blur_kernel,
        grid=(),
        in_specs=[
            pl.BlockSpec(memory_space=pltpu.SMEM),
            pl.BlockSpec(memory_space=pl.ANY),
            pl.BlockSpec(memory_space=pl.ANY),
            pl.BlockSpec(memory_space=pltpu.VMEM),
        ],
        out_specs=[pl.BlockSpec(memory_space=pltpu.VMEM)] * 8,
        out_shape=[jax.ShapeDtypeStruct((rows, 128), BF16)] * 8,
        scratch_shapes=[
            pltpu.VMEM((2, 12, 3, 96, 96), F32),
            pltpu.VMEM((8, rows, 128), BF16),
            pltpu.VMEM((112, 128), F32),
            pltpu.VMEM((CZ, 112, 128), F32),
            pltpu.VMEM((VR, 128), F32),
            pltpu.SemaphoreType.DMA((2,)),
        ],
        name="blur_momenta",
    )(info, momenta, halo, image_halo)


def warp_kernel(info, assign, zy, x0, x1, *rest):
    planes, fields = rest[:8], rest[8:16]
    chunk, edge = rest[16:18]
    image, field, velocity, acc, sems = rest[18:]
    level, me = info[0], info[1]
    copies = []
    for k in range(8):
        copies.append(
            pltpu.make_async_copy(
                planes[k], image.at[k, pl.ds(1 - level, HZ + 1)], sems.at[k]
            )
        )
        copies.append(
            pltpu.make_async_copy(fields[k].at[:VROWS], field.at[k], sems.at[8 + k])
        )
        copies.append(
            pltpu.make_async_copy(
                fields[k].at[VROWS:], image.at[k, (HZ + 1) * level], sems.at[16 + k]
            )
        )
    for copy in copies:
        copy.start()
    acc[...] = jnp.zeros_like(acc)
    for copy in copies:
        copy.wait()
    lane = lax.broadcasted_iota(jnp.int32, (CY, 128), 1)
    sub = lax.broadcasted_iota(jnp.int32, (CY, 128), 0)

    def pair(k, carry):
        base = 2 * (me ^ k)
        slots = [(assign[base + j] // 2) ^ me for j in range(2)]
        for c in range(3):
            parts = [
                field[slots[j], VR * (3 * j + c) : VR * (3 * j + c + 1)] for j in range(2)
            ]
            rough = jnp.dot(
                zy[...], jnp.concatenate(parts, axis=1), preferred_element_type=F32
            )
            high = rough.astype(BF16)
            low = (rough - high.astype(F32)).astype(BF16)
            total = None
            for j, table in enumerate((x0, x1)):
                own = slice(128 * j, 128 * j + 128)
                left = jnp.concatenate([high[:, own], low[:, own]], axis=1)
                fine = jnp.dot(left, table[...], preferred_element_type=F32)
                velocity[c, j] = fine[:, :128]
                total = fine[:, 128:] if total is None else total + fine[:, 128:]
            velocity[c, 2] = total

        def slab(z, carry):
            before = image[k, z].astype(F32)
            centre = image[k, z + 1].astype(F32)
            after = image[k, z + 2].astype(F32)
            part = [centre[CY * b : CY * (b + 1)] for b in range(3)]
            halo = centre[3 * CY :]
            rows = pl.ds(pl.multiple_of(z * CY, 8), CY)
            left0 = jnp.where(lane == 0, 0.0, pltpu.roll(part[0], 1, 1))
            left1 = jnp.where(lane == 0, 0.0, pltpu.roll(part[1], 1, 1))
            right0 = jnp.where(lane == 127, pltpu.roll(part[2], 127, 1), pltpu.roll(part[0], 127, 1))
            right1 = jnp.where(lane == 127, pltpu.roll(part[2], 63, 1), pltpu.roll(part[1], 127, 1))
            left2 = jnp.where(
                lane == 0,
                pltpu.roll(part[0], 1, 1),
                jnp.where(lane == 64, pltpu.roll(part[1], 65, 1), pltpu.roll(part[2], 1, 1)),
            )
            right2 = jnp.where(lane % 64 == 63, 0.0, pltpu.roll(part[2], 127, 1))
            sides = ((left0, right0), (left1, right1), (left2, right2))
            warped = []
            for b in range(3):
                own = slice(CY * b, CY * (b + 1))
                up = jnp.where(sub == 0, halo[2 * b : 2 * b + 1], pltpu.roll(part[b], 1, 0))
                down = jnp.where(
                    sub == CY - 1, halo[2 * b + 1 : 2 * b + 2], pltpu.roll(part[b], CY - 1, 0)
                )
                push = velocity[0, b, rows] * (sides[b][1] - sides[b][0])
                push += velocity[1, b, rows] * (down - up)
                push += velocity[2, b, rows] * (after[own] - before[own])
                warped.append(part[b] - 0.5 * push)
            acc[0, rows] = acc[0, rows] + (warped[0] + warped[1])
            acc[1, rows] = acc[1, rows] + warped[2]
            return carry

        lax.fori_loop(0, HZ, slab, 0)
        return carry

    lax.fori_loop(0, 8, pair, 0)
    weight = SCALE / 16.0
    chunk[: HZ * CY] = acc[0] * weight
    wide = lax.broadcasted_iota(jnp.int32, (CY, 128), 1)

    def joined(z, other):
        one, two = (acc[1, pl.ds(pl.multiple_of(r * CY, 8), CY)] for r in (z, other))
        one = one + pltpu.roll(one, 64, 1)
        two = two + pltpu.roll(two, 64, 1)
        return jnp.where(wide < 64, one, two) * weight

    for z in range(HZ // 2):
        chunk[(HZ + z) * CY : (HZ + z + 1) * CY] = joined(z, z + HZ // 2)
    outer = (HZ - 2) * level
    edge[: 2 * CY] = acc[0, pl.ds(pl.multiple_of(outer * CY, 8), 2 * CY)] * weight
    edge[2 * CY :] = joined(outer, outer + 1)


def warp(info, assign, planes, fields):
    tables = [
        jnp.asarray(t, BF16) for t in (zy_table(), x_table(192, 0), x_table(192, 1))
    ]
    vmem = pl.BlockSpec(memory_space=pltpu.VMEM)
    smem = pl.BlockSpec(memory_space=pltpu.SMEM)
    hbm = pl.BlockSpec(memory_space=pl.ANY)
    return pl.pallas_call(
        warp_kernel,
        grid=(),
        in_specs=[smem, smem, vmem, vmem, vmem] + [hbm] * 16,
        out_specs=[vmem] * 2,
        out_shape=[
            jax.ShapeDtypeStruct((HZ * CY * 3 // 2, 128), F32),
            jax.ShapeDtypeStruct((3 * CY, 128), F32),
        ],
        scratch_shapes=[
            pltpu.VMEM((8, HZ + 2, PROWS, 128), BF16),
            pltpu.VMEM((8, VROWS, 128), BF16),
            pltpu.VMEM((3, 3, HZ * CY, 128), F32),
            pltpu.VMEM((2, HZ * CY, 128), F32),
            pltpu.SemaphoreType.DMA((24,)),
        ],
        name="warp_sum",
    )(info, assign, *tables, *planes, *fields)


def relax_kernel(info, chunks, out, now, later):
    level, me, zone = info[0], info[1], info[2]
    size = now.shape[1] - 16
    for held in (now, later):
        held[:, :8] = jnp.zeros((held.shape[0], 8, 256), F32)
        held[:, size + 8 :] = jnp.zeros((held.shape[0], 8, 256), F32)
    lane = lax.broadcasted_iota(jnp.int32, (CY, 128), 1)
    for half in range(2):
        for peer in range(8):
            slot = (half ^ level) * 8 + (peer ^ me)
            rows = slice(8 + CY * peer, 8 + CY * (peer + 1))
            for z in range(HZ):
                now[2 + HZ * half + z, rows, :128] = chunks[slot, CY * z : CY * (z + 1)]
            outer = 26 * half
            pairs = [(HZ + z, 2 + HZ * half + z, 2 + HZ * half + z + HZ // 2) for z in range(HZ // 2)]
            tail = HZ * 3 // 2
            for z in range(2):
                now[outer + z, rows, :128] = chunks[slot, CY * (tail + z) : CY * (tail + z + 1)]
            pairs.append((tail + 2, outer, outer + 1))
            for source, one, two in pairs:
                both = chunks[slot, CY * source : CY * (source + 1)]
                now[one, rows, 128:] = jnp.where(lane < 64, both, 0.0)
                now[two, rows, 128:] = jnp.where(lane < 64, pltpu.roll(both, 64, 1), 0.0)
    wide = lax.broadcasted_iota(jnp.int32, (size, 256), 1)

    def swept(held, z):
        centre = held[z, 8 : 8 + size]
        around = held[z - 1, 8 : 8 + size] + held[z + 1, 8 : 8 + size]
        around += held[z, 7 : 7 + size] + held[z, 9 : 9 + size]
        around += pltpu.roll(centre, 1, 1) + pltpu.roll(centre, 255, 1)
        return centre + 0.15 * (around - 6.0 * centre)

    def first(z, carry):
        inside = jnp.logical_and(
            jnp.logical_or(z > 1, zone > 0), jnp.logical_or(z < 26, zone < 7)
        )
        keep = jnp.where(inside, 192, 0)
        later[z, 8 : 8 + size] = jnp.where(wide < keep, swept(now, z), 0.0)
        return carry

    def second(z, carry):
        out[z - 2] = swept(later, z)[:, :size] * (1.0 / SCALE)
        return carry

    lax.fori_loop(1, 27, first, 0)
    lax.fori_loop(2, 26, second, 0)


def relax(info, chunks):
    vmem = pl.BlockSpec(memory_space=pltpu.VMEM)
    return pl.pallas_call(
        relax_kernel,
        grid=(),
        in_specs=[pl.BlockSpec(memory_space=pltpu.SMEM), vmem],
        out_specs=vmem,
        out_shape=jax.ShapeDtypeStruct((24, 192, 192), F32),
        scratch_shapes=[pltpu.VMEM((28, 208, 256), F32)] * 2,
        name="relax",
    )(info, chunks)


def shards(images, momenta, assign):
    level = lax.axis_index("level")
    me = lax.axis_index("subj")
    zone = lax.axis_index("gz")
    info = jnp.stack([level, me, zone]).astype(jnp.int32)
    zones = lax.axis_size("gz")
    outward = [(g, g + 1) for g in range(zones - 1)]
    outward += [(zones + g + 1, zones + g) for g in range(zones - 1)]
    nearest = ("level", "gz")
    image_rim = lax.dynamic_slice_in_dim(images, 23 * (1 - level), 1, axis=1)[:, 0]
    rim = lax.dynamic_slice_in_dim(momenta, 9 * (1 - level), 3, axis=1)
    image_rim = lax.ppermute(image_rim, nearest, outward)
    rim = lax.ppermute(rim, nearest, outward)

    def spread(parts):
        return [parts[0]] + [
            lax.ppermute(parts[k], "subj", [(i, i ^ k) for i in range(8)]) for k in range(1, 8)
        ]

    planes = spread(pack_images(info, images))
    fields = spread(blur(info, momenta, rim, image_rim))
    chunk, edge = warp(info, assign, planes, fields)
    cross = [(zones + g, g + 1) for g in range(zones - 1)]
    cross += [(g + 1, zones + g) for g in range(zones - 1)]
    edge = lax.ppermute(edge.astype(jnp.float16), nearest, cross)
    chunk = jnp.concatenate([chunk.astype(jnp.float16), edge], axis=0)
    gathered = []
    for far in range(2):
        for step in range(4):
            part = chunk
            if far or step:
                perm = [
                    (8 * a + i, 8 * (a ^ far) + (i ^ (2 * step))) for a in range(2) for i in range(8)
                ]
                part = lax.ppermute(chunk, ("level", "subj"), perm)
            gathered.append(part)
            gathered.append(lax.ppermute(part, "subj", [(i, i ^ 1) for i in range(8)]))
    chunks = jnp.stack(gathered).astype(F32)
    return relax(info, chunks)


def solution(mesh):
    return jax.shard_map(
        shards,
        mesh=mesh,
        in_specs=(P("subj", "gz", None, None), P("subj", "gz", None, None, None), P()),
        out_specs=P("gz", None, None),
        check_vma=False,
    )
```

```python
import jax
import jax.numpy as jnp
import numpy as np
from jax import lax
from jax.experimental import pallas as pl
from jax.experimental.pallas import tpu as pltpu
from jax.sharding import PartitionSpec as P


SWEEPS = 2
F32 = jnp.float32
BF16 = jnp.bfloat16
HZ = 12
CY = 24
CZ = HZ // 2 + 2
CW = CY // 2 + 2
VR = CZ * CW
VROWS = 6 * VR
PROWS = 80
SCALE = 128.0


def lerp_table(fine):
    table = np.zeros((fine, fine // 2 + 2), np.float32)
    for row in range(fine):
        near = row // 2 + 1
        table[row, near] += 0.75
        table[row, near + 2 * (row % 2) - 1] += 0.25
    return table


def zy_table():
    return np.kron(lerp_table(HZ), lerp_table(CY))


def x_table(fine, slot):
    inner = lerp_table(fine)[:, 1:-1].T
    coarse = fine // 2
    table = np.zeros((256, 256), np.float32)
    for base in (0, 128):
        table[base : base + coarse, :128] = inner[:, :128]
        table[base : base + coarse, 128 + 64 * slot : 192 + 64 * slot] = inner[:, 128:]
    return table


def pack_plane(plane, put):
    count = plane.shape[1] // CY
    low = [plane[0][:, :128], plane[1][:, :128]]
    both = jnp.concatenate([plane[0][:, 128:], plane[1][:, 128:]], axis=1)
    parts = low + [both]
    row = lax.broadcasted_iota(jnp.int32, (8, 128), 0)
    for peer in range(count):
        start = CY * peer
        halo = jnp.zeros((8, 128), F32)
        for index, part in enumerate(parts):
            if peer > 0:
                halo = jnp.where(row == 2 * index, part[start - 1 : start], halo)
            if peer < count - 1:
                halo = jnp.where(row == 2 * index + 1, part[start + CY : start + CY + 1], halo)
        blocks = [part[start : start + CY] for part in parts] + [halo]
        put(peer, jnp.concatenate(blocks, axis=0))


GROUPS = ((0, 4), (4, 3), (7, 3), (10, 3))


def pack_kernel(info, images, momenta, *rest):
    outs, image_rim, rim = rest[:8], rest[8], rest[9]
    held, stage, sems, gone, side = rest[10:]
    level, me = info[0], info[1]
    sides = [
        pltpu.make_async_copy(momenta.at[:, pl.ds(9 - 9 * level, 3)], rim, side.at[0]),
        pltpu.make_async_copy(images.at[:, 23 - 23 * level], image_rim, side.at[1]),
    ]
    loads = []
    for index, (first, count) in enumerate(GROUPS):
        rows = pl.ds((HZ - 1) * level + first, count)
        loads.append(
            pltpu.make_async_copy(
                images.at[:, rows], held.at[:, pl.ds(first, count)], sems.at[index]
            )
        )
    for copy in loads + sides:
        copy.start()
    sent = []
    for index, (first, count) in enumerate(GROUPS):
        loads[index].wait()

        def step(z, carry):
            def put(peer, value):
                stage[peer, z] = value.astype(BF16)

            pack_plane(held[:, z].astype(F32), put)
            return carry

        lax.fori_loop(first, first + count, step, 0)
        for k, out in enumerate(outs):
            rows = pl.ds(first, count)
            copy = pltpu.make_async_copy(
                stage.at[me ^ k, rows], out.at[rows], gone.at[8 * index + k]
            )
            copy.start()
            sent.append(copy)
    for copy in sides + sent:
        copy.wait()


def pack_images(info, images, momenta):
    hbm = pl.BlockSpec(memory_space=pl.ANY)
    return pl.pallas_call(
        pack_kernel,
        grid=(),
        in_specs=[pl.BlockSpec(memory_space=pltpu.SMEM), hbm, hbm],
        out_specs=[hbm] * 10,
        out_shape=[jax.ShapeDtypeStruct((HZ + 1, PROWS, 128), BF16)] * 8
        + [
            jax.ShapeDtypeStruct((2, 192, 192), BF16),
            jax.ShapeDtypeStruct((2, 3, 3, 96, 96), F32),
        ],
        scratch_shapes=[
            pltpu.VMEM((2, HZ + 1, 192, 192), BF16),
            pltpu.VMEM((8, HZ + 1, PROWS, 128), BF16),
            pltpu.SemaphoreType.DMA((len(GROUPS),)),
            pltpu.SemaphoreType.DMA((8 * len(GROUPS),)),
            pltpu.SemaphoreType.DMA((2,)),
        ],
        name="pack_images",
    )(info, images, momenta)


def blur_kernel(info, momenta, halo, image_halo, *rest):
    outs = rest[:8]
    held, stage, tall, wide, piece, sems, gone = rest[8:]
    level, me = info[0], info[1]
    half = info[2] * 2 + level
    own = pltpu.make_async_copy(
        momenta.at[:, pl.ds(3 * level, 9)], held.at[:, pl.ds(3 - 3 * level, 9)], sems.at[0]
    )
    side = pltpu.make_async_copy(halo, held.at[:, pl.ds(9 * level, 3)], sems.at[1])
    own.start()
    side.start()

    def put(peer, value):
        stage[peer, VROWS:] = value.astype(BF16)

    pack_plane(image_halo[...].astype(F32), put)
    for held_rows in (tall, wide):
        held_rows[:, :8] = jnp.zeros((CZ, 8, 128), F32)
        held_rows[:, 104:] = jnp.zeros((CZ, 8, 128), F32)
    own.wait()
    side.wait()
    first = (half > 0).astype(F32)
    last = (half < 15).astype(F32)
    spare = jnp.zeros((96, 32), F32)
    for block in range(6):
        subject, component = block // 3, block % 3

        def row(r, carry, subject=subject, component=component):
            def m(t):
                return held[subject, r + t, component]

            z = (m(0) + m(4)) * 0.0625 + (m(1) + m(3)) * 0.25 + m(2) * 0.375
            z = z * jnp.where(r == 0, first, jnp.where(r == CZ - 1, last, 1.0))
            z = jnp.concatenate([z, spare], axis=1)

            def lane(k):
                return pltpu.roll(z, k % 128, 1)

            x = (lane(2) + lane(-2)) * 0.0625 + (lane(1) + lane(-1)) * 0.25 + z * 0.375
            tall[r, 8:104] = x
            y = (tall[r, 6:102] + tall[r, 10:106]) * 0.0625
            y += (tall[r, 7:103] + tall[r, 9:105]) * 0.25
            wide[r, 8:104] = y + x * 0.375
            return carry

        lax.fori_loop(0, CZ, row, 0, unroll=2)
        for peer in range(8):
            start = 8 + (CY // 2) * peer - 1
            for r in range(CZ):
                piece[CW * r : CW * (r + 1)] = wide[r, start : start + CW]
            stage[peer, VR * block : VR * (block + 1)] = piece[...].astype(BF16)
    sent = [
        pltpu.make_async_copy(stage.at[me ^ k], out, gone.at[k]) for k, out in enumerate(outs)
    ]
    for copy in sent:
        copy.start()
    for copy in sent:
        copy.wait()


def blur(info, momenta, halo, image_halo):
    rows = VROWS + PROWS
    return pl.pallas_call(
        blur_kernel,
        grid=(),
        in_specs=[
            pl.BlockSpec(memory_space=pltpu.SMEM),
            pl.BlockSpec(memory_space=pl.ANY),
            pl.BlockSpec(memory_space=pl.ANY),
            pl.BlockSpec(memory_space=pltpu.VMEM),
        ],
        out_specs=[pl.BlockSpec(memory_space=pl.ANY)] * 8,
        out_shape=[jax.ShapeDtypeStruct((rows, 128), BF16)] * 8,
        scratch_shapes=[
            pltpu.VMEM((2, 12, 3, 96, 96), F32),
            pltpu.VMEM((8, rows, 128), BF16),
            pltpu.VMEM((CZ, 112, 128), F32),
            pltpu.VMEM((CZ, 112, 128), F32),
            pltpu.VMEM((VR, 128), F32),
            pltpu.SemaphoreType.DMA((2,)),
            pltpu.SemaphoreType.DMA((8,)),
        ],
        name="blur_momenta",
    )(info, momenta, halo, image_halo)


def warp_kernel(info, assign, zy, x0, x1, *rest):
    planes, fields = rest[:8], rest[8:16]
    chunk, edge = rest[16:18]
    image, field, even, odd, acc, sems = rest[18:]
    level, me = info[0], info[1]
    copies = []
    for k in range(8):
        copies.append(
            pltpu.make_async_copy(
                planes[k], image.at[k, pl.ds(1 - level, HZ + 1)], sems.at[k]
            )
        )
        copies.append(
            pltpu.make_async_copy(fields[k].at[:VROWS], field.at[k], sems.at[8 + k])
        )
        copies.append(
            pltpu.make_async_copy(
                fields[k].at[VROWS:], image.at[k, (HZ + 1) * level], sems.at[16 + k]
            )
        )
    for copy in copies:
        copy.start()
    acc[...] = jnp.zeros_like(acc)
    for copy in copies:
        copy.wait()
    lane = lax.broadcasted_iota(jnp.int32, (CY, 128), 1)
    sub = lax.broadcasted_iota(jnp.int32, (CY, 128), 0)

    def neighbours(part):
        left0, left1, left2 = (pltpu.roll(p, 1, 1) for p in part)
        right0, right1, right2 = (pltpu.roll(p, 127, 1) for p in part)
        left2 = jnp.where(lane == 0, left0, jnp.where(lane == 64, pltpu.roll(part[1], 65, 1), left2))
        left0 = jnp.where(lane == 0, 0.0, left0)
        left1 = jnp.where(lane == 0, 0.0, left1)
        right0 = jnp.where(lane == 127, right2, right0)
        right1 = jnp.where(lane == 127, pltpu.roll(part[2], 63, 1), right1)
        right2 = jnp.where(lane % 64 == 63, 0.0, right2)
        return (left0, left1, left2), (right0, right1, right2)

    def interpolate(k, velocity):
        base = 2 * (me ^ k)
        slots = [(assign[base + j] // 2) ^ me for j in range(2)]
        stacked = [[], []]
        for c in range(3):
            parts = [
                field[slots[j], VR * (3 * j + c) : VR * (3 * j + c + 1)] for j in range(2)
            ]
            rough = jnp.dot(
                zy[...], jnp.concatenate(parts, axis=1), preferred_element_type=F32
            )
            high = rough.astype(BF16)
            low = (rough - high.astype(F32)).astype(BF16)
            for j in range(2):
                own = slice(128 * j, 128 * j + 128)
                stacked[j].append(jnp.concatenate([high[:, own], low[:, own]], axis=1))
        fine = [
            jnp.dot(jnp.concatenate(stacked[j], axis=0), table[...], preferred_element_type=F32)
            for j, table in enumerate((x0, x1))
        ]
        velocity[0] = fine[0][:, :128]
        velocity[1] = fine[1][:, :128]
        velocity[2] = fine[0][:, 128:] + fine[1][:, 128:]

    def apply(k, velocity):
        for z in range(HZ):
            before = image[k, z].astype(F32)
            centre = image[k, z + 1].astype(F32)
            after = image[k, z + 2].astype(F32)
            part = [centre[CY * b : CY * (b + 1)] for b in range(3)]
            halo = centre[3 * CY :]
            left, right = neighbours(part)
            warped = []
            for b in range(3):
                own = slice(CY * b, CY * (b + 1))
                up = jnp.where(sub == 0, halo[2 * b : 2 * b + 1], pltpu.roll(part[b], 1, 0))
                down = jnp.where(
                    sub == CY - 1, halo[2 * b + 1 : 2 * b + 2], pltpu.roll(part[b], CY - 1, 0)
                )

                def v(c):
                    start = HZ * CY * c + CY * z
                    return velocity[b, start : start + CY]

                push = v(0) * (right[b] - left[b]) + v(1) * (down - up)
                push += v(2) * (after[own] - before[own])
                warped.append(part[b] - 0.5 * push)
            rows = slice(CY * z, CY * (z + 1))
            acc[0, rows] += warped[0] + warped[1]
            acc[1, rows] += warped[2]

    interpolate(0, even)

    def turn(step, carry):
        interpolate(2 * step + 1, odd)
        apply(2 * step, even)
        interpolate(jnp.minimum(2 * step + 2, 7), even)
        apply(2 * step + 1, odd)
        return carry

    lax.fori_loop(0, 4, turn, 0)
    weight = SCALE / 16.0
    chunk[: HZ * CY] = acc[0] * weight
    wide = lax.broadcasted_iota(jnp.int32, (CY, 128), 1)

    def joined(z, other):
        one, two = (acc[1, pl.ds(pl.multiple_of(r * CY, 8), CY)] for r in (z, other))
        one = one + pltpu.roll(one, 64, 1)
        two = two + pltpu.roll(two, 64, 1)
        return jnp.where(wide < 64, one, two) * weight

    for z in range(HZ // 2):
        chunk[(HZ + z) * CY : (HZ + z + 1) * CY] = joined(z, z + HZ // 2)
    outer = (HZ - 2) * level
    edge[: 2 * CY] = acc[0, pl.ds(pl.multiple_of(outer * CY, 8), 2 * CY)] * weight
    edge[2 * CY :] = joined(outer, outer + 1)


def warp(info, assign, planes, fields):
    tables = [
        jnp.asarray(t, BF16) for t in (zy_table(), x_table(192, 0), x_table(192, 1))
    ]
    vmem = pl.BlockSpec(memory_space=pltpu.VMEM)
    smem = pl.BlockSpec(memory_space=pltpu.SMEM)
    hbm = pl.BlockSpec(memory_space=pl.ANY)
    return pl.pallas_call(
        warp_kernel,
        grid=(),
        in_specs=[smem, smem, vmem, vmem, vmem] + [hbm] * 16,
        out_specs=[vmem] * 2,
        out_shape=[
            jax.ShapeDtypeStruct((HZ * CY * 3 // 2, 128), F32),
            jax.ShapeDtypeStruct((3 * CY, 128), F32),
        ],
        scratch_shapes=[
            pltpu.VMEM((8, HZ + 2, PROWS, 128), BF16),
            pltpu.VMEM((8, VROWS, 128), BF16),
            pltpu.VMEM((3, 3 * HZ * CY, 128), F32),
            pltpu.VMEM((3, 3 * HZ * CY, 128), F32),
            pltpu.VMEM((2, HZ * CY, 128), F32),
            pltpu.SemaphoreType.DMA((24,)),
        ],
        name="warp_sum",
    )(info, assign, *tables, *planes, *fields)


def relax_kernel(info, chunks, out, flat, pair, flat2, pair2, ready, sems):
    level, me, zone = info[0], info[1], info[2]
    size = flat.shape[1] - 16
    for held in (flat, pair, flat2, pair2):
        held[:, :8] = jnp.zeros((held.shape[0], 8, 128), F32)
        held[:, size + 8 :] = jnp.zeros((held.shape[0], 8, 128), F32)
    for held in (flat, flat2):
        for z in (0, held.shape[0] - 1):
            held[z, 8 : 8 + size] = jnp.zeros((size, 128), F32)
    narrow = lax.broadcasted_iota(jnp.int32, (CY, 128), 1)
    tail = HZ * 3 // 2
    for peer in range(8):
        rows = slice(8 + CY * peer, 8 + CY * (peer + 1))
        slots = [(half ^ level) * 8 + (peer ^ me) for half in range(2)]

        def block(half, index):
            return chunks[slots[half], CY * index : CY * (index + 1)]

        for half in range(2):
            for z in range(HZ):
                flat[3 + HZ * half + z, rows] = block(half, z)
            for z in range(2):
                flat[1 + 26 * half + z, rows] = block(half, tail + z)
        packed = [HZ + z % (HZ // 2) for z in range(HZ)]
        sides = [z // (HZ // 2) for z in range(HZ)]
        lows = [(tail + 2, 0), (tail + 2, 1)] + list(zip(packed, sides))
        highs = list(zip(packed, sides)) + [(tail + 2, 0), (tail + 2, 1)]
        for index in range(14):
            low, high = block(0, lows[index][0]), block(1, highs[index][0])
            if lows[index][1] == 1:
                low = pltpu.roll(low, 64, 1)
            if highs[index][1] == 0:
                high = pltpu.roll(high, 64, 1)
            pair[1 + index, rows] = jnp.where(narrow < 64, low, high)

    def mirror(held):
        held[0, 8 : 8 + size] = pltpu.roll(held[14, 8 : 8 + size], 64, 1)
        held[15, 8 : 8 + size] = pltpu.roll(held[1, 8 : 8 + size], 64, 1)

    mirror(pair)
    count = 2 * CY
    lane = lax.broadcasted_iota(jnp.int32, (count, 128), 1)

    def swept(planes, index, start, scale):
        refs = [(planes[0], index), (planes[0], index + 14), (planes[1], index)]
        part = [held[z, start : start + count] for held, z in refs]
        left = [pltpu.roll(p, 1, 1) for p in part]
        right = [pltpu.roll(p, 127, 1) for p in part]
        left[2] = jnp.where(
            lane == 0, left[0], jnp.where(lane == 64, pltpu.roll(part[1], 65, 1), left[2])
        )
        left[0] = jnp.where(lane == 0, 0.0, left[0])
        left[1] = jnp.where(lane == 0, 0.0, left[1])
        right[0] = jnp.where(lane == 127, right[2], right[0])
        right[1] = jnp.where(lane == 127, pltpu.roll(part[2], 63, 1), right[1])
        right[2] = jnp.where(lane % 64 == 63, 0.0, right[2])
        done = []
        for b, (held, z) in enumerate(refs):
            around = held[z - 1, start : start + count] + held[z + 1, start : start + count]
            around += held[z, start - 1 : start - 1 + count] + held[z, start + 1 : start + 1 + count]
            around += left[b] + right[b]
            done.append((0.1 * scale) * part[b] + (0.15 * scale) * around)
        return done

    def first(index, carry):
        for start in range(8, 8 + size, count):
            done = swept((flat, pair), index, start, 1.0)
            flat2[index, start : start + count] = done[0]
            flat2[index + 14, start : start + count] = done[1]
            pair2[index, start : start + count] = done[2]
        return carry

    lax.fori_loop(1, 15, first, 0)
    whole = lax.broadcasted_iota(jnp.int32, (size, 128), 1)

    @pl.when(zone == 0)
    def _():
        flat2[2, 8 : 8 + size] = jnp.zeros((size, 128), F32)
        pair2[2, 8 : 8 + size] = jnp.where(whole < 64, 0.0, pair2[2, 8 : 8 + size])

    @pl.when(zone == 7)
    def _():
        flat2[27, 8 : 8 + size] = jnp.zeros((size, 128), F32)
        pair2[13, 8 : 8 + size] = jnp.where(whole < 64, pair2[13, 8 : 8 + size], 0.0)

    mirror(pair2)

    def emit(z):
        return pltpu.make_async_copy(ready.at[z + 2], out.at[z], sems.at[z])

    def second(index, carry):
        for start in range(8, 8 + size, count):
            done = swept((flat2, pair2), index, start, 1.0 / SCALE)
            rows = slice(start - 8, start - 8 + count)
            ready[index - 1, rows, :128] = done[0]
            ready[index - 1, rows, 128:] = done[2][:, :64]
            ready[index + 13, rows, :128] = done[1]
            ready[index + 13, rows, 128:] = pltpu.roll(done[2], 64, 1)[:, :64]

        @pl.when(index >= 3)
        def _():
            emit(index - 3).start()

        @pl.when(index <= 12)
        def _():
            emit(index + 11).start()

        return carry

    lax.fori_loop(1, 15, second, 0)

    def finish(z, carry):
        emit(z).wait()
        return carry

    lax.fori_loop(0, 24, finish, 0)


def relax(info, chunks):
    vmem = pl.BlockSpec(memory_space=pltpu.VMEM)
    return pl.pallas_call(
        relax_kernel,
        grid=(),
        in_specs=[pl.BlockSpec(memory_space=pltpu.SMEM), vmem],
        out_specs=pl.BlockSpec(memory_space=pl.ANY),
        out_shape=jax.ShapeDtypeStruct((24, 192, 192), F32),
        scratch_shapes=[
            pltpu.VMEM((30, 208, 128), F32),
            pltpu.VMEM((16, 208, 128), F32),
            pltpu.VMEM((30, 208, 128), F32),
            pltpu.VMEM((16, 208, 128), F32),
            pltpu.VMEM((28, 192, 192), F32),
            pltpu.SemaphoreType.DMA((24,)),
        ],
        name="relax",
    )(info, chunks)


def shards(images, momenta, assign):
    level = lax.axis_index("level")
    me = lax.axis_index("subj")
    zone = lax.axis_index("gz")
    info = jnp.stack([level, me, zone]).astype(jnp.int32)
    zones = lax.axis_size("gz")
    outward = [(g, g + 1) for g in range(zones - 1)]
    outward += [(zones + g + 1, zones + g) for g in range(zones - 1)]
    nearest = ("level", "gz")
    *packed, image_rim, rim = pack_images(info, images, momenta)
    image_rim = lax.ppermute(image_rim, nearest, outward)
    rim = lax.ppermute(rim, nearest, outward)

    def spread(parts):
        return [parts[0]] + [
            lax.ppermute(parts[k], "subj", [(i, i ^ k) for i in range(8)]) for k in range(1, 8)
        ]

    planes = spread(packed)
    fields = spread(blur(info, momenta, rim, image_rim))
    chunk, edge = warp(info, assign, planes, fields)
    cross = [(zones + g, g + 1) for g in range(zones - 1)]
    cross += [(g + 1, zones + g) for g in range(zones - 1)]
    edge = lax.ppermute(edge.astype(jnp.float16), nearest, cross)
    chunk = jnp.concatenate([chunk.astype(jnp.float16), edge], axis=0)
    gathered = []
    for far in range(2):
        for step in range(4):
            part = chunk
            if far or step:
                perm = [
                    (8 * a + i, 8 * (a ^ far) + (i ^ (2 * step))) for a in range(2) for i in range(8)
                ]
                part = lax.ppermute(chunk, ("level", "subj"), perm)
            gathered.append(part)
            gathered.append(lax.ppermute(part, "subj", [(i, i ^ 1) for i in range(8)]))
    chunks = jnp.stack(gathered).astype(F32)
    return relax(info, chunks)


def solution(mesh):
    return jax.shard_map(
        shards,
        mesh=mesh,
        in_specs=(P("subj", "gz", None, None), P("subj", "gz", None, None, None), P()),
        out_specs=P("gz", None, None),
        check_vma=False,
    )
```

```python
import jax
import jax.numpy as jnp
import numpy as np
from jax import lax
from jax.experimental import pallas as pl
from jax.experimental.pallas import tpu as pltpu
from jax.sharding import PartitionSpec as P


SWEEPS = 2
F32 = jnp.float32
BF16 = jnp.bfloat16
HZ = 12
CY = 24
CZ = HZ // 2 + 2
CW = CY // 2 + 2
VR = CZ * CW
VROWS = 6 * VR
PROWS = 80
SCALE = 128.0


def lerp_table(fine):
    table = np.zeros((fine, fine // 2 + 2), np.float32)
    for row in range(fine):
        near = row // 2 + 1
        table[row, near] += 0.75
        table[row, near + 2 * (row % 2) - 1] += 0.25
    return table


def zy_table():
    return np.kron(lerp_table(HZ), lerp_table(CY))


def x_table(fine, slot):
    inner = lerp_table(fine)[:, 1:-1].T
    coarse = fine // 2
    table = np.zeros((256, 256), np.float32)
    for base in (0, 128):
        table[base : base + coarse, :128] = inner[:, :128]
        table[base : base + coarse, 128 + 64 * slot : 192 + 64 * slot] = inner[:, 128:]
    return table


def pack_plane(plane, put):
    count = plane.shape[1] // CY
    low = [plane[0][:, :128], plane[1][:, :128]]
    both = jnp.concatenate([plane[0][:, 128:], plane[1][:, 128:]], axis=1)
    parts = low + [both]
    row = lax.broadcasted_iota(jnp.int32, (8, 128), 0)
    for peer in range(count):
        start = CY * peer
        halo = jnp.zeros((8, 128), F32)
        for index, part in enumerate(parts):
            if peer > 0:
                halo = jnp.where(row == 2 * index, part[start - 1 : start], halo)
            if peer < count - 1:
                halo = jnp.where(row == 2 * index + 1, part[start + CY : start + CY + 1], halo)
        blocks = [part[start : start + CY] for part in parts] + [halo]
        put(peer, jnp.concatenate(blocks, axis=0))


GROUPS = ((0, 4), (4, 3), (7, 3), (10, 3))


def pack_kernel(info, images, momenta, *rest):
    outs, image_rim, rim = rest[:8], rest[8], rest[9]
    held, stage, edge, image_edge, sems, gone, side = rest[10:]
    level, me = info[0], info[1]
    sides = [
        pltpu.make_async_copy(momenta.at[:, pl.ds(9 - 9 * level, 3)], edge, side.at[0]),
        pltpu.make_async_copy(images.at[:, 23 - 23 * level], image_edge, side.at[1]),
    ]
    leaving = [
        pltpu.make_async_copy(edge, rim, side.at[2]),
        pltpu.make_async_copy(image_edge, image_rim, side.at[3]),
    ]
    loads = []
    for index, (first, count) in enumerate(GROUPS):
        rows = pl.ds((HZ - 1) * level + first, count)
        loads.append(
            pltpu.make_async_copy(
                images.at[:, rows], held.at[:, pl.ds(first, count)], sems.at[index]
            )
        )
    for copy in loads + sides:
        copy.start()
    sent = []
    for index, (first, count) in enumerate(GROUPS):
        loads[index].wait()

        def step(z, carry):
            def put(peer, value):
                stage[peer, z] = value.astype(BF16)

            pack_plane(held[:, z].astype(F32), put)
            return carry

        lax.fori_loop(first, first + count, step, 0)
        for k, out in enumerate(outs):
            rows = pl.ds(first, count)
            copy = pltpu.make_async_copy(
                stage.at[me ^ k, rows], out.at[rows], gone.at[8 * index + k]
            )
            copy.start()
            sent.append(copy)
        if index == 0:
            for arriving, copy in zip(sides, leaving):
                arriving.wait()
                copy.start()
    for copy in leaving + sent:
        copy.wait()


def pack_images(info, images, momenta):
    hbm = pl.BlockSpec(memory_space=pl.ANY)
    return pl.pallas_call(
        pack_kernel,
        grid=(),
        in_specs=[pl.BlockSpec(memory_space=pltpu.SMEM), hbm, hbm],
        out_specs=[hbm] * 10,
        out_shape=[jax.ShapeDtypeStruct((HZ + 1, PROWS, 128), BF16)] * 8
        + [
            jax.ShapeDtypeStruct((2, 192, 192), BF16),
            jax.ShapeDtypeStruct((2, 3, 3, 96, 96), F32),
        ],
        scratch_shapes=[
            pltpu.VMEM((2, HZ + 1, 192, 192), BF16),
            pltpu.VMEM((8, HZ + 1, PROWS, 128), BF16),
            pltpu.VMEM((2, 3, 3, 96, 96), F32),
            pltpu.VMEM((2, 192, 192), BF16),
            pltpu.SemaphoreType.DMA((len(GROUPS),)),
            pltpu.SemaphoreType.DMA((8 * len(GROUPS),)),
            pltpu.SemaphoreType.DMA((4,)),
        ],
        name="pack_images",
    )(info, images, momenta)


def blur_kernel(info, momenta, halo, image_halo, *rest):
    outs = rest[:8]
    held, stage, tall, wide, piece, sems, gone = rest[8:]
    level, me = info[0], info[1]
    half = info[2] * 2 + level
    own = pltpu.make_async_copy(
        momenta.at[:, pl.ds(3 * level, 9)], held.at[:, pl.ds(3 - 3 * level, 9)], sems.at[0]
    )
    side = pltpu.make_async_copy(halo, held.at[:, pl.ds(9 * level, 3)], sems.at[1])
    own.start()
    side.start()

    def put(peer, value):
        stage[peer, VROWS:] = value.astype(BF16)

    pack_plane(image_halo[...].astype(F32), put)
    for held_rows in (tall, wide):
        held_rows[:, :8] = jnp.zeros((CZ, 8, 128), F32)
        held_rows[:, 104:] = jnp.zeros((CZ, 8, 128), F32)
    own.wait()
    side.wait()
    first = (half > 0).astype(F32)
    last = (half < 15).astype(F32)
    spare = jnp.zeros((96, 32), F32)
    for block in range(6):
        subject, component = block // 3, block % 3

        def row(r, carry, subject=subject, component=component):
            def m(t):
                return held[subject, r + t, component]

            z = (m(0) + m(4)) * 0.0625 + (m(1) + m(3)) * 0.25 + m(2) * 0.375
            z = z * jnp.where(r == 0, first, jnp.where(r == CZ - 1, last, 1.0))
            z = jnp.concatenate([z, spare], axis=1)

            def lane(k):
                return pltpu.roll(z, k % 128, 1)

            x = (lane(2) + lane(-2)) * 0.0625 + (lane(1) + lane(-1)) * 0.25 + z * 0.375
            tall[r, 8:104] = x
            y = (tall[r, 6:102] + tall[r, 10:106]) * 0.0625
            y += (tall[r, 7:103] + tall[r, 9:105]) * 0.25
            wide[r, 8:104] = y + x * 0.375
            return carry

        lax.fori_loop(0, CZ, row, 0, unroll=2)
        for peer in range(8):
            start = 8 + (CY // 2) * peer - 1
            for r in range(CZ):
                piece[CW * r : CW * (r + 1)] = wide[r, start : start + CW]
            stage[peer, VR * block : VR * (block + 1)] = piece[...].astype(BF16)
    sent = [
        pltpu.make_async_copy(stage.at[me ^ k], out, gone.at[k]) for k, out in enumerate(outs)
    ]
    for copy in sent:
        copy.start()
    for copy in sent:
        copy.wait()


def blur(info, momenta, halo, image_halo):
    rows = VROWS + PROWS
    return pl.pallas_call(
        blur_kernel,
        grid=(),
        in_specs=[
            pl.BlockSpec(memory_space=pltpu.SMEM),
            pl.BlockSpec(memory_space=pl.ANY),
            pl.BlockSpec(memory_space=pl.ANY),
            pl.BlockSpec(memory_space=pltpu.VMEM),
        ],
        out_specs=[pl.BlockSpec(memory_space=pl.ANY)] * 8,
        out_shape=[jax.ShapeDtypeStruct((rows, 128), BF16)] * 8,
        scratch_shapes=[
            pltpu.VMEM((2, 12, 3, 96, 96), F32),
            pltpu.VMEM((8, rows, 128), BF16),
            pltpu.VMEM((CZ, 112, 128), F32),
            pltpu.VMEM((CZ, 112, 128), F32),
            pltpu.VMEM((VR, 128), F32),
            pltpu.SemaphoreType.DMA((2,)),
            pltpu.SemaphoreType.DMA((8,)),
        ],
        name="blur_momenta",
    )(info, momenta, halo, image_halo)


def warp_kernel(info, assign, zy, x0, x1, *rest):
    planes, fields = rest[:8], rest[8:16]
    chunk, edge = rest[16:18]
    image, field, even, odd, acc, sems = rest[18:]
    level, me = info[0], info[1]
    copies = []
    for k in range(8):
        copies.append(
            pltpu.make_async_copy(
                planes[k], image.at[k, pl.ds(1 - level, HZ + 1)], sems.at[k]
            )
        )
        copies.append(
            pltpu.make_async_copy(fields[k].at[:VROWS], field.at[k], sems.at[8 + k])
        )
        copies.append(
            pltpu.make_async_copy(
                fields[k].at[VROWS:], image.at[k, (HZ + 1) * level], sems.at[16 + k]
            )
        )
    for copy in copies:
        copy.start()
    acc[...] = jnp.zeros_like(acc)
    for copy in copies:
        copy.wait()
    lane = lax.broadcasted_iota(jnp.int32, (CY, 128), 1)
    sub = lax.broadcasted_iota(jnp.int32, (CY, 128), 0)

    def neighbours(part):
        left0, left1, left2 = (pltpu.roll(p, 1, 1) for p in part)
        right0, right1, right2 = (pltpu.roll(p, 127, 1) for p in part)
        left2 = jnp.where(lane == 0, left0, jnp.where(lane == 64, pltpu.roll(part[1], 65, 1), left2))
        left0 = jnp.where(lane == 0, 0.0, left0)
        left1 = jnp.where(lane == 0, 0.0, left1)
        right0 = jnp.where(lane == 127, right2, right0)
        right1 = jnp.where(lane == 127, pltpu.roll(part[2], 63, 1), right1)
        right2 = jnp.where(lane % 64 == 63, 0.0, right2)
        return (left0, left1, left2), (right0, right1, right2)

    def interpolate(k, velocity):
        base = 2 * (me ^ k)
        slots = [(assign[base + j] // 2) ^ me for j in range(2)]
        stacked = [[], []]
        for c in range(3):
            parts = [
                field[slots[j], VR * (3 * j + c) : VR * (3 * j + c + 1)] for j in range(2)
            ]
            rough = jnp.dot(
                zy[...], jnp.concatenate(parts, axis=1), preferred_element_type=F32
            )
            high = rough.astype(BF16)
            low = (rough - high.astype(F32)).astype(BF16)
            for j in range(2):
                own = slice(128 * j, 128 * j + 128)
                stacked[j].append(jnp.concatenate([high[:, own], low[:, own]], axis=1))
        fine = [
            jnp.dot(jnp.concatenate(stacked[j], axis=0), table[...], preferred_element_type=F32)
            for j, table in enumerate((x0, x1))
        ]
        velocity[0] = fine[0][:, :128]
        velocity[1] = fine[1][:, :128]
        velocity[2] = fine[0][:, 128:] + fine[1][:, 128:]

    def apply(k, velocity):
        for z in range(HZ):
            before = image[k, z].astype(F32)
            centre = image[k, z + 1].astype(F32)
            after = image[k, z + 2].astype(F32)
            part = [centre[CY * b : CY * (b + 1)] for b in range(3)]
            halo = centre[3 * CY :]
            left, right = neighbours(part)
            warped = []
            for b in range(3):
                own = slice(CY * b, CY * (b + 1))
                up = jnp.where(sub == 0, halo[2 * b : 2 * b + 1], pltpu.roll(part[b], 1, 0))
                down = jnp.where(
                    sub == CY - 1, halo[2 * b + 1 : 2 * b + 2], pltpu.roll(part[b], CY - 1, 0)
                )

                def v(c):
                    start = HZ * CY * c + CY * z
                    return velocity[b, start : start + CY]

                push = v(0) * (right[b] - left[b]) + v(1) * (down - up)
                push += v(2) * (after[own] - before[own])
                warped.append(part[b] - 0.5 * push)
            rows = slice(CY * z, CY * (z + 1))
            acc[0, rows] += warped[0] + warped[1]
            acc[1, rows] += warped[2]

    interpolate(0, even)

    def turn(step, carry):
        interpolate(2 * step + 1, odd)
        apply(2 * step, even)
        interpolate(jnp.minimum(2 * step + 2, 7), even)
        apply(2 * step + 1, odd)
        return carry

    lax.fori_loop(0, 4, turn, 0)
    weight = SCALE / 16.0
    chunk[: HZ * CY] = acc[0] * weight
    wide = lax.broadcasted_iota(jnp.int32, (CY, 128), 1)

    def joined(z, other):
        one, two = (acc[1, pl.ds(pl.multiple_of(r * CY, 8), CY)] for r in (z, other))
        one = one + pltpu.roll(one, 64, 1)
        two = two + pltpu.roll(two, 64, 1)
        return jnp.where(wide < 64, one, two) * weight

    for z in range(HZ // 2):
        chunk[(HZ + z) * CY : (HZ + z + 1) * CY] = joined(z, z + HZ // 2)
    outer = (HZ - 2) * level
    edge[: 2 * CY] = acc[0, pl.ds(pl.multiple_of(outer * CY, 8), 2 * CY)] * weight
    edge[2 * CY :] = joined(outer, outer + 1)


def warp(info, assign, planes, fields):
    tables = [
        jnp.asarray(t, BF16) for t in (zy_table(), x_table(192, 0), x_table(192, 1))
    ]
    vmem = pl.BlockSpec(memory_space=pltpu.VMEM)
    smem = pl.BlockSpec(memory_space=pltpu.SMEM)
    hbm = pl.BlockSpec(memory_space=pl.ANY)
    return pl.pallas_call(
        warp_kernel,
        grid=(),
        in_specs=[smem, smem, vmem, vmem, vmem] + [hbm] * 16,
        out_specs=[vmem] * 2,
        out_shape=[
            jax.ShapeDtypeStruct((HZ * CY * 3 // 2, 128), F32),
            jax.ShapeDtypeStruct((3 * CY, 128), F32),
        ],
        scratch_shapes=[
            pltpu.VMEM((8, HZ + 2, PROWS, 128), BF16),
            pltpu.VMEM((8, VROWS, 128), BF16),
            pltpu.VMEM((3, 3 * HZ * CY, 128), F32),
            pltpu.VMEM((3, 3 * HZ * CY, 128), F32),
            pltpu.VMEM((2, HZ * CY, 128), F32),
            pltpu.SemaphoreType.DMA((24,)),
        ],
        name="warp_sum",
    )(info, assign, *tables, *planes, *fields)


def relax_kernel(info, chunks, out, flat, pair, flat2, pair2, ready, sems):
    level, me, zone = info[0], info[1], info[2]
    size = flat.shape[1] - 16
    for held in (flat, pair, flat2, pair2):
        held[:, :8] = jnp.zeros((held.shape[0], 8, 128), F32)
        held[:, size + 8 :] = jnp.zeros((held.shape[0], 8, 128), F32)
    for held in (flat, flat2):
        for z in (0, held.shape[0] - 1):
            held[z, 8 : 8 + size] = jnp.zeros((size, 128), F32)
    narrow = lax.broadcasted_iota(jnp.int32, (CY, 128), 1)
    tail = HZ * 3 // 2
    for peer in range(8):
        rows = slice(8 + CY * peer, 8 + CY * (peer + 1))
        slots = [(half ^ level) * 8 + (peer ^ me) for half in range(2)]

        def block(half, index):
            return chunks[slots[half], CY * index : CY * (index + 1)]

        for half in range(2):
            for z in range(HZ):
                flat[3 + HZ * half + z, rows] = block(half, z)
            for z in range(2):
                flat[1 + 26 * half + z, rows] = block(half, tail + z)
        packed = [HZ + z % (HZ // 2) for z in range(HZ)]
        sides = [z // (HZ // 2) for z in range(HZ)]
        lows = [(tail + 2, 0), (tail + 2, 1)] + list(zip(packed, sides))
        highs = list(zip(packed, sides)) + [(tail + 2, 0), (tail + 2, 1)]
        for index in range(14):
            low, high = block(0, lows[index][0]), block(1, highs[index][0])
            if lows[index][1] == 1:
                low = pltpu.roll(low, 64, 1)
            if highs[index][1] == 0:
                high = pltpu.roll(high, 64, 1)
            pair[1 + index, rows] = jnp.where(narrow < 64, low, high)

    def mirror(held):
        held[0, 8 : 8 + size] = pltpu.roll(held[14, 8 : 8 + size], 64, 1)
        held[15, 8 : 8 + size] = pltpu.roll(held[1, 8 : 8 + size], 64, 1)

    mirror(pair)
    count = 2 * CY
    lane = lax.broadcasted_iota(jnp.int32, (count, 128), 1)

    def swept(planes, index, start, scale):
        refs = [(planes[0], index), (planes[0], index + 14), (planes[1], index)]
        part = [held[z, start : start + count] for held, z in refs]
        left = [pltpu.roll(p, 1, 1) for p in part]
        right = [pltpu.roll(p, 127, 1) for p in part]
        left[2] = jnp.where(
            lane == 0, left[0], jnp.where(lane == 64, pltpu.roll(part[1], 65, 1), left[2])
        )
        left[0] = jnp.where(lane == 0, 0.0, left[0])
        left[1] = jnp.where(lane == 0, 0.0, left[1])
        right[0] = jnp.where(lane == 127, right[2], right[0])
        right[1] = jnp.where(lane == 127, pltpu.roll(part[2], 63, 1), right[1])
        right[2] = jnp.where(lane % 64 == 63, 0.0, right[2])
        done = []
        for b, (held, z) in enumerate(refs):
            around = held[z - 1, start : start + count] + held[z + 1, start : start + count]
            around += held[z, start - 1 : start - 1 + count] + held[z, start + 1 : start + 1 + count]
            around += left[b] + right[b]
            done.append((0.1 * scale) * part[b] + (0.15 * scale) * around)
        return done

    def first(index, carry):
        for start in range(8, 8 + size, count):
            done = swept((flat, pair), index, start, 1.0)
            flat2[index, start : start + count] = done[0]
            flat2[index + 14, start : start + count] = done[1]
            pair2[index, start : start + count] = done[2]
        return carry

    lax.fori_loop(1, 15, first, 0)
    whole = lax.broadcasted_iota(jnp.int32, (size, 128), 1)

    @pl.when(zone == 0)
    def _():
        flat2[2, 8 : 8 + size] = jnp.zeros((size, 128), F32)
        pair2[2, 8 : 8 + size] = jnp.where(whole < 64, 0.0, pair2[2, 8 : 8 + size])

    @pl.when(zone == 7)
    def _():
        flat2[27, 8 : 8 + size] = jnp.zeros((size, 128), F32)
        pair2[13, 8 : 8 + size] = jnp.where(whole < 64, pair2[13, 8 : 8 + size], 0.0)

    mirror(pair2)

    def emit(z):
        return pltpu.make_async_copy(ready.at[z + 2], out.at[z], sems.at[z])

    def second(index, carry):
        for start in range(8, 8 + size, count):
            done = swept((flat2, pair2), index, start, 1.0 / SCALE)
            rows = slice(start - 8, start - 8 + count)
            ready[index - 1, rows, :128] = done[0]
            ready[index - 1, rows, 128:] = done[2][:, :64]
            ready[index + 13, rows, :128] = done[1]
            ready[index + 13, rows, 128:] = pltpu.roll(done[2], 64, 1)[:, :64]

        @pl.when(index >= 3)
        def _():
            emit(index - 3).start()

        @pl.when(index <= 12)
        def _():
            emit(index + 11).start()

        return carry

    lax.fori_loop(1, 15, second, 0)

    def finish(z, carry):
        emit(z).wait()
        return carry

    lax.fori_loop(0, 24, finish, 0)


def relax(info, chunks):
    vmem = pl.BlockSpec(memory_space=pltpu.VMEM)
    return pl.pallas_call(
        relax_kernel,
        grid=(),
        in_specs=[pl.BlockSpec(memory_space=pltpu.SMEM), vmem],
        out_specs=pl.BlockSpec(memory_space=pl.ANY),
        out_shape=jax.ShapeDtypeStruct((24, 192, 192), F32),
        scratch_shapes=[
            pltpu.VMEM((30, 208, 128), F32),
            pltpu.VMEM((16, 208, 128), F32),
            pltpu.VMEM((30, 208, 128), F32),
            pltpu.VMEM((16, 208, 128), F32),
            pltpu.VMEM((28, 192, 192), F32),
            pltpu.SemaphoreType.DMA((24,)),
        ],
        name="relax",
    )(info, chunks)


def shards(images, momenta, assign):
    level = lax.axis_index("level")
    me = lax.axis_index("subj")
    zone = lax.axis_index("gz")
    info = jnp.stack([level, me, zone]).astype(jnp.int32)
    zones = lax.axis_size("gz")
    outward = [(g, g + 1) for g in range(zones - 1)]
    outward += [(zones + g + 1, zones + g) for g in range(zones - 1)]
    nearest = ("level", "gz")
    *packed, image_rim, rim = pack_images(info, images, momenta)
    image_rim = lax.ppermute(image_rim, nearest, outward)
    rim = lax.ppermute(rim, nearest, outward)

    def spread(parts):
        return [parts[0]] + [
            lax.ppermute(parts[k], "subj", [(i, i ^ k) for i in range(8)]) for k in range(1, 8)
        ]

    planes = spread(packed)
    fields = spread(blur(info, momenta, rim, image_rim))
    chunk, edge = warp(info, assign, planes, fields)
    cross = [(zones + g, g + 1) for g in range(zones - 1)]
    cross += [(g + 1, zones + g) for g in range(zones - 1)]
    edge = lax.ppermute(edge.astype(jnp.float16), nearest, cross)
    chunk = jnp.concatenate([chunk.astype(jnp.float16), edge], axis=0)
    gathered = []
    for far in range(2):
        for step in range(4):
            part = chunk
            if far or step:
                perm = [
                    (8 * a + i, 8 * (a ^ far) + (i ^ (2 * step))) for a in range(2) for i in range(8)
                ]
                part = lax.ppermute(chunk, ("level", "subj"), perm)
            gathered.append(part)
            gathered.append(lax.ppermute(part, "subj", [(i, i ^ 1) for i in range(8)]))
    chunks = jnp.stack(gathered).astype(F32)
    return relax(info, chunks)


def solution(mesh):
    return jax.shard_map(
        shards,
        mesh=mesh,
        in_specs=(P("subj", "gz", None, None), P("subj", "gz", None, None, None), P()),
        out_specs=P("gz", None, None),
        check_vma=False,
    )
```

```python
import jax
import jax.numpy as jnp
import numpy as np
from jax import lax
from jax.experimental import pallas as pl
from jax.experimental.pallas import tpu as pltpu
from jax.sharding import PartitionSpec as P


SWEEPS = 2
F32 = jnp.float32
BF16 = jnp.bfloat16
HZ = 12
CY = 24
CZ = HZ // 2 + 2
CW = CY // 2 + 2
VR = CZ * CW
VROWS = 5 * VR
PROWS = 80
SCALE = 128.0


def lerp_table(fine):
    table = np.zeros((fine, fine // 2 + 2), np.float32)
    for row in range(fine):
        near = row // 2 + 1
        table[row, near] += 0.75
        table[row, near + 2 * (row % 2) - 1] += 0.25
    return table


def zy_table():
    return np.kron(lerp_table(HZ), lerp_table(CY))


def x_table(fine, slot):
    inner = lerp_table(fine)[:, 1:-1].T
    coarse = fine // 2
    table = np.zeros((256, 256), np.float32)
    for base in (0, 128):
        table[base : base + coarse, :128] = inner[:, :128]
        table[base : base + coarse, 128 + 64 * slot : 192 + 64 * slot] = inner[:, 128:]
    return table


def pack_plane(plane, put):
    count = plane.shape[1] // CY
    low = [plane[0][:, :128], plane[1][:, :128]]
    both = jnp.concatenate([plane[0][:, 128:], plane[1][:, 128:]], axis=1)
    parts = low + [both]
    row = lax.broadcasted_iota(jnp.int32, (8, 128), 0)
    for peer in range(count):
        start = CY * peer
        halo = jnp.zeros((8, 128), F32)
        for index, part in enumerate(parts):
            if peer > 0:
                halo = jnp.where(row == 2 * index, part[start - 1 : start], halo)
            if peer < count - 1:
                halo = jnp.where(row == 2 * index + 1, part[start + CY : start + CY + 1], halo)
        blocks = [part[start : start + CY] for part in parts] + [halo]
        put(peer, jnp.concatenate(blocks, axis=0))


GROUPS = ((0, 4), (4, 3), (7, 3), (10, 3))


def pack_kernel(info, images, *rest):
    outs, image_rim = rest[:8], rest[8]
    held, stage, image_edge, sems, gone, side = rest[9:]
    level, me = info[0], info[1]
    arriving = pltpu.make_async_copy(images.at[:, 23 - 23 * level], image_edge, side.at[0])
    leaving = pltpu.make_async_copy(image_edge, image_rim, side.at[1])
    loads = []
    for index, (first, count) in enumerate(GROUPS):
        rows = pl.ds((HZ - 1) * level + first, count)
        loads.append(
            pltpu.make_async_copy(
                images.at[:, rows], held.at[:, pl.ds(first, count)], sems.at[index]
            )
        )
    for copy in loads + [arriving]:
        copy.start()
    sent = []
    for index, (first, count) in enumerate(GROUPS):
        loads[index].wait()

        def step(z, carry):
            def put(peer, value):
                stage[peer, z] = value.astype(BF16)

            pack_plane(held[:, z].astype(F32), put)
            return carry

        lax.fori_loop(first, first + count, step, 0)
        for k, out in enumerate(outs):
            rows = pl.ds(first, count)
            copy = pltpu.make_async_copy(
                stage.at[me ^ k, rows], out.at[rows], gone.at[8 * index + k]
            )
            copy.start()
            sent.append(copy)
        if index == 0:
            arriving.wait()
            leaving.start()
    for copy in [leaving] + sent:
        copy.wait()


def pack_images(info, images):
    hbm = pl.BlockSpec(memory_space=pl.ANY)
    return pl.pallas_call(
        pack_kernel,
        grid=(),
        in_specs=[pl.BlockSpec(memory_space=pltpu.SMEM), hbm],
        out_specs=[hbm] * 9,
        out_shape=[jax.ShapeDtypeStruct((HZ + 1, PROWS, 128), BF16)] * 8
        + [jax.ShapeDtypeStruct((2, 192, 192), BF16)],
        scratch_shapes=[
            pltpu.VMEM((2, HZ + 1, 192, 192), BF16),
            pltpu.VMEM((8, HZ + 1, PROWS, 128), BF16),
            pltpu.VMEM((2, 192, 192), BF16),
            pltpu.SemaphoreType.DMA((len(GROUPS),)),
            pltpu.SemaphoreType.DMA((8 * len(GROUPS),)),
            pltpu.SemaphoreType.DMA((2,)),
        ],
        name="pack_images",
    )(info, images)


def blur_kernel(info, momenta, halo, image_halo, *rest):
    outs = rest[:8]
    held, stage, tall, wide, third, piece, sems, gone = rest[8:]
    level, me = info[0], info[1]
    half = info[2] * 2 + level
    own = pltpu.make_async_copy(
        momenta.at[:, pl.ds(3 * level, 9)], held.at[:, pl.ds(3 - 3 * level, 9)], sems.at[0]
    )
    side = pltpu.make_async_copy(halo, held.at[:, pl.ds(9 * level, 3)], sems.at[1])
    own.start()
    side.start()

    def put(peer, value):
        stage[peer, VROWS:] = value.astype(BF16)

    pack_plane(image_halo[...].astype(F32), put)
    for held_rows in (tall, wide):
        held_rows[:, :8] = jnp.zeros((CZ, 8, 128), F32)
        held_rows[:, 104:] = jnp.zeros((CZ, 8, 128), F32)
    own.wait()
    side.wait()
    first = (half > 0).astype(F32)
    last = (half < 15).astype(F32)
    spare = jnp.zeros((96, 32), F32)
    plane_lane = lax.broadcasted_iota(jnp.int32, (96, 128), 1)
    for subject, component in ((1, 0), (0, 0), (0, 1), (0, 2), (1, 1), (1, 2)):

        def row(r, carry, subject=subject, component=component):
            def m(t):
                return held[subject, r + t, component]

            z = (m(0) + m(4)) * 0.0625 + (m(1) + m(3)) * 0.25 + m(2) * 0.375
            z = z * jnp.where(r == 0, first, jnp.where(r == CZ - 1, last, 1.0))
            z = jnp.concatenate([z, spare], axis=1)

            def lane(k):
                return pltpu.roll(z, k % 128, 1)

            x = (lane(2) + lane(-2)) * 0.0625 + (lane(1) + lane(-1)) * 0.25 + z * 0.375
            tall[r, 8:104] = x
            y = (tall[r, 6:102] + tall[r, 10:106]) * 0.0625
            y += (tall[r, 7:103] + tall[r, 9:105]) * 0.25
            y += x * 0.375
            if (subject, component) == (1, 0):
                third[r] = y
            elif subject == 0:
                extra = pltpu.roll(third[r], 96 - 32 * component, 1)
                wide[r, 8:104] = jnp.where(plane_lane < 96, y, extra)
            else:
                wide[r, 8:104] = y
            return carry

        lax.fori_loop(0, CZ, row, 0, unroll=2)
        if (subject, component) == (1, 0):
            continue
        block = 2 * subject + component
        for peer in range(8):
            start = 8 + (CY // 2) * peer - 1
            for r in range(CZ):
                piece[CW * r : CW * (r + 1)] = wide[r, start : start + CW]
            stage[peer, VR * block : VR * (block + 1)] = piece[...].astype(BF16)
    sent = [
        pltpu.make_async_copy(stage.at[me ^ k], out, gone.at[k]) for k, out in enumerate(outs)
    ]
    for copy in sent:
        copy.start()
    for copy in sent:
        copy.wait()


def blur(info, momenta, halo, image_halo):
    rows = VROWS + PROWS
    return pl.pallas_call(
        blur_kernel,
        grid=(),
        in_specs=[
            pl.BlockSpec(memory_space=pltpu.SMEM),
            pl.BlockSpec(memory_space=pl.ANY),
            pl.BlockSpec(memory_space=pl.ANY),
            pl.BlockSpec(memory_space=pltpu.VMEM),
        ],
        out_specs=[pl.BlockSpec(memory_space=pl.ANY)] * 8,
        out_shape=[jax.ShapeDtypeStruct((rows, 128), BF16)] * 8,
        scratch_shapes=[
            pltpu.VMEM((2, 12, 3, 96, 96), F32),
            pltpu.VMEM((8, rows, 128), BF16),
            pltpu.VMEM((CZ, 112, 128), F32),
            pltpu.VMEM((CZ, 112, 128), F32),
            pltpu.VMEM((CZ, 96, 128), F32),
            pltpu.VMEM((VR, 128), F32),
            pltpu.SemaphoreType.DMA((2,)),
            pltpu.SemaphoreType.DMA((8,)),
        ],
        name="blur_momenta",
    )(info, momenta, halo, image_halo)


def warp_kernel(info, assign, zy, x0, x1, *rest):
    planes, fields = rest[:8], rest[8:16]
    chunk, edge = rest[16:18]
    image, field, even, odd, acc, sems = rest[18:]
    level, me = info[0], info[1]
    copies = []
    for k in range(8):
        copies.append(
            pltpu.make_async_copy(
                planes[k], image.at[k, pl.ds(1 - level, HZ + 1)], sems.at[k]
            )
        )
        copies.append(
            pltpu.make_async_copy(fields[k].at[:VROWS], field.at[k], sems.at[8 + k])
        )
        copies.append(
            pltpu.make_async_copy(
                fields[k].at[VROWS:], image.at[k, (HZ + 1) * level], sems.at[16 + k]
            )
        )
    for copy in copies:
        copy.start()
    acc[...] = jnp.zeros_like(acc)
    for copy in copies:
        copy.wait()
    lane = lax.broadcasted_iota(jnp.int32, (CY, 128), 1)
    sub = lax.broadcasted_iota(jnp.int32, (CY, 128), 0)
    coarse_lane = lax.broadcasted_iota(jnp.int32, (VR, 128), 1)

    def neighbours(part):
        left0, left1, left2 = (pltpu.roll(p, 1, 1) for p in part)
        right0, right1, right2 = (pltpu.roll(p, 127, 1) for p in part)
        left2 = jnp.where(lane == 0, left0, jnp.where(lane == 64, pltpu.roll(part[1], 65, 1), left2))
        left0 = jnp.where(lane == 0, 0.0, left0)
        left1 = jnp.where(lane == 0, 0.0, left1)
        right0 = jnp.where(lane == 127, right2, right0)
        right1 = jnp.where(lane == 127, pltpu.roll(part[2], 63, 1), right1)
        right2 = jnp.where(lane % 64 == 63, 0.0, right2)
        return (left0, left1, left2), (right0, right1, right2)

    def interpolate(k, velocity):
        base = 2 * (me ^ k)
        slots = [(assign[base + j] // 2) ^ me for j in range(2)]
        stacked = [[], []]
        for c in range(3):
            parts = [field[slots[0], VR * c : VR * (c + 1)]]
            if c > 0:
                parts.append(field[slots[1], VR * (c + 2) : VR * (c + 3)])
            else:
                spread = [
                    pltpu.roll(
                        field[slots[1], VR * t : VR * (t + 1)].astype(F32), 32 * t + 32, 1
                    )
                    for t in range(3)
                ]
                third = jnp.where(
                    coarse_lane < 32, spread[0], jnp.where(coarse_lane < 64, spread[1], spread[2])
                )
                parts.append(third.astype(BF16))
            rough = jnp.dot(
                zy[...], jnp.concatenate(parts, axis=1), preferred_element_type=F32
            )
            high = rough.astype(BF16)
            low = (rough - high.astype(F32)).astype(BF16)
            for j in range(2):
                own = slice(128 * j, 128 * j + 128)
                stacked[j].append(jnp.concatenate([high[:, own], low[:, own]], axis=1))
        fine = [
            jnp.dot(jnp.concatenate(stacked[j], axis=0), table[...], preferred_element_type=F32)
            for j, table in enumerate((x0, x1))
        ]
        velocity[0] = fine[0][:, :128]
        velocity[1] = fine[1][:, :128]
        velocity[2] = fine[0][:, 128:] + fine[1][:, 128:]

    def apply(k, velocity):
        for z in range(HZ):
            before = image[k, z].astype(F32)
            centre = image[k, z + 1].astype(F32)
            after = image[k, z + 2].astype(F32)
            part = [centre[CY * b : CY * (b + 1)] for b in range(3)]
            halo = centre[3 * CY :]
            left, right = neighbours(part)
            warped = []
            for b in range(3):
                own = slice(CY * b, CY * (b + 1))
                up = jnp.where(sub == 0, halo[2 * b : 2 * b + 1], pltpu.roll(part[b], 1, 0))
                down = jnp.where(
                    sub == CY - 1, halo[2 * b + 1 : 2 * b + 2], pltpu.roll(part[b], CY - 1, 0)
                )

                def v(c):
                    start = HZ * CY * c + CY * z
                    return velocity[b, start : start + CY]

                push = v(0) * (right[b] - left[b]) + v(1) * (down - up)
                push += v(2) * (after[own] - before[own])
                warped.append(part[b] - 0.5 * push)
            rows = slice(CY * z, CY * (z + 1))
            acc[0, rows] += warped[0] + warped[1]
            acc[1, rows] += warped[2]

    interpolate(0, even)

    def turn(step, carry):
        interpolate(2 * step + 1, odd)
        apply(2 * step, even)
        interpolate(jnp.minimum(2 * step + 2, 7), even)
        apply(2 * step + 1, odd)
        return carry

    lax.fori_loop(0, 4, turn, 0)
    weight = SCALE / 16.0
    chunk[: HZ * CY] = pltpu.roll(acc[0] * weight, 64 * level, 1)
    wide = lax.broadcasted_iota(jnp.int32, (CY, 128), 1)

    def joined(z, other):
        one, two = (acc[1, pl.ds(pl.multiple_of(r * CY, 8), CY)] for r in (z, other))
        one = one + pltpu.roll(one, 64, 1)
        two = two + pltpu.roll(two, 64, 1)
        return jnp.where(wide < 64, one, two) * weight

    for z in range(HZ // 2):
        chunk[(HZ + z) * CY : (HZ + z + 1) * CY] = joined(z, z + HZ // 2)
    outer = (HZ - 2) * level
    rim = acc[0, pl.ds(pl.multiple_of(outer * CY, 8), 2 * CY)] * weight
    edge[: 2 * CY] = pltpu.roll(rim, 64 - 64 * level, 1)
    edge[2 * CY :] = joined(outer, outer + 1)


def warp(info, assign, planes, fields):
    tables = [
        jnp.asarray(t, BF16) for t in (zy_table(), x_table(192, 0), x_table(192, 1))
    ]
    vmem = pl.BlockSpec(memory_space=pltpu.VMEM)
    smem = pl.BlockSpec(memory_space=pltpu.SMEM)
    hbm = pl.BlockSpec(memory_space=pl.ANY)
    return pl.pallas_call(
        warp_kernel,
        grid=(),
        in_specs=[smem, smem, vmem, vmem, vmem] + [hbm] * 16,
        out_specs=[vmem] * 2,
        out_shape=[
            jax.ShapeDtypeStruct((HZ * CY * 3 // 2, 128), F32),
            jax.ShapeDtypeStruct((3 * CY, 128), F32),
        ],
        scratch_shapes=[
            pltpu.VMEM((8, HZ + 2, PROWS, 128), BF16),
            pltpu.VMEM((8, VROWS, 128), BF16),
            pltpu.VMEM((3, 3 * HZ * CY, 128), F32),
            pltpu.VMEM((3, 3 * HZ * CY, 128), F32),
            pltpu.VMEM((2, HZ * CY, 128), F32),
            pltpu.SemaphoreType.DMA((24,)),
        ],
        name="warp_sum",
    )(info, assign, *tables, *planes, *fields)


def relax_kernel(info, chunks, out, flat, pair, flat2, pair2, ready, sems):
    level, me, zone = info[0], info[1], info[2]
    size = flat.shape[1] - 16
    for held in (flat, pair, flat2, pair2):
        held[:, :8] = jnp.zeros((held.shape[0], 8, 128), F32)
        held[:, size + 8 :] = jnp.zeros((held.shape[0], 8, 128), F32)
    for held in (flat, flat2):
        for z in (0, held.shape[0] - 1):
            held[z, 8 : 8 + size] = jnp.zeros((size, 128), F32)
    narrow = lax.broadcasted_iota(jnp.int32, (CY, 128), 1)
    tail = HZ * 3 // 2
    for peer in range(8):
        rows = slice(8 + CY * peer, 8 + CY * (peer + 1))
        slots = [(half ^ level) * 8 + (peer ^ me) for half in range(2)]

        def block(half, index):
            return chunks[slots[half], CY * index : CY * (index + 1)]

        for half in range(2):
            for z in range(HZ):
                flat[3 + 14 * half + z, rows] = block(half, z)
            for z in range(2):
                flat[1 + 28 * half + z, rows] = block(half, tail + z)
        packed = [HZ + z % (HZ // 2) for z in range(HZ)]
        sides = [z // (HZ // 2) for z in range(HZ)]
        lows = [(tail + 2, 0), (tail + 2, 1)] + list(zip(packed, sides))
        highs = list(zip(packed, sides)) + [(tail + 2, 0), (tail + 2, 1)]
        for index in range(14):
            low, high = block(0, lows[index][0]), block(1, highs[index][0])
            if lows[index][1] == 1:
                low = pltpu.roll(low, 64, 1)
            if highs[index][1] == 0:
                high = pltpu.roll(high, 64, 1)
            pair[1 + index, rows] = jnp.where(narrow < 64, low, high)

    def mirror(planes, both):
        body = slice(8, 8 + size)
        both[0, body] = pltpu.roll(both[14, body], 64, 1)
        both[15, body] = pltpu.roll(both[1, body], 64, 1)
        planes[16, body] = pltpu.roll(planes[14, body], 64, 1)
        planes[15, body] = pltpu.roll(planes[17, body], 64, 1)

    mirror(flat, pair)
    count = 2 * CY
    lane = lax.broadcasted_iota(jnp.int32, (count, 128), 1)

    def swept(planes, index, start, scale):
        refs = [(planes[0], index), (planes[0], index + 16), (planes[1], index)]
        part = [held[z, start : start + count] for held, z in refs]
        left = [pltpu.roll(p, 1, 1) for p in part]
        right = [pltpu.roll(p, 127, 1) for p in part]
        left[2] = jnp.where(lane == 0, left[0], jnp.where(lane == 64, left[1], left[2]))
        left[0] = jnp.where(lane == 0, 0.0, left[0])
        left[1] = jnp.where(lane == 64, 0.0, left[1])
        right[0] = jnp.where(lane == 127, right[2], right[0])
        right[1] = jnp.where(lane == 63, right[2], right[1])
        right[2] = jnp.where(lane % 64 == 63, 0.0, right[2])
        done = []
        for b, (held, z) in enumerate(refs):
            around = held[z - 1, start : start + count] + held[z + 1, start : start + count]
            around += held[z, start - 1 : start - 1 + count] + held[z, start + 1 : start + 1 + count]
            around += left[b] + right[b]
            done.append((0.1 * scale) * part[b] + (0.15 * scale) * around)
        return done

    def first(index, carry):
        for start in range(8, 8 + size, count):
            done = swept((flat, pair), index, start, 1.0)
            flat2[index, start : start + count] = done[0]
            flat2[index + 16, start : start + count] = done[1]
            pair2[index, start : start + count] = done[2]
        return carry

    lax.fori_loop(1, 15, first, 0)
    whole = lax.broadcasted_iota(jnp.int32, (size, 128), 1)

    @pl.when(zone == 0)
    def _():
        flat2[2, 8 : 8 + size] = jnp.zeros((size, 128), F32)
        pair2[2, 8 : 8 + size] = jnp.where(whole < 64, 0.0, pair2[2, 8 : 8 + size])

    @pl.when(zone == 7)
    def _():
        flat2[29, 8 : 8 + size] = jnp.zeros((size, 128), F32)
        pair2[13, 8 : 8 + size] = jnp.where(whole < 64, pair2[13, 8 : 8 + size], 0.0)

    mirror(flat2, pair2)

    def emit(z):
        return pltpu.make_async_copy(ready.at[z + 2], out.at[z], sems.at[z])

    def second(index, carry):
        for start in range(8, 8 + size, count):
            done = swept((flat2, pair2), index, start, 1.0 / SCALE)
            rows = slice(start - 8, start - 8 + count)
            ready[index - 1, rows, :128] = done[0]
            ready[index - 1, rows, 128:] = done[2][:, :64]
            ready[index + 13, rows, :128] = pltpu.roll(done[1], 64, 1)
            ready[index + 13, rows, 128:] = pltpu.roll(done[2], 64, 1)[:, :64]

        @pl.when(index >= 3)
        def _():
            emit(index - 3).start()

        @pl.when(index <= 12)
        def _():
            emit(index + 11).start()

        return carry

    lax.fori_loop(1, 15, second, 0)

    def finish(z, carry):
        emit(z).wait()
        return carry

    lax.fori_loop(0, 24, finish, 0)


def relax(info, chunks):
    vmem = pl.BlockSpec(memory_space=pltpu.VMEM)
    return pl.pallas_call(
        relax_kernel,
        grid=(),
        in_specs=[pl.BlockSpec(memory_space=pltpu.SMEM), vmem],
        out_specs=pl.BlockSpec(memory_space=pl.ANY),
        out_shape=jax.ShapeDtypeStruct((24, 192, 192), F32),
        scratch_shapes=[
            pltpu.VMEM((32, 208, 128), F32),
            pltpu.VMEM((16, 208, 128), F32),
            pltpu.VMEM((32, 208, 128), F32),
            pltpu.VMEM((16, 208, 128), F32),
            pltpu.VMEM((28, 192, 192), F32),
            pltpu.SemaphoreType.DMA((24,)),
        ],
        name="relax",
    )(info, chunks)


def shards(images, momenta, assign):
    level = lax.axis_index("level")
    me = lax.axis_index("subj")
    zone = lax.axis_index("gz")
    info = jnp.stack([level, me, zone]).astype(jnp.int32)
    zones = lax.axis_size("gz")
    outward = [(g, g + 1) for g in range(zones - 1)]
    outward += [(zones + g + 1, zones + g) for g in range(zones - 1)]
    nearest = ("level", "gz")
    rim = lax.dynamic_slice_in_dim(momenta, 9 * (1 - level), 3, axis=1)
    rim = lax.ppermute(rim, nearest, outward)
    *packed, image_rim = pack_images(info, images)
    image_rim = lax.ppermute(image_rim, nearest, outward)

    def spread(parts):
        return [parts[0]] + [
            lax.ppermute(parts[k], "subj", [(i, i ^ k) for i in range(8)]) for k in range(1, 8)
        ]

    planes = spread(packed)
    fields = spread(blur(info, momenta, rim, image_rim))
    chunk, edge = warp(info, assign, planes, fields)
    cross = [(zones + g, g + 1) for g in range(zones - 1)]
    cross += [(g + 1, zones + g) for g in range(zones - 1)]
    edge = lax.ppermute(edge.astype(jnp.float16), nearest, cross)
    chunk = jnp.concatenate([chunk.astype(jnp.float16), edge], axis=0)
    gathered = []
    for far in range(2):
        for step in range(4):
            part = chunk
            if far or step:
                perm = [
                    (8 * a + i, 8 * (a ^ far) + (i ^ (2 * step))) for a in range(2) for i in range(8)
                ]
                part = lax.ppermute(chunk, ("level", "subj"), perm)
            gathered.append(part)
            gathered.append(lax.ppermute(part, "subj", [(i, i ^ 1) for i in range(8)]))
    chunks = jnp.stack(gathered).astype(F32)
    return relax(info, chunks)


def solution(mesh):
    return jax.shard_map(
        shards,
        mesh=mesh,
        in_specs=(P("subj", "gz", None, None), P("subj", "gz", None, None, None), P()),
        out_specs=P("gz", None, None),
        check_vma=False,
    )
```

```python
import jax
import jax.numpy as jnp
import numpy as np
from jax import lax
from jax.experimental import pallas as pl
from jax.experimental.pallas import tpu as pltpu
from jax.sharding import PartitionSpec as P


F32 = jnp.float32
BF16 = jnp.bfloat16
HZ = 12
CY = 24
CZ = HZ // 2 + 2
CW = CY // 2 + 2
VR = CZ * CW
VROWS = 5 * VR
PROWS = 80
SCALE = 128.0


def lerp_table(fine):
    table = np.zeros((fine, fine // 2 + 2), np.float32)
    for row in range(fine):
        near = row // 2 + 1
        table[row, near] += 0.75
        table[row, near + 2 * (row % 2) - 1] += 0.25
    return table


def zy_table():
    return np.kron(lerp_table(HZ), lerp_table(CY))


def x_table(fine, slot):
    inner = lerp_table(fine)[:, 1:-1].T
    coarse = fine // 2
    table = np.zeros((256, 256), np.float32)
    for base in (0, 128):
        table[base : base + coarse, :128] = inner[:, :128]
        table[base : base + coarse, 128 + 64 * slot : 192 + 64 * slot] = inner[:, 128:]
    return table


def pack_plane(plane, put):
    count = plane.shape[1] // CY
    low = [plane[0][:, :128], plane[1][:, :128]]
    both = jnp.concatenate([plane[0][:, 128:], plane[1][:, 128:]], axis=1)
    parts = low + [both]
    row = lax.broadcasted_iota(jnp.int32, (8, 128), 0)
    for peer in range(count):
        start = CY * peer
        halo = jnp.zeros((8, 128), F32)
        for index, part in enumerate(parts):
            if peer > 0:
                halo = jnp.where(row == 2 * index, part[start - 1 : start], halo)
            if peer < count - 1:
                halo = jnp.where(row == 2 * index + 1, part[start + CY : start + CY + 1], halo)
        blocks = [part[start : start + CY] for part in parts] + [halo]
        put(peer, jnp.concatenate(blocks, axis=0))


GROUPS = ((0, 3), (3, 3), (6, 3), (9, 3))


def pack_kernel(info, images, *rest):
    outs = rest[:8]
    held, stage, sems, gone = rest[8:]
    level, me = info[0], info[1]
    loads = []
    for index, (first, count) in enumerate(GROUPS):
        rows = pl.ds(HZ * level + first, count)
        loads.append(
            pltpu.make_async_copy(
                images.at[:, rows], held.at[:, pl.ds(first, count)], sems.at[index]
            )
        )
    for copy in loads:
        copy.start()
    sent = []
    for index, (first, count) in enumerate(GROUPS):
        loads[index].wait()

        def step(z, carry):
            def put(peer, value):
                stage[peer, z] = value.astype(BF16)

            pack_plane(held[:, z].astype(F32), put)
            return carry

        lax.fori_loop(first, first + count, step, 0)
        for k, out in enumerate(outs):
            rows = pl.ds(first, count)
            copy = pltpu.make_async_copy(
                stage.at[me ^ k, rows], out.at[rows], gone.at[8 * index + k]
            )
            copy.start()
            sent.append(copy)
    for copy in sent:
        copy.wait()


def pack_images(info, images):
    hbm = pl.BlockSpec(memory_space=pl.ANY)
    return pl.pallas_call(
        pack_kernel,
        grid=(),
        in_specs=[pl.BlockSpec(memory_space=pltpu.SMEM), hbm],
        out_specs=[hbm] * 8,
        out_shape=[jax.ShapeDtypeStruct((HZ, PROWS, 128), BF16)] * 8,
        scratch_shapes=[
            pltpu.VMEM((2, HZ, 192, 192), BF16),
            pltpu.VMEM((8, HZ, PROWS, 128), BF16),
            pltpu.SemaphoreType.DMA((len(GROUPS),)),
            pltpu.SemaphoreType.DMA((8 * len(GROUPS),)),
        ],
        name="pack_images",
    )(info, images)


def blur_kernel(info, momenta, halo, other, *rest):
    outs = rest[:8]
    held, stage, tall, wide, third, piece, sems, gone = rest[8:]
    level, me = info[0], info[1]
    half = info[2] * 2 + level
    own = pltpu.make_async_copy(
        momenta.at[:, pl.ds(3 * level, 9)], held.at[:, pl.ds(3 - 3 * level, 9)], sems.at[0]
    )
    sides = [
        pltpu.make_async_copy(rows, held.at[j, pl.ds(9 * level, 3)], sems.at[1 + j])
        for j, rows in enumerate((halo, other))
    ]
    for copy in [own] + sides:
        copy.start()
    for held_rows in (tall, wide):
        held_rows[:, :8] = jnp.zeros((CZ, 8, 128), F32)
        held_rows[:, 104:] = jnp.zeros((CZ, 8, 128), F32)
    for copy in [own] + sides:
        copy.wait()
    first = (half > 0).astype(F32)
    last = (half < 15).astype(F32)
    spare = jnp.zeros((96, 32), F32)
    plane_lane = lax.broadcasted_iota(jnp.int32, (96, 128), 1)
    for subject, component in ((1, 0), (0, 0), (0, 1), (0, 2), (1, 1), (1, 2)):

        def row(r, carry, subject=subject, component=component):
            def m(t):
                return held[subject, r + t, component]

            z = (m(0) + m(4)) * 0.0625 + (m(1) + m(3)) * 0.25 + m(2) * 0.375
            z = z * jnp.where(r == 0, first, jnp.where(r == CZ - 1, last, 1.0))
            z = jnp.concatenate([z, spare], axis=1)

            def lane(k):
                return pltpu.roll(z, k % 128, 1)

            x = (lane(2) + lane(-2)) * 0.0625 + (lane(1) + lane(-1)) * 0.25 + z * 0.375
            tall[r, 8:104] = x
            y = (tall[r, 6:102] + tall[r, 10:106]) * 0.0625
            y += (tall[r, 7:103] + tall[r, 9:105]) * 0.25
            y += x * 0.375
            if (subject, component) == (1, 0):
                third[r] = y
            elif subject == 0:
                extra = pltpu.roll(third[r], 96 - 32 * component, 1)
                wide[r, 8:104] = jnp.where(plane_lane < 96, y, extra)
            else:
                wide[r, 8:104] = y
            return carry

        lax.fori_loop(0, CZ, row, 0, unroll=2)
        if (subject, component) == (1, 0):
            continue
        block = 2 * subject + component
        for peer in range(8):
            start = 8 + (CY // 2) * peer - 1
            for r in range(CZ):
                piece[CW * r : CW * (r + 1)] = wide[r, start : start + CW]
            stage[peer, VR * block : VR * (block + 1)] = piece[...].astype(BF16)
    sent = [
        pltpu.make_async_copy(stage.at[me ^ k], out, gone.at[k]) for k, out in enumerate(outs)
    ]
    for copy in sent:
        copy.start()
    for copy in sent:
        copy.wait()


def blur(info, momenta, halo, other):
    rows = VROWS
    return pl.pallas_call(
        blur_kernel,
        grid=(),
        in_specs=[
            pl.BlockSpec(memory_space=pltpu.SMEM),
            pl.BlockSpec(memory_space=pl.ANY),
            pl.BlockSpec(memory_space=pl.ANY),
            pl.BlockSpec(memory_space=pl.ANY),
        ],
        out_specs=[pl.BlockSpec(memory_space=pl.ANY)] * 8,
        out_shape=[jax.ShapeDtypeStruct((rows, 128), BF16)] * 8,
        scratch_shapes=[
            pltpu.VMEM((2, 12, 3, 96, 96), F32),
            pltpu.VMEM((8, rows, 128), BF16),
            pltpu.VMEM((CZ, 112, 128), F32),
            pltpu.VMEM((CZ, 112, 128), F32),
            pltpu.VMEM((CZ, 96, 128), F32),
            pltpu.VMEM((VR, 128), F32),
            pltpu.SemaphoreType.DMA((3,)),
            pltpu.SemaphoreType.DMA((8,)),
        ],
        name="blur_momenta",
    )(info, momenta, halo, other)


def edge_kernel(*refs):
    planes, below, above = refs[:8], refs[8], refs[9]
    low, high, sems, gone = refs[10:]
    copies = []
    for k, plane in enumerate(planes):
        copies.append(pltpu.make_async_copy(plane.at[0], low.at[k], sems.at[k]))
        copies.append(pltpu.make_async_copy(plane.at[HZ - 1], high.at[k], sems.at[8 + k]))
    for copy in copies:
        copy.start()
    for copy in copies:
        copy.wait()
    leaving = [
        pltpu.make_async_copy(low, below, gone.at[0]),
        pltpu.make_async_copy(high, above, gone.at[1]),
    ]
    for copy in leaving:
        copy.start()
    for copy in leaving:
        copy.wait()


def edges(planes):
    hbm = pl.BlockSpec(memory_space=pl.ANY)
    shape = (8, PROWS, 128)
    return pl.pallas_call(
        edge_kernel,
        grid=(),
        in_specs=[hbm] * 8,
        out_specs=[hbm] * 2,
        out_shape=[jax.ShapeDtypeStruct(shape, BF16)] * 2,
        scratch_shapes=[
            pltpu.VMEM(shape, BF16),
            pltpu.VMEM(shape, BF16),
            pltpu.SemaphoreType.DMA((16,)),
            pltpu.SemaphoreType.DMA((2,)),
        ],
        name="cut_edges",
    )(*planes)


def warp_kernel(info, assign, zy, x0, x1, *rest):
    planes, fields, below, above = rest[:8], rest[8:16], rest[16], rest[17]
    chunk, edge = rest[18:20]
    image, field, even, odd, acc, sems = rest[20:]
    level, me = info[0], info[1]
    copies = [
        pltpu.make_async_copy(below, image.at[:, 0], sems.at[16]),
        pltpu.make_async_copy(above, image.at[:, HZ + 1], sems.at[17]),
    ]
    for k in range(8):
        copies.append(
            pltpu.make_async_copy(planes[k], image.at[k, 1 : HZ + 1], sems.at[k])
        )
        copies.append(pltpu.make_async_copy(fields[k], field.at[k], sems.at[8 + k]))
    for copy in copies:
        copy.start()
    acc[...] = jnp.zeros_like(acc)
    for copy in copies:
        copy.wait()
    lane = lax.broadcasted_iota(jnp.int32, (CY, 128), 1)
    sub = lax.broadcasted_iota(jnp.int32, (CY, 128), 0)
    coarse_lane = lax.broadcasted_iota(jnp.int32, (VR, 128), 1)

    def neighbours(part):
        left0, left1, left2 = (pltpu.roll(p, 1, 1) for p in part)
        right0, right1, right2 = (pltpu.roll(p, 127, 1) for p in part)
        left2 = jnp.where(lane == 0, left0, jnp.where(lane == 64, pltpu.roll(part[1], 65, 1), left2))
        left0 = jnp.where(lane == 0, 0.0, left0)
        left1 = jnp.where(lane == 0, 0.0, left1)
        right0 = jnp.where(lane == 127, right2, right0)
        right1 = jnp.where(lane == 127, pltpu.roll(part[2], 63, 1), right1)
        right2 = jnp.where(lane % 64 == 63, 0.0, right2)
        return (left0, left1, left2), (right0, right1, right2)

    def interpolate(k, velocity):
        base = 2 * (me ^ k)
        slots = [(assign[base + j] // 2) ^ me for j in range(2)]
        stacked = [[], []]
        for c in range(3):
            parts = [field[slots[0], VR * c : VR * (c + 1)]]
            if c > 0:
                parts.append(field[slots[1], VR * (c + 2) : VR * (c + 3)])
            else:
                spread = [
                    pltpu.roll(
                        field[slots[1], VR * t : VR * (t + 1)].astype(F32), 32 * t + 32, 1
                    )
                    for t in range(3)
                ]
                third = jnp.where(
                    coarse_lane < 32, spread[0], jnp.where(coarse_lane < 64, spread[1], spread[2])
                )
                parts.append(third.astype(BF16))
            rough = jnp.dot(
                zy[...], jnp.concatenate(parts, axis=1), preferred_element_type=F32
            )
            high = rough.astype(BF16)
            low = (rough - high.astype(F32)).astype(BF16)
            for j in range(2):
                own = slice(128 * j, 128 * j + 128)
                stacked[j].append(jnp.concatenate([high[:, own], low[:, own]], axis=1))
        fine = [
            jnp.dot(jnp.concatenate(stacked[j], axis=0), table[...], preferred_element_type=F32)
            for j, table in enumerate((x0, x1))
        ]
        velocity[0] = fine[0][:, :128]
        velocity[1] = fine[1][:, :128]
        velocity[2] = fine[0][:, 128:] + fine[1][:, 128:]

    def apply(k, velocity):
        for z in range(HZ):
            before = image[k, z].astype(F32)
            centre = image[k, z + 1].astype(F32)
            after = image[k, z + 2].astype(F32)
            part = [centre[CY * b : CY * (b + 1)] for b in range(3)]
            halo = centre[3 * CY :]
            left, right = neighbours(part)
            warped = []
            for b in range(3):
                own = slice(CY * b, CY * (b + 1))
                up = jnp.where(sub == 0, halo[2 * b : 2 * b + 1], pltpu.roll(part[b], 1, 0))
                down = jnp.where(
                    sub == CY - 1, halo[2 * b + 1 : 2 * b + 2], pltpu.roll(part[b], CY - 1, 0)
                )

                def v(c):
                    start = HZ * CY * c + CY * z
                    return velocity[b, start : start + CY]

                push = v(0) * (right[b] - left[b]) + v(1) * (down - up)
                push += v(2) * (after[own] - before[own])
                warped.append(part[b] - 0.5 * push)
            rows = slice(CY * z, CY * (z + 1))
            acc[0, rows] += warped[0] + warped[1]
            acc[1, rows] += warped[2]

    interpolate(0, even)

    def turn(step, carry):
        interpolate(2 * step + 1, odd)
        apply(2 * step, even)
        interpolate(jnp.minimum(2 * step + 2, 7), even)
        apply(2 * step + 1, odd)
        return carry

    lax.fori_loop(0, 4, turn, 0)
    weight = SCALE / 16.0
    chunk[: HZ * CY] = pltpu.roll(acc[0] * weight, 64 * level, 1)
    wide = lax.broadcasted_iota(jnp.int32, (CY, 128), 1)

    def joined(z, other):
        one, two = (acc[1, pl.ds(pl.multiple_of(r * CY, 8), CY)] for r in (z, other))
        one = one + pltpu.roll(one, 64, 1)
        two = two + pltpu.roll(two, 64, 1)
        return jnp.where(wide < 64, one, two) * weight

    for z in range(HZ // 2):
        chunk[(HZ + z) * CY : (HZ + z + 1) * CY] = joined(z, z + HZ // 2)
    outer = (HZ - 2) * level
    rim = acc[0, pl.ds(pl.multiple_of(outer * CY, 8), 2 * CY)] * weight
    edge[: 2 * CY] = pltpu.roll(rim, 64 - 64 * level, 1)
    edge[2 * CY :] = joined(outer, outer + 1)


def warp(info, assign, planes, fields, below, above):
    tables = [
        jnp.asarray(t, BF16) for t in (zy_table(), x_table(192, 0), x_table(192, 1))
    ]
    vmem = pl.BlockSpec(memory_space=pltpu.VMEM)
    smem = pl.BlockSpec(memory_space=pltpu.SMEM)
    hbm = pl.BlockSpec(memory_space=pl.ANY)
    return pl.pallas_call(
        warp_kernel,
        grid=(),
        in_specs=[smem, smem, vmem, vmem, vmem] + [hbm] * 18,
        out_specs=[vmem] * 2,
        out_shape=[
            jax.ShapeDtypeStruct((HZ * CY * 3 // 2, 128), F32),
            jax.ShapeDtypeStruct((3 * CY, 128), F32),
        ],
        scratch_shapes=[
            pltpu.VMEM((8, HZ + 2, PROWS, 128), BF16),
            pltpu.VMEM((8, VROWS, 128), BF16),
            pltpu.VMEM((3, 3 * HZ * CY, 128), F32),
            pltpu.VMEM((3, 3 * HZ * CY, 128), F32),
            pltpu.VMEM((2, HZ * CY, 128), F32),
            pltpu.SemaphoreType.DMA((18,)),
        ],
        name="warp_sum",
    )(info, assign, *tables, *planes, *fields, below, above)


def relax_kernel(info, chunks, out, flat, pair, flat2, pair2, ready, sems):
    level, me, zone = info[0], info[1], info[2]
    size = flat.shape[1] - 16
    for held in (flat, pair, flat2, pair2):
        held[:, :8] = jnp.zeros((held.shape[0], 8, 128), F32)
        held[:, size + 8 :] = jnp.zeros((held.shape[0], 8, 128), F32)
    for held in (flat, flat2):
        for z in (0, held.shape[0] - 1):
            held[z, 8 : 8 + size] = jnp.zeros((size, 128), F32)
    narrow = lax.broadcasted_iota(jnp.int32, (CY, 128), 1)
    tail = HZ * 3 // 2
    for peer in range(8):
        rows = slice(8 + CY * peer, 8 + CY * (peer + 1))
        slots = [(half ^ level) * 8 + (peer ^ me) for half in range(2)]

        def block(half, index):
            return chunks[slots[half], CY * index : CY * (index + 1)]

        for half in range(2):
            for z in range(HZ):
                flat[3 + 14 * half + z, rows] = block(half, z)
            for z in range(2):
                flat[1 + 28 * half + z, rows] = block(half, tail + z)
        packed = [HZ + z % (HZ // 2) for z in range(HZ)]
        sides = [z // (HZ // 2) for z in range(HZ)]
        lows = [(tail + 2, 0), (tail + 2, 1)] + list(zip(packed, sides))
        highs = list(zip(packed, sides)) + [(tail + 2, 0), (tail + 2, 1)]
        for index in range(14):
            low, high = block(0, lows[index][0]), block(1, highs[index][0])
            if lows[index][1] == 1:
                low = pltpu.roll(low, 64, 1)
            if highs[index][1] == 0:
                high = pltpu.roll(high, 64, 1)
            pair[1 + index, rows] = jnp.where(narrow < 64, low, high)

    def mirror(planes, both):
        body = slice(8, 8 + size)
        both[0, body] = pltpu.roll(both[14, body], 64, 1)
        both[15, body] = pltpu.roll(both[1, body], 64, 1)
        planes[16, body] = pltpu.roll(planes[14, body], 64, 1)
        planes[15, body] = pltpu.roll(planes[17, body], 64, 1)

    mirror(flat, pair)
    count = 2 * CY
    lane = lax.broadcasted_iota(jnp.int32, (count, 128), 1)

    def swept(planes, index, start, scale):
        refs = [(planes[0], index), (planes[0], index + 16), (planes[1], index)]
        part = [held[z, start : start + count] for held, z in refs]
        left = [pltpu.roll(p, 1, 1) for p in part]
        right = [pltpu.roll(p, 127, 1) for p in part]
        left[2] = jnp.where(lane == 0, left[0], jnp.where(lane == 64, left[1], left[2]))
        left[0] = jnp.where(lane == 0, 0.0, left[0])
        left[1] = jnp.where(lane == 64, 0.0, left[1])
        right[0] = jnp.where(lane == 127, right[2], right[0])
        right[1] = jnp.where(lane == 63, right[2], right[1])
        right[2] = jnp.where(lane % 64 == 63, 0.0, right[2])
        done = []
        for b, (held, z) in enumerate(refs):
            around = held[z - 1, start : start + count] + held[z + 1, start : start + count]
            around += held[z, start - 1 : start - 1 + count] + held[z, start + 1 : start + 1 + count]
            around += left[b] + right[b]
            done.append((0.1 * scale) * part[b] + (0.15 * scale) * around)
        return done

    def first(index, carry):
        for start in range(8, 8 + size, count):
            done = swept((flat, pair), index, start, 1.0)
            flat2[index, start : start + count] = done[0]
            flat2[index + 16, start : start + count] = done[1]
            pair2[index, start : start + count] = done[2]
        return carry

    lax.fori_loop(1, 15, first, 0)
    whole = lax.broadcasted_iota(jnp.int32, (size, 128), 1)

    @pl.when(zone == 0)
    def _():
        flat2[2, 8 : 8 + size] = jnp.zeros((size, 128), F32)
        pair2[2, 8 : 8 + size] = jnp.where(whole < 64, 0.0, pair2[2, 8 : 8 + size])

    @pl.when(zone == 7)
    def _():
        flat2[29, 8 : 8 + size] = jnp.zeros((size, 128), F32)
        pair2[13, 8 : 8 + size] = jnp.where(whole < 64, pair2[13, 8 : 8 + size], 0.0)

    mirror(flat2, pair2)

    def emit(z):
        return pltpu.make_async_copy(ready.at[z + 2], out.at[z], sems.at[z])

    def second(index, carry):
        for start in range(8, 8 + size, count):
            done = swept((flat2, pair2), index, start, 1.0 / SCALE)
            rows = slice(start - 8, start - 8 + count)
            ready[index - 1, rows, :128] = done[0]
            ready[index - 1, rows, 128:] = done[2][:, :64]
            ready[index + 13, rows, :128] = pltpu.roll(done[1], 64, 1)
            ready[index + 13, rows, 128:] = pltpu.roll(done[2], 64, 1)[:, :64]

        @pl.when(index >= 3)
        def _():
            emit(index - 3).start()

        @pl.when(index <= 12)
        def _():
            emit(index + 11).start()

        return carry

    lax.fori_loop(1, 15, second, 0)

    def finish(z, carry):
        emit(z).wait()
        return carry

    lax.fori_loop(0, 24, finish, 0)


def relax(info, chunks):
    vmem = pl.BlockSpec(memory_space=pltpu.VMEM)
    return pl.pallas_call(
        relax_kernel,
        grid=(),
        in_specs=[pl.BlockSpec(memory_space=pltpu.SMEM), vmem],
        out_specs=pl.BlockSpec(memory_space=pl.ANY),
        out_shape=jax.ShapeDtypeStruct((24, 192, 192), F32),
        scratch_shapes=[
            pltpu.VMEM((32, 208, 128), F32),
            pltpu.VMEM((16, 208, 128), F32),
            pltpu.VMEM((32, 208, 128), F32),
            pltpu.VMEM((16, 208, 128), F32),
            pltpu.VMEM((28, 192, 192), F32),
            pltpu.SemaphoreType.DMA((24,)),
        ],
        name="relax",
    )(info, chunks)


def update(images, momenta, assign):
    level = lax.axis_index("level")
    me = lax.axis_index("subj")
    zone = lax.axis_index("gz")
    info = jnp.stack([level, me, zone]).astype(jnp.int32)
    zones = lax.axis_size("gz")
    outward = [(g, g + 1) for g in range(zones - 1)]
    outward += [(zones + g + 1, zones + g) for g in range(zones - 1)]
    nearest = ("level", "gz")
    cross = [(zones + g, g + 1) for g in range(zones - 1)]
    cross += [(g + 1, zones + g) for g in range(zones - 1)]
    climb = [(g, zones + g) for g in range(zones)]
    climb += [(zones + g, g + 1) for g in range(zones - 1)]
    rim = lax.dynamic_slice_in_dim(momenta[0], 9 * (1 - level), 3, axis=0)
    other = lax.dynamic_slice_in_dim(momenta[1], 9 * level, 3, axis=0)
    rim = lax.ppermute(rim, nearest, outward)
    other = lax.ppermute(other, nearest, cross)

    def spread(parts):
        return [parts[0]] + [
            lax.ppermute(parts[k], "subj", [(i, i ^ k) for i in range(8)]) for k in range(1, 8)
        ]

    packed = pack_images(info, images)
    planes = spread(packed)
    blurred = blur(info, momenta, rim, other)
    fields = spread(blurred)
    low, high = edges(planes)
    below = lax.ppermute(high, nearest, climb)
    above = lax.ppermute(low, nearest, [(b, a) for a, b in climb])
    chunk, edge = warp(info, assign, planes, fields, below, above)
    edge = lax.ppermute(edge.astype(jnp.float16), nearest, cross)
    chunk = jnp.concatenate([chunk.astype(jnp.float16), edge], axis=0)
    gathered = []
    for far in range(2):
        for step in range(4):
            part = chunk
            if far or step:
                perm = [
                    (8 * a + i, 8 * (a ^ far) + (i ^ (2 * step))) for a in range(2) for i in range(8)
                ]
                part = lax.ppermute(chunk, ("level", "subj"), perm)
            gathered.append(part)
            gathered.append(lax.ppermute(part, "subj", [(i, i ^ 1) for i in range(8)]))
    chunks = jnp.stack(gathered).astype(F32)
    return relax(info, chunks)


def solution(mesh):
    return jax.shard_map(
        update,
        mesh=mesh,
        in_specs=(P("subj", "gz", None, None), P("subj", "gz", None, None, None), P()),
        out_specs=P("gz", None, None),
        check_vma=False,
    )
```

```python
import jax
import jax.numpy as jnp
import numpy as np
from jax import lax
from jax.experimental import pallas as pl
from jax.experimental.pallas import tpu as pltpu
from jax.sharding import PartitionSpec as P


F32 = jnp.float32
BF16 = jnp.bfloat16
HZ = 12
CY = 24
CZ = HZ // 2 + 2
CW = CY // 2 + 2
VR = CZ * CW
VROWS = 5 * VR
PROWS = 80
SCALE = 128.0


def lerp_table(fine):
    table = np.zeros((fine, fine // 2 + 2), np.float32)
    for row in range(fine):
        near = row // 2 + 1
        table[row, near] += 0.75
        table[row, near + 2 * (row % 2) - 1] += 0.25
    return table


def zy_table():
    return np.kron(lerp_table(HZ), lerp_table(CY))


def x_table(fine, slot):
    inner = lerp_table(fine)[:, 1:-1].T
    coarse = fine // 2
    table = np.zeros((256, 256), np.float32)
    for base in (0, 128):
        table[base : base + coarse, :128] = inner[:, :128]
        table[base : base + coarse, 128 + 64 * slot : 192 + 64 * slot] = inner[:, 128:]
    return table


def pack_plane(plane, put):
    count = plane.shape[1] // CY
    low = [plane[0][:, :128], plane[1][:, :128]]
    both = jnp.concatenate([plane[0][:, 128:], plane[1][:, 128:]], axis=1)
    parts = low + [both]
    row = lax.broadcasted_iota(jnp.int32, (8, 128), 0)
    for peer in range(count):
        start = CY * peer
        halo = jnp.zeros((8, 128), F32)
        for index, part in enumerate(parts):
            if peer > 0:
                halo = jnp.where(row == 2 * index, part[start - 1 : start], halo)
            if peer < count - 1:
                halo = jnp.where(row == 2 * index + 1, part[start + CY : start + CY + 1], halo)
        blocks = [part[start : start + CY] for part in parts] + [halo]
        put(peer, jnp.concatenate(blocks, axis=0))


GROUPS = ((0, 3), (3, 3), (6, 3), (9, 3))


def pack_kernel(info, images, *rest):
    outs = rest[:8]
    held, stage, sems, gone = rest[8:]
    level, me = info[0], info[1]
    loads = []
    for index, (first, count) in enumerate(GROUPS):
        rows = pl.ds(HZ * level + first, count)
        loads.append(
            pltpu.make_async_copy(
                images.at[:, rows], held.at[:, pl.ds(first, count)], sems.at[index]
            )
        )
    for copy in loads:
        copy.start()
    sent = []
    for index, (first, count) in enumerate(GROUPS):
        loads[index].wait()

        def step(z, carry):
            def put(peer, value):
                stage[peer, z] = value.astype(BF16)

            pack_plane(held[:, z].astype(F32), put)
            return carry

        lax.fori_loop(first, first + count, step, 0)
        for k, out in enumerate(outs):
            rows = pl.ds(first, count)
            copy = pltpu.make_async_copy(
                stage.at[me ^ k, rows], out.at[rows], gone.at[8 * index + k]
            )
            copy.start()
            sent.append(copy)
    for copy in sent:
        copy.wait()


def pack_images(info, images):
    hbm = pl.BlockSpec(memory_space=pl.ANY)
    return pl.pallas_call(
        pack_kernel,
        grid=(),
        in_specs=[pl.BlockSpec(memory_space=pltpu.SMEM), hbm],
        out_specs=[hbm] * 8,
        out_shape=[jax.ShapeDtypeStruct((HZ, PROWS, 128), BF16)] * 8,
        scratch_shapes=[
            pltpu.VMEM((2, HZ, 192, 192), BF16),
            pltpu.VMEM((8, HZ, PROWS, 128), BF16),
            pltpu.SemaphoreType.DMA((len(GROUPS),)),
            pltpu.SemaphoreType.DMA((8 * len(GROUPS),)),
        ],
        name="pack_images",
    )(info, images)


def blur_kernel(info, momenta, halo, other, *rest):
    outs = rest[:8]
    held, stage, tall, wide, third, piece, sems, gone = rest[8:]
    level, me = info[0], info[1]
    half = info[2] * 2 + level
    own = pltpu.make_async_copy(
        momenta.at[:, pl.ds(3 * level, 9)], held.at[:, pl.ds(3 - 3 * level, 9)], sems.at[0]
    )
    sides = [
        pltpu.make_async_copy(rows.at[0], held.at[j, pl.ds(9 * level, 3)], sems.at[1 + j])
        for j, rows in enumerate((halo, other))
    ]
    for copy in [own] + sides:
        copy.start()
    for held_rows in (tall, wide):
        held_rows[:, :8] = jnp.zeros((CZ, 8, 128), F32)
        held_rows[:, 104:] = jnp.zeros((CZ, 8, 128), F32)
    for copy in [own] + sides:
        copy.wait()
    first = (half > 0).astype(F32)
    last = (half < 15).astype(F32)
    spare = jnp.zeros((96, 32), F32)
    plane_lane = lax.broadcasted_iota(jnp.int32, (96, 128), 1)
    for subject, component in ((1, 0), (0, 0), (0, 1), (0, 2), (1, 1), (1, 2)):

        def row(r, carry, subject=subject, component=component):
            def m(t):
                return held[subject, r + t, component]

            z = (m(0) + m(4)) * 0.0625 + (m(1) + m(3)) * 0.25 + m(2) * 0.375
            z = z * jnp.where(r == 0, first, jnp.where(r == CZ - 1, last, 1.0))
            z = jnp.concatenate([z, spare], axis=1)

            def lane(k):
                return pltpu.roll(z, k % 128, 1)

            x = (lane(2) + lane(-2)) * 0.0625 + (lane(1) + lane(-1)) * 0.25 + z * 0.375
            tall[r, 8:104] = x
            y = (tall[r, 6:102] + tall[r, 10:106]) * 0.0625
            y += (tall[r, 7:103] + tall[r, 9:105]) * 0.25
            y += x * 0.375
            if (subject, component) == (1, 0):
                third[r] = y
            elif subject == 0:
                extra = pltpu.roll(third[r], 96 - 32 * component, 1)
                wide[r, 8:104] = jnp.where(plane_lane < 96, y, extra)
            else:
                wide[r, 8:104] = y
            return carry

        lax.fori_loop(0, CZ, row, 0, unroll=2)
        if (subject, component) == (1, 0):
            continue
        block = 2 * subject + component
        for peer in range(8):
            start = 8 + (CY // 2) * peer - 1
            for r in range(CZ):
                piece[CW * r : CW * (r + 1)] = wide[r, start : start + CW]
            stage[peer, VR * block : VR * (block + 1)] = piece[...].astype(BF16)
    sent = [
        pltpu.make_async_copy(stage.at[me ^ k], out, gone.at[k]) for k, out in enumerate(outs)
    ]
    for copy in sent:
        copy.start()
    for copy in sent:
        copy.wait()


def blur(info, momenta, halo, other):
    rows = VROWS
    return pl.pallas_call(
        blur_kernel,
        grid=(),
        in_specs=[
            pl.BlockSpec(memory_space=pltpu.SMEM),
            pl.BlockSpec(memory_space=pl.ANY),
            pl.BlockSpec(memory_space=pl.ANY),
            pl.BlockSpec(memory_space=pl.ANY),
        ],
        out_specs=[pl.BlockSpec(memory_space=pl.ANY)] * 8,
        out_shape=[jax.ShapeDtypeStruct((rows, 128), BF16)] * 8,
        scratch_shapes=[
            pltpu.VMEM((2, 12, 3, 96, 96), F32),
            pltpu.VMEM((8, rows, 128), BF16),
            pltpu.VMEM((CZ, 112, 128), F32),
            pltpu.VMEM((CZ, 112, 128), F32),
            pltpu.VMEM((CZ, 96, 128), F32),
            pltpu.VMEM((VR, 128), F32),
            pltpu.SemaphoreType.DMA((3,)),
            pltpu.SemaphoreType.DMA((8,)),
        ],
        name="blur_momenta",
    )(info, momenta, halo, other)


def edge_kernel(*refs):
    planes, below, above = refs[:8], refs[8], refs[9]
    low, high, sems, gone = refs[10:]
    copies = []
    for k, plane in enumerate(planes):
        copies.append(pltpu.make_async_copy(plane.at[0], low.at[k], sems.at[k]))
        copies.append(pltpu.make_async_copy(plane.at[HZ - 1], high.at[k], sems.at[8 + k]))
    for copy in copies:
        copy.start()
    for copy in copies:
        copy.wait()
    leaving = [
        pltpu.make_async_copy(low, below, gone.at[0]),
        pltpu.make_async_copy(high, above, gone.at[1]),
    ]
    for copy in leaving:
        copy.start()
    for copy in leaving:
        copy.wait()


def edges(planes):
    hbm = pl.BlockSpec(memory_space=pl.ANY)
    shape = (8, PROWS, 128)
    return pl.pallas_call(
        edge_kernel,
        grid=(),
        in_specs=[hbm] * 8,
        out_specs=[hbm] * 2,
        out_shape=[jax.ShapeDtypeStruct(shape, BF16)] * 2,
        scratch_shapes=[
            pltpu.VMEM(shape, BF16),
            pltpu.VMEM(shape, BF16),
            pltpu.SemaphoreType.DMA((16,)),
            pltpu.SemaphoreType.DMA((2,)),
        ],
        name="cut_edges",
    )(*planes)


def warp_kernel(info, assign, zy, x0, x1, *rest):
    planes, fields, below, above = rest[:8], rest[8:16], rest[16], rest[17]
    chunk, edge = rest[18:20]
    image, field, even, odd, acc, sems = rest[20:]
    level, me = info[0], info[1]
    copies = [
        pltpu.make_async_copy(below, image.at[:, 0], sems.at[16]),
        pltpu.make_async_copy(above, image.at[:, HZ + 1], sems.at[17]),
    ]
    for k in range(8):
        copies.append(
            pltpu.make_async_copy(planes[k], image.at[k, 1 : HZ + 1], sems.at[k])
        )
        copies.append(pltpu.make_async_copy(fields[k], field.at[k], sems.at[8 + k]))
    for copy in copies:
        copy.start()
    acc[...] = jnp.zeros_like(acc)
    for copy in copies:
        copy.wait()
    lane = lax.broadcasted_iota(jnp.int32, (CY, 128), 1)
    sub = lax.broadcasted_iota(jnp.int32, (CY, 128), 0)
    coarse_lane = lax.broadcasted_iota(jnp.int32, (VR, 128), 1)

    def neighbours(part):
        left0, left1, left2 = (pltpu.roll(p, 1, 1) for p in part)
        right0, right1, right2 = (pltpu.roll(p, 127, 1) for p in part)
        left2 = jnp.where(lane == 0, left0, jnp.where(lane == 64, pltpu.roll(part[1], 65, 1), left2))
        left0 = jnp.where(lane == 0, 0.0, left0)
        left1 = jnp.where(lane == 0, 0.0, left1)
        right0 = jnp.where(lane == 127, right2, right0)
        right1 = jnp.where(lane == 127, pltpu.roll(part[2], 63, 1), right1)
        right2 = jnp.where(lane % 64 == 63, 0.0, right2)
        return (left0, left1, left2), (right0, right1, right2)

    def interpolate(k, velocity):
        base = 2 * (me ^ k)
        slots = [(assign[base + j] // 2) ^ me for j in range(2)]
        stacked = [[], []]
        for c in range(3):
            parts = [field[slots[0], VR * c : VR * (c + 1)]]
            if c > 0:
                parts.append(field[slots[1], VR * (c + 2) : VR * (c + 3)])
            else:
                spread = [
                    pltpu.roll(
                        field[slots[1], VR * t : VR * (t + 1)].astype(F32), 32 * t + 32, 1
                    )
                    for t in range(3)
                ]
                third = jnp.where(
                    coarse_lane < 32, spread[0], jnp.where(coarse_lane < 64, spread[1], spread[2])
                )
                parts.append(third.astype(BF16))
            rough = jnp.dot(
                zy[...], jnp.concatenate(parts, axis=1), preferred_element_type=F32
            )
            high = rough.astype(BF16)
            low = (rough - high.astype(F32)).astype(BF16)
            for j in range(2):
                own = slice(128 * j, 128 * j + 128)
                stacked[j].append(jnp.concatenate([high[:, own], low[:, own]], axis=1))
        fine = [
            jnp.dot(jnp.concatenate(stacked[j], axis=0), table[...], preferred_element_type=F32)
            for j, table in enumerate((x0, x1))
        ]
        velocity[0] = fine[0][:, :128]
        velocity[1] = fine[1][:, :128]
        velocity[2] = fine[0][:, 128:] + fine[1][:, 128:]

    def apply(k, velocity):
        for z in range(HZ):
            before = image[k, z].astype(F32)
            centre = image[k, z + 1].astype(F32)
            after = image[k, z + 2].astype(F32)
            part = [centre[CY * b : CY * (b + 1)] for b in range(3)]
            halo = centre[3 * CY :]
            left, right = neighbours(part)
            warped = []
            for b in range(3):
                own = slice(CY * b, CY * (b + 1))
                up = jnp.where(sub == 0, halo[2 * b : 2 * b + 1], pltpu.roll(part[b], 1, 0))
                down = jnp.where(
                    sub == CY - 1, halo[2 * b + 1 : 2 * b + 2], pltpu.roll(part[b], CY - 1, 0)
                )

                def v(c):
                    start = HZ * CY * c + CY * z
                    return velocity[b, start : start + CY]

                push = v(0) * (right[b] - left[b]) + v(1) * (down - up)
                push += v(2) * (after[own] - before[own])
                warped.append(part[b] - 0.5 * push)
            rows = slice(CY * z, CY * (z + 1))
            acc[0, rows] += warped[0] + warped[1]
            acc[1, rows] += warped[2]

    interpolate(0, even)

    def turn(step, carry):
        interpolate(2 * step + 1, odd)
        apply(2 * step, even)
        interpolate(jnp.minimum(2 * step + 2, 7), even)
        apply(2 * step + 1, odd)
        return carry

    lax.fori_loop(0, 4, turn, 0)
    weight = SCALE / 16.0
    chunk[: HZ * CY] = pltpu.roll(acc[0] * weight, 64 * level, 1)
    wide = lax.broadcasted_iota(jnp.int32, (CY, 128), 1)

    def joined(z, other):
        one, two = (acc[1, pl.ds(pl.multiple_of(r * CY, 8), CY)] for r in (z, other))
        one = one + pltpu.roll(one, 64, 1)
        two = two + pltpu.roll(two, 64, 1)
        return jnp.where(wide < 64, one, two) * weight

    for z in range(HZ // 2):
        chunk[(HZ + z) * CY : (HZ + z + 1) * CY] = joined(z, z + HZ // 2)
    outer = (HZ - 2) * level
    rim = acc[0, pl.ds(pl.multiple_of(outer * CY, 8), 2 * CY)] * weight
    edge[: 2 * CY] = pltpu.roll(rim, 64 - 64 * level, 1)
    edge[2 * CY :] = joined(outer, outer + 1)


def warp(info, assign, planes, fields, below, above):
    tables = [
        jnp.asarray(t, BF16) for t in (zy_table(), x_table(192, 0), x_table(192, 1))
    ]
    vmem = pl.BlockSpec(memory_space=pltpu.VMEM)
    smem = pl.BlockSpec(memory_space=pltpu.SMEM)
    hbm = pl.BlockSpec(memory_space=pl.ANY)
    return pl.pallas_call(
        warp_kernel,
        grid=(),
        in_specs=[smem, smem, vmem, vmem, vmem] + [hbm] * 18,
        out_specs=[vmem] * 2,
        out_shape=[
            jax.ShapeDtypeStruct((HZ * CY * 3 // 2, 128), F32),
            jax.ShapeDtypeStruct((3 * CY, 128), F32),
        ],
        scratch_shapes=[
            pltpu.VMEM((8, HZ + 2, PROWS, 128), BF16),
            pltpu.VMEM((8, VROWS, 128), BF16),
            pltpu.VMEM((3, 3 * HZ * CY, 128), F32),
            pltpu.VMEM((3, 3 * HZ * CY, 128), F32),
            pltpu.VMEM((2, HZ * CY, 128), F32),
            pltpu.SemaphoreType.DMA((18,)),
        ],
        name="warp_sum",
    )(info, assign, *tables, *planes, *fields, below, above)


def relax_kernel(info, chunks, out, flat, pair, flat2, pair2, even, odd, ready, sems):
    level, me, zone = info[0], info[1], info[2]
    size = flat.shape[1] - 16
    for held in (flat, pair, flat2, pair2):
        held[:, :8] = jnp.zeros((held.shape[0], 8, 128), F32)
        held[:, size + 8 :] = jnp.zeros((held.shape[0], 8, 128), F32)
    for held in (flat, flat2):
        for z in (0, held.shape[0] - 1):
            held[z, 8 : 8 + size] = jnp.zeros((size, 128), F32)
    narrow = lax.broadcasted_iota(jnp.int32, (CY, 128), 1)
    tail = HZ * 3 // 2
    for peer in range(8):
        rows = slice(8 + CY * peer, 8 + CY * (peer + 1))
        slots = [(half ^ level) * 8 + (peer ^ me) for half in range(2)]

        def block(half, index):
            return chunks[slots[half], CY * index : CY * (index + 1)]

        for half in range(2):
            for z in range(HZ):
                flat[3 + 14 * half + z, rows] = block(half, z)
            for z in range(2):
                flat[1 + 28 * half + z, rows] = block(half, tail + z)
        packed = [HZ + z % (HZ // 2) for z in range(HZ)]
        sides = [z // (HZ // 2) for z in range(HZ)]
        lows = [(tail + 2, 0), (tail + 2, 1)] + list(zip(packed, sides))
        highs = list(zip(packed, sides)) + [(tail + 2, 0), (tail + 2, 1)]
        for index in range(14):
            low, high = block(0, lows[index][0]), block(1, highs[index][0])
            if lows[index][1] == 1:
                low = pltpu.roll(low, 64, 1)
            if highs[index][1] == 0:
                high = pltpu.roll(high, 64, 1)
            pair[1 + index, rows] = jnp.where(narrow < 64, low, high)

    def mirror(planes, both):
        body = slice(8, 8 + size)
        both[0, body] = pltpu.roll(both[14, body], 64, 1)
        both[15, body] = pltpu.roll(both[1, body], 64, 1)
        planes[16, body] = pltpu.roll(planes[14, body], 64, 1)
        planes[15, body] = pltpu.roll(planes[17, body], 64, 1)

    mirror(flat, pair)
    count = 2 * CY
    lane = lax.broadcasted_iota(jnp.int32, (count, 128), 1)

    def shift(planes, index, sums):
        for start in range(8, 8 + size, count):
            refs = [(planes[0], index), (planes[0], index + 16), (planes[1], index)]
            part = [held[z, start : start + count] for held, z in refs]
            left = [pltpu.roll(p, 1, 1) for p in part]
            right = [pltpu.roll(p, 127, 1) for p in part]
            left[2] = jnp.where(lane == 0, left[0], jnp.where(lane == 64, left[1], left[2]))
            left[0] = jnp.where(lane == 0, 0.0, left[0])
            left[1] = jnp.where(lane == 64, 0.0, left[1])
            right[0] = jnp.where(lane == 127, right[2], right[0])
            right[1] = jnp.where(lane == 63, right[2], right[1])
            right[2] = jnp.where(lane % 64 == 63, 0.0, right[2])
            for b in range(3):
                sums[b, start - 8 : start - 8 + count] = left[b] + right[b]

    def swept(planes, index, sums, start, scale):
        refs = [(planes[0], index), (planes[0], index + 16), (planes[1], index)]
        done = []
        for b, (held, z) in enumerate(refs):
            around = held[z - 1, start : start + count] + held[z + 1, start : start + count]
            around += held[z, start - 1 : start - 1 + count] + held[z, start + 1 : start + 1 + count]
            around += sums[b, start - 8 : start - 8 + count]
            done.append(
                (0.1 * scale) * held[z, start : start + count] + (0.15 * scale) * around
            )
        return done

    def sweep(planes, store, scale, after):
        shift(planes, 1, even)

        def turn(step, carry):
            index = 2 * step + 1
            shift(planes, index + 1, odd)
            for start in range(8, 8 + size, count):
                store(index, start, swept(planes, index, even, start, scale))
            shift(planes, jnp.minimum(index + 2, 14), even)
            for start in range(8, 8 + size, count):
                store(index + 1, start, swept(planes, index + 1, odd, start, scale))
            after(index)
            after(index + 1)
            return carry

        lax.fori_loop(0, 7, turn, 0)

    def first(index, start, done):
        flat2[index, start : start + count] = done[0]
        flat2[index + 16, start : start + count] = done[1]
        pair2[index, start : start + count] = done[2]

    sweep((flat, pair), first, 1.0, lambda index: None)
    whole = lax.broadcasted_iota(jnp.int32, (size, 128), 1)

    @pl.when(zone == 0)
    def _():
        flat2[2, 8 : 8 + size] = jnp.zeros((size, 128), F32)
        pair2[2, 8 : 8 + size] = jnp.where(whole < 64, 0.0, pair2[2, 8 : 8 + size])

    @pl.when(zone == 7)
    def _():
        flat2[29, 8 : 8 + size] = jnp.zeros((size, 128), F32)
        pair2[13, 8 : 8 + size] = jnp.where(whole < 64, pair2[13, 8 : 8 + size], 0.0)

    mirror(flat2, pair2)

    def emit(z):
        return pltpu.make_async_copy(ready.at[z + 2], out.at[z], sems.at[z])

    def second(index, start, done):
        rows = slice(start - 8, start - 8 + count)
        ready[index - 1, rows, :128] = done[0]
        ready[index - 1, rows, 128:] = done[2][:, :64]
        ready[index + 13, rows, :128] = pltpu.roll(done[1], 64, 1)
        ready[index + 13, rows, 128:] = pltpu.roll(done[2], 64, 1)[:, :64]

    def depart(index):
        @pl.when(index >= 3)
        def _():
            emit(index - 3).start()

        @pl.when(index <= 12)
        def _():
            emit(index + 11).start()

    sweep((flat2, pair2), second, 1.0 / SCALE, depart)

    def finish(z, carry):
        emit(z).wait()
        return carry

    lax.fori_loop(0, 24, finish, 0)


def relax(info, chunks):
    vmem = pl.BlockSpec(memory_space=pltpu.VMEM)
    return pl.pallas_call(
        relax_kernel,
        grid=(),
        in_specs=[pl.BlockSpec(memory_space=pltpu.SMEM), vmem],
        out_specs=pl.BlockSpec(memory_space=pl.ANY),
        out_shape=jax.ShapeDtypeStruct((24, 192, 192), F32),
        scratch_shapes=[
            pltpu.VMEM((32, 208, 128), F32),
            pltpu.VMEM((16, 208, 128), F32),
            pltpu.VMEM((32, 208, 128), F32),
            pltpu.VMEM((16, 208, 128), F32),
            pltpu.VMEM((3, 192, 128), F32),
            pltpu.VMEM((3, 192, 128), F32),
            pltpu.VMEM((28, 192, 192), F32),
            pltpu.SemaphoreType.DMA((24,)),
        ],
        name="relax",
    )(info, chunks)


def update(images, momenta, assign):
    level = lax.axis_index("level")
    me = lax.axis_index("subj")
    zone = lax.axis_index("gz")
    info = jnp.stack([level, me, zone]).astype(jnp.int32)
    zones = lax.axis_size("gz")
    outward = [(g, g + 1) for g in range(zones - 1)]
    outward += [(zones + g + 1, zones + g) for g in range(zones - 1)]
    nearest = ("level", "gz")
    cross = [(zones + g, g + 1) for g in range(zones - 1)]
    cross += [(g + 1, zones + g) for g in range(zones - 1)]
    climb = [(g, zones + g) for g in range(zones)]
    climb += [(zones + g, g + 1) for g in range(zones - 1)]
    part = (1, 3) + momenta.shape[2:]
    rim = lax.dynamic_slice(momenta, (0, 9 * (1 - level), 0, 0, 0), part)
    other = lax.dynamic_slice(momenta, (1, 9 * level, 0, 0, 0), part)
    rim = lax.ppermute(rim, nearest, outward)
    other = lax.ppermute(other, nearest, cross)

    def spread(parts):
        arrived = {0: parts[0]}
        for k in (3, 7, 5, 2, 6, 4, 1):
            arrived[k] = lax.ppermute(parts[k], "subj", [(i, i ^ k) for i in range(8)])
        return [arrived[k] for k in range(8)]

    packed = pack_images(info, images)
    planes = spread(packed)
    blurred = blur(info, momenta, rim, other)
    fields = spread(blurred)
    low, high = edges(planes)
    below = lax.ppermute(high, nearest, climb)
    above = lax.ppermute(low, nearest, [(b, a) for a, b in climb])
    chunk, edge = warp(info, assign, planes, fields, below, above)
    edge = lax.ppermute(edge.astype(jnp.float16), nearest, cross)
    chunk = jnp.concatenate([chunk.astype(jnp.float16), edge], axis=0)
    mine = {(0, 0): chunk}
    for far, step in ((0, 1), (0, 3), (1, 0), (0, 2), (1, 1), (1, 3), (1, 2)):
        perm = [(8 * a + i, 8 * (a ^ far) + (i ^ (2 * step))) for a in range(2) for i in range(8)]
        mine[far, step] = lax.ppermute(chunk, ("level", "subj"), perm)
    gathered = []
    for far in range(2):
        for step in range(4):
            part = mine[far, step]
            gathered += [part, lax.ppermute(part, "subj", [(i, i ^ 1) for i in range(8)])]
    chunks = jnp.stack(gathered).astype(F32)
    return relax(info, chunks)


def solution(mesh):
    return jax.shard_map(
        update,
        mesh=mesh,
        in_specs=(P("subj", "gz", None, None), P("subj", "gz", None, None, None), P()),
        out_specs=P("gz", None, None),
        check_vma=False,
    )
```

```python
import jax
import jax.numpy as jnp
import numpy as np
from jax import lax
from jax.experimental import pallas as pl
from jax.experimental.pallas import tpu as pltpu
from jax.sharding import PartitionSpec as P


F32 = jnp.float32
BF16 = jnp.bfloat16
HZ = 12
CY = 24
CZ = HZ // 2 + 2
CW = CY // 2 + 2
VR = CZ * CW
VROWS = 5 * VR
PROWS = 80
SPREAD = (1, 3, 7, 5, 2, 6, 4)
GATHER = ((0, 1), (0, 3), (0, 2), (1, 0), (1, 1), (1, 3), (1, 2))
SCALE = 128.0


def lerp_table(fine):
    table = np.zeros((fine, fine // 2 + 2), np.float32)
    for row in range(fine):
        near = row // 2 + 1
        table[row, near] += 0.75
        table[row, near + 2 * (row % 2) - 1] += 0.25
    return table


def zy_table():
    return np.kron(lerp_table(HZ), lerp_table(CY))


def x_table(fine, slot):
    inner = lerp_table(fine)[:, 1:-1].T
    coarse = fine // 2
    table = np.zeros((256, 256), np.float32)
    for base in (0, 128):
        table[base : base + coarse, :128] = inner[:, :128]
        table[base : base + coarse, 128 + 64 * slot : 192 + 64 * slot] = inner[:, 128:]
    return table


def pack_plane(plane, put):
    count = plane.shape[1] // CY
    low = [plane[0][:, :128], plane[1][:, :128]]
    both = jnp.concatenate([plane[0][:, 128:], plane[1][:, 128:]], axis=1)
    parts = low + [both]
    row = lax.broadcasted_iota(jnp.int32, (8, 128), 0)
    for peer in range(count):
        start = CY * peer
        halo = jnp.zeros((8, 128), F32)
        for index, part in enumerate(parts):
            if peer > 0:
                halo = jnp.where(row == 2 * index, part[start - 1 : start], halo)
            if peer < count - 1:
                halo = jnp.where(row == 2 * index + 1, part[start + CY : start + CY + 1], halo)
        blocks = [part[start : start + CY] for part in parts] + [halo]
        put(peer, jnp.concatenate(blocks, axis=0))


GROUPS = ((0, 3), (3, 3), (6, 3), (9, 3))


def pack_kernel(info, images, *rest):
    outs = rest[:8]
    held, stage, sems, gone = rest[8:]
    level, me = info[0], info[1]
    loads = []
    for index, (first, count) in enumerate(GROUPS):
        rows = pl.ds(HZ * level + first, count)
        loads.append(
            pltpu.make_async_copy(
                images.at[:, rows], held.at[:, pl.ds(first, count)], sems.at[index]
            )
        )
    for copy in loads:
        copy.start()
    sent = []
    for index, (first, count) in enumerate(GROUPS):
        loads[index].wait()

        def step(z, carry):
            def put(peer, value):
                stage[peer, z] = value.astype(BF16)

            pack_plane(held[:, z].astype(F32), put)
            return carry

        lax.fori_loop(first, first + count, step, 0)
        for k, out in enumerate(outs):
            rows = pl.ds(first, count)
            copy = pltpu.make_async_copy(
                stage.at[me ^ k, rows], out.at[rows], gone.at[8 * index + k]
            )
            copy.start()
            sent.append(copy)
    for copy in sent:
        copy.wait()


def pack_images(info, images):
    hbm = pl.BlockSpec(memory_space=pl.ANY)
    return pl.pallas_call(
        pack_kernel,
        grid=(),
        in_specs=[pl.BlockSpec(memory_space=pltpu.SMEM), hbm],
        out_specs=[hbm] * 8,
        out_shape=[jax.ShapeDtypeStruct((HZ, PROWS, 128), BF16)] * 8,
        scratch_shapes=[
            pltpu.VMEM((2, HZ, 192, 192), BF16),
            pltpu.VMEM((8, HZ, PROWS, 128), BF16),
            pltpu.SemaphoreType.DMA((len(GROUPS),)),
            pltpu.SemaphoreType.DMA((8 * len(GROUPS),)),
        ],
        name="pack_images",
    )(info, images)


def blur_kernel(info, momenta, halo, other, *rest):
    outs = rest[:8]
    held, stage, tall, wide, third, piece, sems, gone = rest[8:]
    level, me = info[0], info[1]
    half = info[2] * 2 + level
    own = pltpu.make_async_copy(
        momenta.at[:, pl.ds(3 * level, 9)], held.at[:, pl.ds(3 - 3 * level, 9)], sems.at[0]
    )
    sides = [
        pltpu.make_async_copy(rows.at[0], held.at[j, pl.ds(9 * level, 3)], sems.at[1 + j])
        for j, rows in enumerate((halo, other))
    ]
    for copy in [own] + sides:
        copy.start()
    for held_rows in (tall, wide):
        held_rows[:, :8] = jnp.zeros((CZ, 8, 128), F32)
        held_rows[:, 104:] = jnp.zeros((CZ, 8, 128), F32)
    for copy in [own] + sides:
        copy.wait()
    first = (half > 0).astype(F32)
    last = (half < 15).astype(F32)
    spare = jnp.zeros((96, 32), F32)
    plane_lane = lax.broadcasted_iota(jnp.int32, (96, 128), 1)
    for subject, component in ((1, 0), (0, 0), (0, 1), (0, 2), (1, 1), (1, 2)):

        def row(r, carry, subject=subject, component=component):
            def m(t):
                return held[subject, r + t, component]

            z = (m(0) + m(4)) * 0.0625 + (m(1) + m(3)) * 0.25 + m(2) * 0.375
            z = z * jnp.where(r == 0, first, jnp.where(r == CZ - 1, last, 1.0))
            z = jnp.concatenate([z, spare], axis=1)

            def lane(k):
                return pltpu.roll(z, k % 128, 1)

            x = (lane(2) + lane(-2)) * 0.0625 + (lane(1) + lane(-1)) * 0.25 + z * 0.375
            tall[r, 8:104] = x
            y = (tall[r, 6:102] + tall[r, 10:106]) * 0.0625
            y += (tall[r, 7:103] + tall[r, 9:105]) * 0.25
            y += x * 0.375
            if (subject, component) == (1, 0):
                third[r] = y
            elif subject == 0:
                extra = pltpu.roll(third[r], 96 - 32 * component, 1)
                wide[r, 8:104] = jnp.where(plane_lane < 96, y, extra)
            else:
                wide[r, 8:104] = y
            return carry

        lax.fori_loop(0, CZ, row, 0, unroll=2)
        if (subject, component) == (1, 0):
            continue
        block = 2 * subject + component
        for peer in range(8):
            start = 8 + (CY // 2) * peer - 1
            for r in range(CZ):
                piece[CW * r : CW * (r + 1)] = wide[r, start : start + CW]
            stage[peer, VR * block : VR * (block + 1)] = piece[...].astype(BF16)
    sent = [
        pltpu.make_async_copy(stage.at[me ^ k], out, gone.at[k]) for k, out in enumerate(outs)
    ]
    for copy in sent:
        copy.start()
    for copy in sent:
        copy.wait()


def blur(info, momenta, halo, other):
    rows = VROWS
    return pl.pallas_call(
        blur_kernel,
        grid=(),
        in_specs=[
            pl.BlockSpec(memory_space=pltpu.SMEM),
            pl.BlockSpec(memory_space=pl.ANY),
            pl.BlockSpec(memory_space=pl.ANY),
            pl.BlockSpec(memory_space=pl.ANY),
        ],
        out_specs=[pl.BlockSpec(memory_space=pl.ANY)] * 8,
        out_shape=[jax.ShapeDtypeStruct((rows, 128), BF16)] * 8,
        scratch_shapes=[
            pltpu.VMEM((2, 12, 3, 96, 96), F32),
            pltpu.VMEM((8, rows, 128), BF16),
            pltpu.VMEM((CZ, 112, 128), F32),
            pltpu.VMEM((CZ, 112, 128), F32),
            pltpu.VMEM((CZ, 96, 128), F32),
            pltpu.VMEM((VR, 128), F32),
            pltpu.SemaphoreType.DMA((3,)),
            pltpu.SemaphoreType.DMA((8,)),
        ],
        name="blur_momenta",
    )(info, momenta, halo, other)


def edge_kernel(*refs):
    planes, below, above = refs[:8], refs[8], refs[9]
    low, high, sems, gone = refs[10:]
    copies = []
    for k, plane in enumerate(planes):
        copies.append(pltpu.make_async_copy(plane.at[0], low.at[k], sems.at[k]))
        copies.append(pltpu.make_async_copy(plane.at[HZ - 1], high.at[k], sems.at[8 + k]))
    for copy in copies:
        copy.start()
    for copy in copies:
        copy.wait()
    leaving = [
        pltpu.make_async_copy(low, below, gone.at[0]),
        pltpu.make_async_copy(high, above, gone.at[1]),
    ]
    for copy in leaving:
        copy.start()
    for copy in leaving:
        copy.wait()


def edges(planes):
    hbm = pl.BlockSpec(memory_space=pl.ANY)
    shape = (8, PROWS, 128)
    return pl.pallas_call(
        edge_kernel,
        grid=(),
        in_specs=[hbm] * 8,
        out_specs=[hbm] * 2,
        out_shape=[jax.ShapeDtypeStruct(shape, BF16)] * 2,
        scratch_shapes=[
            pltpu.VMEM(shape, BF16),
            pltpu.VMEM(shape, BF16),
            pltpu.SemaphoreType.DMA((16,)),
            pltpu.SemaphoreType.DMA((2,)),
        ],
        name="cut_edges",
    )(*planes)


def warp_kernel(info, assign, zy, x0, x1, *rest):
    planes, fields, below, above = rest[:8], rest[8:16], rest[16], rest[17]
    chunk, upward, downward = rest[18:21]
    image, field, even, odd, acc, sems = rest[21:]
    me = info[1]
    copies = [
        pltpu.make_async_copy(below, image.at[:, 0], sems.at[16]),
        pltpu.make_async_copy(above, image.at[:, HZ + 1], sems.at[17]),
    ]
    for k in range(8):
        copies.append(
            pltpu.make_async_copy(planes[k], image.at[k, 1 : HZ + 1], sems.at[k])
        )
        copies.append(pltpu.make_async_copy(fields[k], field.at[k], sems.at[8 + k]))
    for copy in copies:
        copy.start()
    acc[...] = jnp.zeros_like(acc)
    for copy in copies:
        copy.wait()
    lane = lax.broadcasted_iota(jnp.int32, (CY, 128), 1)
    sub = lax.broadcasted_iota(jnp.int32, (CY, 128), 0)
    coarse_lane = lax.broadcasted_iota(jnp.int32, (VR, 128), 1)

    def neighbours(part):
        left0, left1, left2 = (pltpu.roll(p, 1, 1) for p in part)
        right0, right1, right2 = (pltpu.roll(p, 127, 1) for p in part)
        left2 = jnp.where(lane == 0, left0, jnp.where(lane == 64, pltpu.roll(part[1], 65, 1), left2))
        left0 = jnp.where(lane == 0, 0.0, left0)
        left1 = jnp.where(lane == 0, 0.0, left1)
        right0 = jnp.where(lane == 127, right2, right0)
        right1 = jnp.where(lane == 127, pltpu.roll(part[2], 63, 1), right1)
        right2 = jnp.where(lane % 64 == 63, 0.0, right2)
        return (left0, left1, left2), (right0, right1, right2)

    def interpolate(k, velocity):
        base = 2 * (me ^ k)
        slots = [(assign[base + j] // 2) ^ me for j in range(2)]
        stacked = [[], []]
        for c in range(3):
            parts = [field[slots[0], VR * c : VR * (c + 1)]]
            if c > 0:
                parts.append(field[slots[1], VR * (c + 2) : VR * (c + 3)])
            else:
                spread = [
                    pltpu.roll(
                        field[slots[1], VR * t : VR * (t + 1)].astype(F32), 32 * t + 32, 1
                    )
                    for t in range(3)
                ]
                third = jnp.where(
                    coarse_lane < 32, spread[0], jnp.where(coarse_lane < 64, spread[1], spread[2])
                )
                parts.append(third.astype(BF16))
            rough = jnp.dot(
                zy[...], jnp.concatenate(parts, axis=1), preferred_element_type=F32
            )
            high = rough.astype(BF16)
            low = (rough - high.astype(F32)).astype(BF16)
            for j in range(2):
                own = slice(128 * j, 128 * j + 128)
                stacked[j].append(jnp.concatenate([high[:, own], low[:, own]], axis=1))
        fine = [
            jnp.dot(jnp.concatenate(stacked[j], axis=0), table[...], preferred_element_type=F32)
            for j, table in enumerate((x0, x1))
        ]
        velocity[0] = fine[0][:, :128]
        velocity[1] = fine[1][:, :128]
        velocity[2] = fine[0][:, 128:] + fine[1][:, 128:]

    def apply(k, velocity):
        for z in range(HZ):
            before = image[k, z].astype(F32)
            centre = image[k, z + 1].astype(F32)
            after = image[k, z + 2].astype(F32)
            part = [centre[CY * b : CY * (b + 1)] for b in range(3)]
            halo = centre[3 * CY :]
            left, right = neighbours(part)
            warped = []
            for b in range(3):
                own = slice(CY * b, CY * (b + 1))
                up = jnp.where(sub == 0, halo[2 * b : 2 * b + 1], pltpu.roll(part[b], 1, 0))
                down = jnp.where(
                    sub == CY - 1, halo[2 * b + 1 : 2 * b + 2], pltpu.roll(part[b], CY - 1, 0)
                )

                def v(c):
                    start = HZ * CY * c + CY * z
                    return velocity[b, start : start + CY]

                push = v(0) * (right[b] - left[b]) + v(1) * (down - up)
                push += v(2) * (after[own] - before[own])
                warped.append(part[b] - 0.5 * push)
            rows = slice(CY * z, CY * (z + 1))
            acc[0, rows] += warped[0] + warped[1]
            acc[1, rows] += warped[2]

    interpolate(0, even)

    def turn(step, carry):
        interpolate(2 * step + 1, odd)
        apply(2 * step, even)
        interpolate(jnp.minimum(2 * step + 2, 7), even)
        apply(2 * step + 1, odd)
        return carry

    lax.fori_loop(0, 4, turn, 0)
    weight = SCALE / 16.0
    middle = HZ * CY // 2
    chunk[:middle] = acc[0, :middle] * weight
    chunk[middle : 2 * middle] = pltpu.roll(acc[0, middle:] * weight, 64, 1)

    def joined(one, two):
        one, two = (acc[1, r * CY : (r + 1) * CY] for r in (one, two))
        one = one + pltpu.roll(one, 64, 1)
        two = two + pltpu.roll(two, 64, 1)
        return jnp.where(lane < 64, one, two) * weight

    for z in range(HZ // 2):
        chunk[(HZ + z) * CY : (HZ + z + 1) * CY] = joined(z, z + HZ // 2)
    rows = slice((HZ - 2) * CY, HZ * CY)
    upward[: 2 * CY] = acc[0, rows] * weight
    upward[2 * CY :] = joined(HZ - 2, HZ - 1)
    downward[: 2 * CY] = pltpu.roll(acc[0, : 2 * CY] * weight, 64, 1)
    downward[2 * CY :] = joined(1, 0)


def warp(info, assign, planes, fields, below, above):
    tables = [
        jnp.asarray(t, BF16) for t in (zy_table(), x_table(192, 0), x_table(192, 1))
    ]
    vmem = pl.BlockSpec(memory_space=pltpu.VMEM)
    smem = pl.BlockSpec(memory_space=pltpu.SMEM)
    hbm = pl.BlockSpec(memory_space=pl.ANY)
    return pl.pallas_call(
        warp_kernel,
        grid=(),
        in_specs=[smem, smem, vmem, vmem, vmem] + [hbm] * 18,
        out_specs=[vmem] * 3,
        out_shape=[
            jax.ShapeDtypeStruct((HZ * CY * 3 // 2, 128), F32),
            jax.ShapeDtypeStruct((3 * CY, 128), F32),
            jax.ShapeDtypeStruct((3 * CY, 128), F32),
        ],
        scratch_shapes=[
            pltpu.VMEM((8, HZ + 2, PROWS, 128), BF16),
            pltpu.VMEM((8, VROWS, 128), BF16),
            pltpu.VMEM((3, 3 * HZ * CY, 128), F32),
            pltpu.VMEM((3, 3 * HZ * CY, 128), F32),
            pltpu.VMEM((2, HZ * CY, 128), F32),
            pltpu.SemaphoreType.DMA((18,)),
        ],
        name="warp_sum",
    )(info, assign, *tables, *planes, *fields, below, above)


COUNT = HZ // 2 + 2


def relax_kernel(info, chunks, *rest):
    out, flat, pair, flat2, pair2, even, odd, ready, sems = rest[-9:]
    far = len(rest) - 9
    me, zone = info[1], info[2]
    half = info[0] ^ far
    size = flat.shape[1] - 16
    high = COUNT + 2
    for held in (flat, pair, flat2, pair2):
        held[:, :8] = jnp.zeros((held.shape[0], 8, 128), F32)
        held[:, size + 8 :] = jnp.zeros((held.shape[0], 8, 128), F32)
    for held in (flat, flat2):
        for z in (0, held.shape[0] - 1):
            held[z, 8 : 8 + size] = jnp.zeros((size, 128), F32)
    narrow = lax.broadcasted_iota(jnp.int32, (CY, 128), 1)
    tail = HZ * 3 // 2
    for peer in range(8):
        rows = slice(8 + CY * peer, 8 + CY * (peer + 1))
        slot = peer ^ me

        def block(index):
            return chunks[slot, CY * index : CY * (index + 1)]

        for z in range(HZ // 2):
            flat[3 + z, rows] = block(z)
            flat[high + 1 + z, rows] = block(z + HZ // 2)
        for z in range(2):
            flat[1 + z, rows] = block(tail + z)
            flat[high + COUNT - 1 + z, rows] = block(tail + 3 + z)
        under, over = block(tail + 2), block(tail + 5)
        lows = [under, pltpu.roll(under, 64, 1)] + [block(HZ + z) for z in range(HZ // 2)]
        highs = [block(HZ + z) for z in range(HZ // 2)] + [over, pltpu.roll(over, 64, 1)]
        for index in range(COUNT):
            pair[1 + index, rows] = jnp.where(narrow < 64, lows[index], highs[index])

    def mirror(planes, both):
        body = slice(8, 8 + size)
        both[0, body] = pltpu.roll(both[COUNT, body], 64, 1)
        both[COUNT + 1, body] = pltpu.roll(both[1, body], 64, 1)
        planes[high, body] = pltpu.roll(planes[COUNT, body], 64, 1)
        planes[COUNT + 1, body] = pltpu.roll(planes[high + 1, body], 64, 1)

    mirror(flat, pair)
    count = 2 * CY
    lane = lax.broadcasted_iota(jnp.int32, (count, 128), 1)

    def shift(planes, index, sums):
        for start in range(8, 8 + size, count):
            refs = [(planes[0], index), (planes[0], index + high), (planes[1], index)]
            part = [held[z, start : start + count] for held, z in refs]
            left = [pltpu.roll(p, 1, 1) for p in part]
            right = [pltpu.roll(p, 127, 1) for p in part]
            left[2] = jnp.where(lane == 0, left[0], jnp.where(lane == 64, left[1], left[2]))
            left[0] = jnp.where(lane == 0, 0.0, left[0])
            left[1] = jnp.where(lane == 64, 0.0, left[1])
            right[0] = jnp.where(lane == 127, right[2], right[0])
            right[1] = jnp.where(lane == 63, right[2], right[1])
            right[2] = jnp.where(lane % 64 == 63, 0.0, right[2])
            for b in range(3):
                sums[b, start - 8 : start - 8 + count] = left[b] + right[b]

    def swept(planes, index, sums, start, scale):
        refs = [(planes[0], index), (planes[0], index + high), (planes[1], index)]
        done = []
        for b, (held, z) in enumerate(refs):
            around = held[z - 1, start : start + count] + held[z + 1, start : start + count]
            around += held[z, start - 1 : start - 1 + count] + held[z, start + 1 : start + 1 + count]
            around += sums[b, start - 8 : start - 8 + count]
            done.append(
                (0.1 * scale) * held[z, start : start + count] + (0.15 * scale) * around
            )
        return done

    def sweep(planes, store, scale, after):
        shift(planes, 1, even)

        def turn(step, carry):
            index = 2 * step + 1
            shift(planes, index + 1, odd)
            for start in range(8, 8 + size, count):
                store(index, start, swept(planes, index, even, start, scale))
            shift(planes, jnp.minimum(index + 2, COUNT), even)
            for start in range(8, 8 + size, count):
                store(index + 1, start, swept(planes, index + 1, odd, start, scale))
            after(index)
            after(index + 1)
            return carry

        lax.fori_loop(0, COUNT // 2, turn, 0)

    def first(index, start, done):
        flat2[index, start : start + count] = done[0]
        flat2[index + high, start : start + count] = done[1]
        pair2[index, start : start + count] = done[2]

    sweep((flat, pair), first, 1.0, lambda index: None)
    whole = lax.broadcasted_iota(jnp.int32, (size, 128), 1)

    @pl.when(jnp.logical_and(zone == 0, half == 0))
    def _():
        flat2[2, 8 : 8 + size] = jnp.zeros((size, 128), F32)
        pair2[2, 8 : 8 + size] = jnp.where(whole < 64, 0.0, pair2[2, 8 : 8 + size])

    @pl.when(jnp.logical_and(zone == 7, half == 1))
    def _():
        flat2[high + COUNT - 1, 8 : 8 + size] = jnp.zeros((size, 128), F32)
        pair2[COUNT - 1, 8 : 8 + size] = jnp.where(whole < 64, pair2[COUNT - 1, 8 : 8 + size], 0.0)

    mirror(flat2, pair2)

    def emit(z):
        return pltpu.make_async_copy(ready.at[z + 2], out.at[HZ * half + z], sems.at[z])

    def second(index, start, done):
        rows = slice(start - 8, start - 8 + count)
        ready[index - 1, rows, :128] = done[0]
        ready[index - 1, rows, 128:] = done[2][:, :64]
        ready[index + COUNT - 1, rows, :128] = pltpu.roll(done[1], 64, 1)
        ready[index + COUNT - 1, rows, 128:] = pltpu.roll(done[2], 64, 1)[:, :64]

    def depart(index):
        @pl.when(index >= 3)
        def _():
            emit(index - 3).start()

        @pl.when(index <= COUNT - 2)
        def _():
            emit(index + COUNT - 3).start()

    sweep((flat2, pair2), second, 1.0 / SCALE, depart)

    def finish(z, carry):
        emit(z).wait()
        return carry

    lax.fori_loop(0, HZ, finish, 0)


def relax(info, chunks, *before):
    hbm = pl.BlockSpec(memory_space=pl.ANY)
    vmem = pl.BlockSpec(memory_space=pltpu.VMEM)
    held = [
        pltpu.VMEM((2 * COUNT + 4, 208, 128), F32),
        pltpu.VMEM((COUNT + 2, 208, 128), F32),
    ]
    return pl.pallas_call(
        relax_kernel,
        grid=(),
        in_specs=[pl.BlockSpec(memory_space=pltpu.SMEM), vmem] + [hbm] * len(before),
        out_specs=hbm,
        out_shape=jax.ShapeDtypeStruct((24, 192, 192), F32),
        input_output_aliases={2: 0} if before else {},
        scratch_shapes=held
        + held
        + [
            pltpu.VMEM((3, 192, 128), F32),
            pltpu.VMEM((3, 192, 128), F32),
            pltpu.VMEM((2 * COUNT, 192, 192), F32),
            pltpu.SemaphoreType.DMA((HZ,)),
        ],
        name="relax",
    )(info, chunks, *before)


def update(images, momenta, assign):
    level = lax.axis_index("level")
    me = lax.axis_index("subj")
    zone = lax.axis_index("gz")
    info = jnp.stack([level, me, zone]).astype(jnp.int32)
    zones = lax.axis_size("gz")
    outward = [(g, g + 1) for g in range(zones - 1)]
    outward += [(zones + g + 1, zones + g) for g in range(zones - 1)]
    nearest = ("level", "gz")
    cross = [(zones + g, g + 1) for g in range(zones - 1)]
    cross += [(g + 1, zones + g) for g in range(zones - 1)]
    climb = [(g, zones + g) for g in range(zones)]
    climb += [(zones + g, g + 1) for g in range(zones - 1)]
    part = (1, 3) + momenta.shape[2:]
    rim = lax.dynamic_slice(momenta, (0, 9 * (1 - level), 0, 0, 0), part)
    other = lax.dynamic_slice(momenta, (1, 9 * level, 0, 0, 0), part)
    rim = lax.ppermute(rim, nearest, outward)
    other = lax.ppermute(other, nearest, cross)

    def spread(parts):
        arrived = {0: parts[0]}
        for k in SPREAD:
            arrived[k] = lax.ppermute(parts[k], "subj", [(i, i ^ k) for i in range(8)])
        return [arrived[k] for k in range(8)]

    packed = pack_images(info, images)
    planes = spread(packed)
    blurred = blur(info, momenta, rim, other)
    fields = spread(blurred)
    low, high = edges(planes)
    below = lax.ppermute(high, nearest, climb)
    above = lax.ppermute(low, nearest, [(b, a) for a, b in climb])
    chunk, upward, downward = warp(info, assign, planes, fields, below, above)
    half = jnp.float16
    back = [(b, a) for a, b in climb]
    under = lax.ppermute(upward.astype(half), nearest, climb)
    over = lax.ppermute(downward.astype(half), nearest, back)
    chunk = jnp.concatenate([chunk.astype(half), under, over], axis=0)
    mine = {(0, 0): chunk}
    for far, step in GATHER:
        perm = [(8 * a + i, 8 * (a ^ far) + (i ^ (2 * step))) for a in range(2) for i in range(8)]
        mine[far, step] = lax.ppermute(chunk, ("level", "subj"), perm)
    result = ()
    for far in range(2):
        parts = []
        for step in range(4):
            part = mine[far, step]
            parts += [part, lax.ppermute(part, "subj", [(i, i ^ 1) for i in range(8)])]
        result = (relax(info, jnp.stack(parts).astype(F32), *result),)
    return result[0]


def solution(mesh):
    return jax.shard_map(
        update,
        mesh=mesh,
        in_specs=(P("subj", "gz", None, None), P("subj", "gz", None, None, None), P()),
        out_specs=P("gz", None, None),
        check_vma=False,
    )
```

```python
import jax
import jax.numpy as jnp
import numpy as np
from jax import lax
from jax.experimental import pallas as pl
from jax.experimental.pallas import tpu as pltpu
from jax.sharding import PartitionSpec as P


F32 = jnp.float32
BF16 = jnp.bfloat16
HZ = 12
CY = 24
CZ = HZ // 2 + 2
CW = CY // 2 + 2
VR = CZ * CW
VROWS = 5 * VR
PROWS = 80
SPREAD = (1, 3, 7, 5, 2, 6, 4)
SCALE = 128.0


def lerp_table(fine):
    table = np.zeros((fine, fine // 2 + 2), np.float32)
    for row in range(fine):
        near = row // 2 + 1
        table[row, near] += 0.75
        table[row, near + 2 * (row % 2) - 1] += 0.25
    return table


def zy_table():
    return np.kron(lerp_table(HZ), lerp_table(CY))


def x_table(fine, slot):
    inner = lerp_table(fine)[:, 1:-1].T
    coarse = fine // 2
    table = np.zeros((256, 256), np.float32)
    for base in (0, 128):
        table[base : base + coarse, :128] = inner[:, :128]
        table[base : base + coarse, 128 + 64 * slot : 192 + 64 * slot] = inner[:, 128:]
    return table


def pack_plane(plane, put):
    count = plane.shape[1] // CY
    low = [plane[0][:, :128], plane[1][:, :128]]
    both = jnp.concatenate([plane[0][:, 128:], plane[1][:, 128:]], axis=1)
    parts = low + [both]
    row = lax.broadcasted_iota(jnp.int32, (8, 128), 0)
    for peer in range(count):
        start = CY * peer
        halo = jnp.zeros((8, 128), F32)
        for index, part in enumerate(parts):
            if peer > 0:
                halo = jnp.where(row == 2 * index, part[start - 1 : start], halo)
            if peer < count - 1:
                halo = jnp.where(row == 2 * index + 1, part[start + CY : start + CY + 1], halo)
        blocks = [part[start : start + CY] for part in parts] + [halo]
        put(peer, jnp.concatenate(blocks, axis=0))


GROUPS = ((0, 3), (3, 3), (6, 3), (9, 3))


def pack_kernel(info, images, *rest):
    outs = rest[:8]
    held, stage, sems, gone = rest[8:]
    level, me = info[0], info[1]
    loads = []
    for index, (first, count) in enumerate(GROUPS):
        rows = pl.ds(HZ * level + first, count)
        loads.append(
            pltpu.make_async_copy(
                images.at[:, rows], held.at[:, pl.ds(first, count)], sems.at[index]
            )
        )
    for copy in loads:
        copy.start()
    sent = []
    for index, (first, count) in enumerate(GROUPS):
        loads[index].wait()

        def step(z, carry):
            def put(peer, value):
                stage[peer, z] = value.astype(BF16)

            pack_plane(held[:, z].astype(F32), put)
            return carry

        lax.fori_loop(first, first + count, step, 0)
        for k, out in enumerate(outs):
            rows = pl.ds(first, count)
            copy = pltpu.make_async_copy(
                stage.at[me ^ k, rows], out.at[rows], gone.at[8 * index + k]
            )
            copy.start()
            sent.append(copy)
    for copy in sent:
        copy.wait()


def pack_images(info, images):
    hbm = pl.BlockSpec(memory_space=pl.ANY)
    return pl.pallas_call(
        pack_kernel,
        grid=(),
        in_specs=[pl.BlockSpec(memory_space=pltpu.SMEM), hbm],
        out_specs=[hbm] * 8,
        out_shape=[jax.ShapeDtypeStruct((HZ, PROWS, 128), BF16)] * 8,
        scratch_shapes=[
            pltpu.VMEM((2, HZ, 192, 192), BF16),
            pltpu.VMEM((8, HZ, PROWS, 128), BF16),
            pltpu.SemaphoreType.DMA((len(GROUPS),)),
            pltpu.SemaphoreType.DMA((8 * len(GROUPS),)),
        ],
        name="pack_images",
    )(info, images)


def blur_kernel(info, momenta, halo, other, *rest):
    outs = rest[:8]
    held, stage, tall, wide, third, piece, sems, gone = rest[8:]
    level, me = info[0], info[1]
    half = info[2] * 2 + level
    own = pltpu.make_async_copy(
        momenta.at[:, pl.ds(3 * level, 9)], held.at[:, pl.ds(3 - 3 * level, 9)], sems.at[0]
    )
    sides = [
        pltpu.make_async_copy(rows.at[0], held.at[j, pl.ds(9 * level, 3)], sems.at[1 + j])
        for j, rows in enumerate((halo, other))
    ]
    for copy in [own] + sides:
        copy.start()
    for held_rows in (tall, wide):
        held_rows[:, :8] = jnp.zeros((CZ, 8, 128), F32)
        held_rows[:, 104:] = jnp.zeros((CZ, 8, 128), F32)
    for copy in [own] + sides:
        copy.wait()
    first = (half > 0).astype(F32)
    last = (half < 15).astype(F32)
    spare = jnp.zeros((96, 32), F32)
    plane_lane = lax.broadcasted_iota(jnp.int32, (96, 128), 1)
    for subject, component in ((1, 0), (0, 0), (0, 1), (0, 2), (1, 1), (1, 2)):

        def row(r, carry, subject=subject, component=component):
            def m(t):
                return held[subject, r + t, component]

            z = (m(0) + m(4)) * 0.0625 + (m(1) + m(3)) * 0.25 + m(2) * 0.375
            z = z * jnp.where(r == 0, first, jnp.where(r == CZ - 1, last, 1.0))
            z = jnp.concatenate([z, spare], axis=1)

            def lane(k):
                return pltpu.roll(z, k % 128, 1)

            x = (lane(2) + lane(-2)) * 0.0625 + (lane(1) + lane(-1)) * 0.25 + z * 0.375
            tall[r, 8:104] = x
            y = (tall[r, 6:102] + tall[r, 10:106]) * 0.0625
            y += (tall[r, 7:103] + tall[r, 9:105]) * 0.25
            y += x * 0.375
            if (subject, component) == (1, 0):
                third[r] = y
            elif subject == 0:
                extra = pltpu.roll(third[r], 96 - 32 * component, 1)
                wide[r, 8:104] = jnp.where(plane_lane < 96, y, extra)
            else:
                wide[r, 8:104] = y
            return carry

        lax.fori_loop(0, CZ, row, 0, unroll=2)
        if (subject, component) == (1, 0):
            continue
        block = 2 * subject + component
        for peer in range(8):
            start = 8 + (CY // 2) * peer - 1
            for r in range(CZ):
                piece[CW * r : CW * (r + 1)] = wide[r, start : start + CW]
            stage[peer, VR * block : VR * (block + 1)] = piece[...].astype(BF16)
    sent = [
        pltpu.make_async_copy(stage.at[me ^ k], out, gone.at[k]) for k, out in enumerate(outs)
    ]
    for copy in sent:
        copy.start()
    for copy in sent:
        copy.wait()


def blur(info, momenta, halo, other):
    rows = VROWS
    return pl.pallas_call(
        blur_kernel,
        grid=(),
        in_specs=[
            pl.BlockSpec(memory_space=pltpu.SMEM),
            pl.BlockSpec(memory_space=pl.ANY),
            pl.BlockSpec(memory_space=pl.ANY),
            pl.BlockSpec(memory_space=pl.ANY),
        ],
        out_specs=[pl.BlockSpec(memory_space=pl.ANY)] * 8,
        out_shape=[jax.ShapeDtypeStruct((rows, 128), BF16)] * 8,
        scratch_shapes=[
            pltpu.VMEM((2, 12, 3, 96, 96), F32),
            pltpu.VMEM((8, rows, 128), BF16),
            pltpu.VMEM((CZ, 112, 128), F32),
            pltpu.VMEM((CZ, 112, 128), F32),
            pltpu.VMEM((CZ, 96, 128), F32),
            pltpu.VMEM((VR, 128), F32),
            pltpu.SemaphoreType.DMA((3,)),
            pltpu.SemaphoreType.DMA((8,)),
        ],
        name="blur_momenta",
    )(info, momenta, halo, other)


def edge_kernel(*refs):
    planes, below, above = refs[:8], refs[8], refs[9]
    low, high, sems, gone = refs[10:]
    copies = []
    for k, plane in enumerate(planes):
        copies.append(pltpu.make_async_copy(plane.at[0], low.at[k], sems.at[k]))
        copies.append(pltpu.make_async_copy(plane.at[HZ - 1], high.at[k], sems.at[8 + k]))
    for copy in copies:
        copy.start()
    for copy in copies:
        copy.wait()
    leaving = [
        pltpu.make_async_copy(low, below, gone.at[0]),
        pltpu.make_async_copy(high, above, gone.at[1]),
    ]
    for copy in leaving:
        copy.start()
    for copy in leaving:
        copy.wait()


def edges(planes):
    hbm = pl.BlockSpec(memory_space=pl.ANY)
    shape = (8, PROWS, 128)
    return pl.pallas_call(
        edge_kernel,
        grid=(),
        in_specs=[hbm] * 8,
        out_specs=[hbm] * 2,
        out_shape=[jax.ShapeDtypeStruct(shape, BF16)] * 2,
        scratch_shapes=[
            pltpu.VMEM(shape, BF16),
            pltpu.VMEM(shape, BF16),
            pltpu.SemaphoreType.DMA((16,)),
            pltpu.SemaphoreType.DMA((2,)),
        ],
        name="cut_edges",
    )(*planes)


def warp_kernel(info, assign, zy, x0, x1, *rest):
    planes, fields, below, above = rest[:8], rest[8:16], rest[16], rest[17]
    chunk, edge = rest[18:20]
    image, field, even, odd, acc, sems = rest[20:]
    level, me = info[0], info[1]
    copies = [
        pltpu.make_async_copy(below, image.at[:, 0], sems.at[16]),
        pltpu.make_async_copy(above, image.at[:, HZ + 1], sems.at[17]),
    ]
    for k in range(8):
        copies.append(
            pltpu.make_async_copy(planes[k], image.at[k, 1 : HZ + 1], sems.at[k])
        )
        copies.append(pltpu.make_async_copy(fields[k], field.at[k], sems.at[8 + k]))
    for copy in copies:
        copy.start()
    acc[...] = jnp.zeros_like(acc)
    for copy in copies:
        copy.wait()
    lane = lax.broadcasted_iota(jnp.int32, (CY, 128), 1)
    sub = lax.broadcasted_iota(jnp.int32, (CY, 128), 0)
    coarse_lane = lax.broadcasted_iota(jnp.int32, (VR, 128), 1)

    def neighbours(part):
        left0, left1, left2 = (pltpu.roll(p, 1, 1) for p in part)
        right0, right1, right2 = (pltpu.roll(p, 127, 1) for p in part)
        left2 = jnp.where(lane == 0, left0, jnp.where(lane == 64, pltpu.roll(part[1], 65, 1), left2))
        left0 = jnp.where(lane == 0, 0.0, left0)
        left1 = jnp.where(lane == 0, 0.0, left1)
        right0 = jnp.where(lane == 127, right2, right0)
        right1 = jnp.where(lane == 127, pltpu.roll(part[2], 63, 1), right1)
        right2 = jnp.where(lane % 64 == 63, 0.0, right2)
        return (left0, left1, left2), (right0, right1, right2)

    def interpolate(k, velocity):
        base = 2 * (me ^ k)
        slots = [(assign[base + j] // 2) ^ me for j in range(2)]
        stacked = [[], []]
        for c in range(3):
            parts = [field[slots[0], VR * c : VR * (c + 1)]]
            if c > 0:
                parts.append(field[slots[1], VR * (c + 2) : VR * (c + 3)])
            else:
                spread = [
                    pltpu.roll(
                        field[slots[1], VR * t : VR * (t + 1)].astype(F32), 32 * t + 32, 1
                    )
                    for t in range(3)
                ]
                third = jnp.where(
                    coarse_lane < 32, spread[0], jnp.where(coarse_lane < 64, spread[1], spread[2])
                )
                parts.append(third.astype(BF16))
            rough = jnp.dot(
                zy[...], jnp.concatenate(parts, axis=1), preferred_element_type=F32
            )
            high = rough.astype(BF16)
            low = (rough - high.astype(F32)).astype(BF16)
            for j in range(2):
                own = slice(128 * j, 128 * j + 128)
                stacked[j].append(jnp.concatenate([high[:, own], low[:, own]], axis=1))
        fine = [
            jnp.dot(jnp.concatenate(stacked[j], axis=0), table[...], preferred_element_type=F32)
            for j, table in enumerate((x0, x1))
        ]
        velocity[0] = fine[0][:, :128]
        velocity[1] = fine[1][:, :128]
        velocity[2] = fine[0][:, 128:] + fine[1][:, 128:]

    def apply(k, velocity):
        for z in range(HZ):
            before = image[k, z].astype(F32)
            centre = image[k, z + 1].astype(F32)
            after = image[k, z + 2].astype(F32)
            part = [centre[CY * b : CY * (b + 1)] for b in range(3)]
            halo = centre[3 * CY :]
            left, right = neighbours(part)
            warped = []
            for b in range(3):
                own = slice(CY * b, CY * (b + 1))
                up = jnp.where(sub == 0, halo[2 * b : 2 * b + 1], pltpu.roll(part[b], 1, 0))
                down = jnp.where(
                    sub == CY - 1, halo[2 * b + 1 : 2 * b + 2], pltpu.roll(part[b], CY - 1, 0)
                )

                def v(c):
                    start = HZ * CY * c + CY * z
                    return velocity[b, start : start + CY]

                push = v(0) * (right[b] - left[b]) + v(1) * (down - up)
                push += v(2) * (after[own] - before[own])
                warped.append(part[b] - 0.5 * push)
            rows = slice(CY * z, CY * (z + 1))
            acc[0, rows] += warped[0] + warped[1]
            acc[1, rows] += warped[2]

    interpolate(0, even)

    def turn(step, carry):
        interpolate(2 * step + 1, odd)
        apply(2 * step, even)
        interpolate(jnp.minimum(2 * step + 2, 7), even)
        apply(2 * step + 1, odd)
        return carry

    lax.fori_loop(0, 4, turn, 0)
    weight = SCALE / 16.0
    chunk[: HZ * CY] = pltpu.roll(acc[0] * weight, 64 * level, 1)
    wide = lax.broadcasted_iota(jnp.int32, (CY, 128), 1)

    def joined(z, other):
        one, two = (acc[1, pl.ds(pl.multiple_of(r * CY, 8), CY)] for r in (z, other))
        one = one + pltpu.roll(one, 64, 1)
        two = two + pltpu.roll(two, 64, 1)
        return jnp.where(wide < 64, one, two) * weight

    for z in range(HZ // 2):
        chunk[(HZ + z) * CY : (HZ + z + 1) * CY] = joined(z, z + HZ // 2)
    outer = (HZ - 2) * level
    rim = acc[0, pl.ds(pl.multiple_of(outer * CY, 8), 2 * CY)] * weight
    edge[: 2 * CY] = pltpu.roll(rim, 64 - 64 * level, 1)
    edge[2 * CY :] = joined(outer, outer + 1)


def warp(info, assign, planes, fields, below, above):
    tables = [
        jnp.asarray(t, BF16) for t in (zy_table(), x_table(192, 0), x_table(192, 1))
    ]
    vmem = pl.BlockSpec(memory_space=pltpu.VMEM)
    smem = pl.BlockSpec(memory_space=pltpu.SMEM)
    hbm = pl.BlockSpec(memory_space=pl.ANY)
    return pl.pallas_call(
        warp_kernel,
        grid=(),
        in_specs=[smem, smem, vmem, vmem, vmem] + [hbm] * 18,
        out_specs=[vmem] * 2,
        out_shape=[
            jax.ShapeDtypeStruct((HZ * CY * 3 // 2, 128), F32),
            jax.ShapeDtypeStruct((3 * CY, 128), F32),
        ],
        scratch_shapes=[
            pltpu.VMEM((8, HZ + 2, PROWS, 128), BF16),
            pltpu.VMEM((8, VROWS, 128), BF16),
            pltpu.VMEM((3, 3 * HZ * CY, 128), F32),
            pltpu.VMEM((3, 3 * HZ * CY, 128), F32),
            pltpu.VMEM((2, HZ * CY, 128), F32),
            pltpu.SemaphoreType.DMA((18,)),
        ],
        name="warp_sum",
    )(info, assign, *tables, *planes, *fields, below, above)


def relax_kernel(info, chunks, out, flat, pair, flat2, pair2, even, odd, ready, sems):
    level, me, zone = info[0], info[1], info[2]
    size = flat.shape[1] - 16
    for held in (flat, pair, flat2, pair2):
        held[:, :8] = jnp.zeros((held.shape[0], 8, 128), F32)
        held[:, size + 8 :] = jnp.zeros((held.shape[0], 8, 128), F32)
    for held in (flat, flat2):
        for z in (0, held.shape[0] - 1):
            held[z, 8 : 8 + size] = jnp.zeros((size, 128), F32)
    narrow = lax.broadcasted_iota(jnp.int32, (CY, 128), 1)
    tail = HZ * 3 // 2
    for peer in range(8):
        rows = slice(8 + CY * peer, 8 + CY * (peer + 1))

        def block(half, index):
            return chunks[peer ^ me, half ^ level, CY * index : CY * (index + 1)]

        for half in range(2):
            for z in range(HZ):
                flat[3 + 14 * half + z, rows] = block(half, z)
            for z in range(2):
                flat[1 + 28 * half + z, rows] = block(half, tail + z)
        packed = [HZ + z % (HZ // 2) for z in range(HZ)]
        sides = [z // (HZ // 2) for z in range(HZ)]
        lows = [(tail + 2, 0), (tail + 2, 1)] + list(zip(packed, sides))
        highs = list(zip(packed, sides)) + [(tail + 2, 0), (tail + 2, 1)]
        for index in range(14):
            low, high = block(0, lows[index][0]), block(1, highs[index][0])
            if lows[index][1] == 1:
                low = pltpu.roll(low, 64, 1)
            if highs[index][1] == 0:
                high = pltpu.roll(high, 64, 1)
            pair[1 + index, rows] = jnp.where(narrow < 64, low, high)

    def mirror(planes, both):
        body = slice(8, 8 + size)
        both[0, body] = pltpu.roll(both[14, body], 64, 1)
        both[15, body] = pltpu.roll(both[1, body], 64, 1)
        planes[16, body] = pltpu.roll(planes[14, body], 64, 1)
        planes[15, body] = pltpu.roll(planes[17, body], 64, 1)

    mirror(flat, pair)
    count = 2 * CY
    lane = lax.broadcasted_iota(jnp.int32, (count, 128), 1)

    def shift(planes, index, sums):
        for start in range(8, 8 + size, count):
            refs = [(planes[0], index), (planes[0], index + 16), (planes[1], index)]
            part = [held[z, start : start + count] for held, z in refs]
            left = [pltpu.roll(p, 1, 1) for p in part]
            right = [pltpu.roll(p, 127, 1) for p in part]
            left[2] = jnp.where(lane == 0, left[0], jnp.where(lane == 64, left[1], left[2]))
            left[0] = jnp.where(lane == 0, 0.0, left[0])
            left[1] = jnp.where(lane == 64, 0.0, left[1])
            right[0] = jnp.where(lane == 127, right[2], right[0])
            right[1] = jnp.where(lane == 63, right[2], right[1])
            right[2] = jnp.where(lane % 64 == 63, 0.0, right[2])
            for b in range(3):
                sums[b, start - 8 : start - 8 + count] = left[b] + right[b]

    def swept(planes, index, sums, start, scale):
        refs = [(planes[0], index), (planes[0], index + 16), (planes[1], index)]
        done = []
        for b, (held, z) in enumerate(refs):
            around = held[z - 1, start : start + count] + held[z + 1, start : start + count]
            around += held[z, start - 1 : start - 1 + count] + held[z, start + 1 : start + 1 + count]
            around += sums[b, start - 8 : start - 8 + count]
            value = around + (2.0 / 3.0) * held[z, start : start + count]
            done.append(value if scale is None else scale * value)
        return done

    def sweep(planes, store, scale, after):
        shift(planes, 1, even)

        def turn(step, carry):
            index = 2 * step + 1
            shift(planes, index + 1, odd)
            for start in range(8, 8 + size, count):
                store(index, start, swept(planes, index, even, start, scale))
            shift(planes, jnp.minimum(index + 2, 14), even)
            for start in range(8, 8 + size, count):
                store(index + 1, start, swept(planes, index + 1, odd, start, scale))
            after(index)
            after(index + 1)
            return carry

        lax.fori_loop(0, 7, turn, 0)

    def first(index, start, done):
        flat2[index, start : start + count] = done[0]
        flat2[index + 16, start : start + count] = done[1]
        pair2[index, start : start + count] = done[2]

    sweep((flat, pair), first, None, lambda index: None)
    whole = lax.broadcasted_iota(jnp.int32, (size, 128), 1)

    @pl.when(zone == 0)
    def _():
        flat2[2, 8 : 8 + size] = jnp.zeros((size, 128), F32)
        pair2[2, 8 : 8 + size] = jnp.where(whole < 64, 0.0, pair2[2, 8 : 8 + size])

    @pl.when(zone == 7)
    def _():
        flat2[29, 8 : 8 + size] = jnp.zeros((size, 128), F32)
        pair2[13, 8 : 8 + size] = jnp.where(whole < 64, pair2[13, 8 : 8 + size], 0.0)

    mirror(flat2, pair2)

    def emit(z):
        return pltpu.make_async_copy(ready.at[z + 2], out.at[z], sems.at[z])

    def second(index, start, done):
        rows = slice(start - 8, start - 8 + count)
        ready[index - 1, rows, :128] = done[0]
        ready[index - 1, rows, 128:] = done[2][:, :64]
        ready[index + 13, rows, :128] = pltpu.roll(done[1], 64, 1)
        ready[index + 13, rows, 128:] = pltpu.roll(done[2], 64, 1)[:, :64]

    def depart(index):
        @pl.when(index >= 3)
        def _():
            emit(index - 3).start()

        @pl.when(index <= 12)
        def _():
            emit(index + 11).start()

    sweep((flat2, pair2), second, 0.15 * 0.15 / SCALE, depart)

    def finish(z, carry):
        emit(z).wait()
        return carry

    lax.fori_loop(0, 24, finish, 0)


def relax(info, chunks):
    vmem = pl.BlockSpec(memory_space=pltpu.VMEM)
    return pl.pallas_call(
        relax_kernel,
        grid=(),
        in_specs=[pl.BlockSpec(memory_space=pltpu.SMEM), vmem],
        out_specs=pl.BlockSpec(memory_space=pl.ANY),
        out_shape=jax.ShapeDtypeStruct((24, 192, 192), F32),
        scratch_shapes=[
            pltpu.VMEM((32, 208, 128), F32),
            pltpu.VMEM((16, 208, 128), F32),
            pltpu.VMEM((32, 208, 128), F32),
            pltpu.VMEM((16, 208, 128), F32),
            pltpu.VMEM((3, 192, 128), F32),
            pltpu.VMEM((3, 192, 128), F32),
            pltpu.VMEM((28, 192, 192), F32),
            pltpu.SemaphoreType.DMA((24,)),
        ],
        name="relax",
    )(info, chunks)


def update(images, momenta, assign):
    level = lax.axis_index("level")
    me = lax.axis_index("subj")
    zone = lax.axis_index("gz")
    info = jnp.stack([level, me, zone]).astype(jnp.int32)
    zones = lax.axis_size("gz")
    outward = [(g, g + 1) for g in range(zones - 1)]
    outward += [(zones + g + 1, zones + g) for g in range(zones - 1)]
    nearest = ("level", "gz")
    cross = [(zones + g, g + 1) for g in range(zones - 1)]
    cross += [(g + 1, zones + g) for g in range(zones - 1)]
    climb = [(g, zones + g) for g in range(zones)]
    climb += [(zones + g, g + 1) for g in range(zones - 1)]
    part = (1, 3) + momenta.shape[2:]
    rim = lax.dynamic_slice(momenta, (0, 9 * (1 - level), 0, 0, 0), part)
    other = lax.dynamic_slice(momenta, (1, 9 * level, 0, 0, 0), part)
    rim = lax.ppermute(rim, nearest, outward)
    other = lax.ppermute(other, nearest, cross)

    def spread(parts):
        arrived = {0: parts[0]}
        for k in SPREAD:
            arrived[k] = lax.ppermute(parts[k], "subj", [(i, i ^ k) for i in range(8)])
        return [arrived[k] for k in range(8)]

    packed = pack_images(info, images)
    planes = spread(packed)
    blurred = blur(info, momenta, rim, other)
    fields = spread(blurred)
    low, high = edges(planes)
    below = lax.ppermute(high, nearest, climb)
    above = lax.ppermute(low, nearest, [(b, a) for a, b in climb])
    chunk, edge = warp(info, assign, planes, fields, below, above)
    edge = edge.astype(jnp.float16)
    chunk = chunk.astype(jnp.float16)
    inward = [(g + 1, g) for g in range(zones - 1)]
    inward += [(zones + g, zones + g + 1) for g in range(zones - 1)]
    swapped = lax.ppermute(chunk, "level", [(0, 1), (1, 0)])
    own_edge = lax.ppermute(edge, nearest, cross)
    far_edge = lax.ppermute(edge, nearest, inward)
    both = jnp.concatenate([chunk, own_edge, swapped, far_edge], axis=0)
    arrived = {0: both}
    for step in (1, 3, 2):
        perm = [(i, i ^ (2 * step)) for i in range(8)]
        arrived[step] = lax.ppermute(both, "subj", perm)
    gathered = []
    for step in range(4):
        part = arrived[step]
        gathered += [part, lax.ppermute(part, "subj", [(i, i ^ 1) for i in range(8)])]
    chunks = jnp.stack(gathered).astype(F32)
    return relax(info, chunks.reshape(8, 2, -1, 128))


def solution(mesh):
    return jax.shard_map(
        update,
        mesh=mesh,
        in_specs=(P("subj", "gz", None, None), P("subj", "gz", None, None, None), P()),
        out_specs=P("gz", None, None),
        check_vma=False,
    )
```

```python
import jax
import jax.numpy as jnp
import numpy as np
from jax import lax
from jax.experimental import pallas as pl
from jax.experimental.pallas import tpu as pltpu
from jax.sharding import PartitionSpec as P


F32 = jnp.float32
BF16 = jnp.bfloat16
HZ = 12
CY = 24
CZ = HZ // 2 + 2
CW = CY // 2 + 2
VR = CZ * CW
VROWS = 5 * VR
PROWS = 80
SPREAD = (2, 1, 3)
SCALE = 128.0


def lerp_table(fine):
    table = np.zeros((fine, fine // 2 + 2), np.float32)
    for row in range(fine):
        near = row // 2 + 1
        table[row, near] += 0.75
        table[row, near + 2 * (row % 2) - 1] += 0.25
    return table


def zy_table():
    return np.kron(lerp_table(HZ), lerp_table(CY))


def x_table(fine, slot):
    inner = lerp_table(fine)[:, 1:-1].T
    coarse = fine // 2
    table = np.zeros((256, 256), np.float32)
    for base in (0, 128):
        table[base : base + coarse, :128] = inner[:, :128]
        table[base : base + coarse, 128 + 64 * slot : 192 + 64 * slot] = inner[:, 128:]
    return table


def pack_plane(plane, put):
    count = plane.shape[1] // CY
    low = [plane[0][:, :128], plane[1][:, :128]]
    both = jnp.concatenate([plane[0][:, 128:], plane[1][:, 128:]], axis=1)
    parts = low + [both]
    row = lax.broadcasted_iota(jnp.int32, (8, 128), 0)
    for peer in range(count):
        start = CY * peer
        halo = jnp.zeros((8, 128), F32)
        for index, part in enumerate(parts):
            if peer > 0:
                halo = jnp.where(row == 2 * index, part[start - 1 : start], halo)
            if peer < count - 1:
                halo = jnp.where(row == 2 * index + 1, part[start + CY : start + CY + 1], halo)
        blocks = [part[start : start + CY] for part in parts] + [halo]
        put(peer, jnp.concatenate(blocks, axis=0))


GROUPS = ((0, 3), (3, 3), (6, 3), (9, 3))


def pack_kernel(info, images, *rest):
    outs = rest[:4]
    held, stage, sems, gone = rest[4:]
    level, me = info[0], info[1]
    loads = []
    for index, (first, count) in enumerate(GROUPS):
        rows = pl.ds(HZ * level + first, count)
        loads.append(
            pltpu.make_async_copy(
                images.at[:, rows], held.at[:, pl.ds(first, count)], sems.at[index]
            )
        )
    for copy in loads:
        copy.start()
    sent = []
    for index, (first, count) in enumerate(GROUPS):
        loads[index].wait()

        def step(z, carry):
            def put(peer, value):
                stage[peer, z] = value.astype(BF16)

            pack_plane(held[:, z].astype(F32), put)
            return carry

        lax.fori_loop(first, first + count, step, 0)
        for k in range(8):
            rows = pl.ds(first, count)
            copy = pltpu.make_async_copy(
                stage.at[me ^ k, rows], outs[k // 2].at[k % 2, rows], gone.at[8 * index + k]
            )
            copy.start()
            sent.append(copy)
    for copy in sent:
        copy.wait()


def pack_images(info, images):
    hbm = pl.BlockSpec(memory_space=pl.ANY)
    return pl.pallas_call(
        pack_kernel,
        grid=(),
        in_specs=[pl.BlockSpec(memory_space=pltpu.SMEM), hbm],
        out_specs=[hbm] * 4,
        out_shape=[jax.ShapeDtypeStruct((2, HZ, PROWS, 128), BF16)] * 4,
        scratch_shapes=[
            pltpu.VMEM((2, HZ, 192, 192), BF16),
            pltpu.VMEM((8, HZ, PROWS, 128), BF16),
            pltpu.SemaphoreType.DMA((len(GROUPS),)),
            pltpu.SemaphoreType.DMA((8 * len(GROUPS),)),
        ],
        name="pack_images",
    )(info, images)


def blur_kernel(info, momenta, halo, other, *rest):
    outs = rest[:4]
    held, stage, tall, wide, third, piece, sems, gone = rest[4:]
    level, me = info[0], info[1]
    half = info[2] * 2 + level
    own = pltpu.make_async_copy(
        momenta.at[:, pl.ds(3 * level, 9)], held.at[:, pl.ds(3 - 3 * level, 9)], sems.at[0]
    )
    sides = [
        pltpu.make_async_copy(rows.at[0], held.at[j, pl.ds(9 * level, 3)], sems.at[1 + j])
        for j, rows in enumerate((halo, other))
    ]
    for copy in [own] + sides:
        copy.start()
    for held_rows in (tall, wide):
        held_rows[:, :8] = jnp.zeros((CZ, 8, 128), F32)
        held_rows[:, 104:] = jnp.zeros((CZ, 8, 128), F32)
    for copy in [own] + sides:
        copy.wait()
    first = (half > 0).astype(F32)
    last = (half < 15).astype(F32)
    spare = jnp.zeros((96, 32), F32)
    plane_lane = lax.broadcasted_iota(jnp.int32, (96, 128), 1)
    for subject, component in ((1, 0), (0, 0), (0, 1), (0, 2), (1, 1), (1, 2)):

        def row(r, carry, subject=subject, component=component):
            def m(t):
                return held[subject, r + t, component]

            z = (m(0) + m(4)) * 0.0625 + (m(1) + m(3)) * 0.25 + m(2) * 0.375
            z = z * jnp.where(r == 0, first, jnp.where(r == CZ - 1, last, 1.0))
            z = jnp.concatenate([z, spare], axis=1)

            def lane(k):
                return pltpu.roll(z, k % 128, 1)

            x = (lane(2) + lane(-2)) * 0.0625 + (lane(1) + lane(-1)) * 0.25 + z * 0.375
            tall[r, 8:104] = x
            y = (tall[r, 6:102] + tall[r, 10:106]) * 0.0625
            y += (tall[r, 7:103] + tall[r, 9:105]) * 0.25
            y += x * 0.375
            if (subject, component) == (1, 0):
                third[r] = y
            elif subject == 0:
                extra = pltpu.roll(third[r], 96 - 32 * component, 1)
                wide[r, 8:104] = jnp.where(plane_lane < 96, y, extra)
            else:
                wide[r, 8:104] = y
            return carry

        lax.fori_loop(0, CZ, row, 0, unroll=2)
        if (subject, component) == (1, 0):
            continue
        block = 2 * subject + component
        for peer in range(8):
            start = 8 + (CY // 2) * peer - 1
            for r in range(CZ):
                piece[CW * r : CW * (r + 1)] = wide[r, start : start + CW]
            stage[peer, VR * block : VR * (block + 1)] = piece[...].astype(BF16)
    sent = [
        pltpu.make_async_copy(stage.at[me ^ k], outs[k // 2].at[k % 2], gone.at[k])
        for k in range(8)
    ]
    for copy in sent:
        copy.start()
    for copy in sent:
        copy.wait()


def blur(info, momenta, halo, other):
    rows = VROWS
    return pl.pallas_call(
        blur_kernel,
        grid=(),
        in_specs=[
            pl.BlockSpec(memory_space=pltpu.SMEM),
            pl.BlockSpec(memory_space=pl.ANY),
            pl.BlockSpec(memory_space=pl.ANY),
            pl.BlockSpec(memory_space=pl.ANY),
        ],
        out_specs=[pl.BlockSpec(memory_space=pl.ANY)] * 4,
        out_shape=[jax.ShapeDtypeStruct((2, rows, 128), BF16)] * 4,
        scratch_shapes=[
            pltpu.VMEM((2, 12, 3, 96, 96), F32),
            pltpu.VMEM((8, rows, 128), BF16),
            pltpu.VMEM((CZ, 112, 128), F32),
            pltpu.VMEM((CZ, 112, 128), F32),
            pltpu.VMEM((CZ, 96, 128), F32),
            pltpu.VMEM((VR, 128), F32),
            pltpu.SemaphoreType.DMA((3,)),
            pltpu.SemaphoreType.DMA((8,)),
        ],
        name="blur_momenta",
    )(info, momenta, halo, other)


def edge_kernel(*refs):
    planes, below, above = refs[:8], refs[8], refs[9]
    low, high, sems, gone = refs[10:]
    copies = []
    for k, plane in enumerate(planes):
        copies.append(pltpu.make_async_copy(plane.at[k % 2, 0], low.at[k], sems.at[k]))
        copies.append(pltpu.make_async_copy(plane.at[k % 2, HZ - 1], high.at[k], sems.at[8 + k]))
    for copy in copies:
        copy.start()
    for copy in copies:
        copy.wait()
    leaving = [
        pltpu.make_async_copy(low, below, gone.at[0]),
        pltpu.make_async_copy(high, above, gone.at[1]),
    ]
    for copy in leaving:
        copy.start()
    for copy in leaving:
        copy.wait()


def edges(planes):
    hbm = pl.BlockSpec(memory_space=pl.ANY)
    shape = (8, PROWS, 128)
    return pl.pallas_call(
        edge_kernel,
        grid=(),
        in_specs=[hbm] * 8,
        out_specs=[hbm] * 2,
        out_shape=[jax.ShapeDtypeStruct(shape, BF16)] * 2,
        scratch_shapes=[
            pltpu.VMEM(shape, BF16),
            pltpu.VMEM(shape, BF16),
            pltpu.SemaphoreType.DMA((16,)),
            pltpu.SemaphoreType.DMA((2,)),
        ],
        name="cut_edges",
    )(*planes)


def warp_kernel(info, assign, zy, x0, x1, *rest):
    planes, fields, below, above = rest[:8], rest[8:16], rest[16], rest[17]
    chunk, edge = rest[18:20]
    image, field, even, odd, acc, sems = rest[20:]
    level, me = info[0], info[1]
    copies = [
        pltpu.make_async_copy(below, image.at[:, 0], sems.at[16]),
        pltpu.make_async_copy(above, image.at[:, HZ + 1], sems.at[17]),
    ]
    for k in range(8):
        copies.append(
            pltpu.make_async_copy(planes[k].at[k % 2], image.at[k, 1 : HZ + 1], sems.at[k])
        )
        copies.append(pltpu.make_async_copy(fields[k].at[k % 2], field.at[k], sems.at[8 + k]))
    for copy in copies:
        copy.start()
    acc[...] = jnp.zeros_like(acc)
    for copy in copies:
        copy.wait()
    lane = lax.broadcasted_iota(jnp.int32, (CY, 128), 1)
    sub = lax.broadcasted_iota(jnp.int32, (CY, 128), 0)
    coarse_lane = lax.broadcasted_iota(jnp.int32, (VR, 128), 1)

    def neighbours(part):
        left0, left1, left2 = (pltpu.roll(p, 1, 1) for p in part)
        right0, right1, right2 = (pltpu.roll(p, 127, 1) for p in part)
        left2 = jnp.where(lane == 0, left0, jnp.where(lane == 64, pltpu.roll(part[1], 65, 1), left2))
        left0 = jnp.where(lane == 0, 0.0, left0)
        left1 = jnp.where(lane == 0, 0.0, left1)
        right0 = jnp.where(lane == 127, right2, right0)
        right1 = jnp.where(lane == 127, pltpu.roll(part[2], 63, 1), right1)
        right2 = jnp.where(lane % 64 == 63, 0.0, right2)
        return (left0, left1, left2), (right0, right1, right2)

    def interpolate(k, velocity):
        base = 2 * (me ^ k)
        slots = [(assign[base + j] // 2) ^ me for j in range(2)]
        stacked = [[], []]
        for c in range(3):
            parts = [field[slots[0], VR * c : VR * (c + 1)]]
            if c > 0:
                parts.append(field[slots[1], VR * (c + 2) : VR * (c + 3)])
            else:
                spread = [
                    pltpu.roll(
                        field[slots[1], VR * t : VR * (t + 1)].astype(F32), 32 * t + 32, 1
                    )
                    for t in range(3)
                ]
                third = jnp.where(
                    coarse_lane < 32, spread[0], jnp.where(coarse_lane < 64, spread[1], spread[2])
                )
                parts.append(third.astype(BF16))
            rough = jnp.dot(
                zy[...], jnp.concatenate(parts, axis=1), preferred_element_type=F32
            )
            high = rough.astype(BF16)
            low = (rough - high.astype(F32)).astype(BF16)
            for j in range(2):
                own = slice(128 * j, 128 * j + 128)
                stacked[j].append(jnp.concatenate([high[:, own], low[:, own]], axis=1))
        fine = [
            jnp.dot(jnp.concatenate(stacked[j], axis=0), table[...], preferred_element_type=F32)
            for j, table in enumerate((x0, x1))
        ]
        velocity[0] = fine[0][:, :128]
        velocity[1] = fine[1][:, :128]
        velocity[2] = fine[0][:, 128:] + fine[1][:, 128:]

    def apply(k, velocity):
        for z in range(HZ):
            before = image[k, z].astype(F32)
            centre = image[k, z + 1].astype(F32)
            after = image[k, z + 2].astype(F32)
            part = [centre[CY * b : CY * (b + 1)] for b in range(3)]
            halo = centre[3 * CY :]
            left, right = neighbours(part)
            warped = []
            for b in range(3):
                own = slice(CY * b, CY * (b + 1))
                up = jnp.where(sub == 0, halo[2 * b : 2 * b + 1], pltpu.roll(part[b], 1, 0))
                down = jnp.where(
                    sub == CY - 1, halo[2 * b + 1 : 2 * b + 2], pltpu.roll(part[b], CY - 1, 0)
                )

                def v(c):
                    start = HZ * CY * c + CY * z
                    return velocity[b, start : start + CY]

                push = v(0) * (right[b] - left[b]) + v(1) * (down - up)
                push += v(2) * (after[own] - before[own])
                warped.append(part[b] - 0.5 * push)
            rows = slice(CY * z, CY * (z + 1))
            acc[0, rows] += warped[0] + warped[1]
            acc[1, rows] += warped[2]

    interpolate(0, even)

    def turn(step, carry):
        interpolate(2 * step + 1, odd)
        apply(2 * step, even)
        interpolate(jnp.minimum(2 * step + 2, 7), even)
        apply(2 * step + 1, odd)
        return carry

    lax.fori_loop(0, 4, turn, 0)
    weight = SCALE / 16.0
    chunk[: HZ * CY] = pltpu.roll(acc[0] * weight, 64 * level, 1)
    wide = lax.broadcasted_iota(jnp.int32, (CY, 128), 1)

    def joined(z, other):
        one, two = (acc[1, pl.ds(pl.multiple_of(r * CY, 8), CY)] for r in (z, other))
        one = one + pltpu.roll(one, 64, 1)
        two = two + pltpu.roll(two, 64, 1)
        return jnp.where(wide < 64, one, two) * weight

    for z in range(HZ // 2):
        chunk[(HZ + z) * CY : (HZ + z + 1) * CY] = joined(z, z + HZ // 2)
    outer = (HZ - 2) * level
    rim = acc[0, pl.ds(pl.multiple_of(outer * CY, 8), 2 * CY)] * weight
    edge[: 2 * CY] = pltpu.roll(rim, 64 - 64 * level, 1)
    edge[2 * CY :] = joined(outer, outer + 1)


def warp(info, assign, planes, fields, below, above):
    tables = [
        jnp.asarray(t, BF16) for t in (zy_table(), x_table(192, 0), x_table(192, 1))
    ]
    vmem = pl.BlockSpec(memory_space=pltpu.VMEM)
    smem = pl.BlockSpec(memory_space=pltpu.SMEM)
    hbm = pl.BlockSpec(memory_space=pl.ANY)
    return pl.pallas_call(
        warp_kernel,
        grid=(),
        in_specs=[smem, smem, vmem, vmem, vmem] + [hbm] * 18,
        out_specs=[vmem] * 2,
        out_shape=[
            jax.ShapeDtypeStruct((HZ * CY * 3 // 2, 128), F32),
            jax.ShapeDtypeStruct((3 * CY, 128), F32),
        ],
        scratch_shapes=[
            pltpu.VMEM((8, HZ + 2, PROWS, 128), BF16),
            pltpu.VMEM((8, VROWS, 128), BF16),
            pltpu.VMEM((3, 3 * HZ * CY, 128), F32),
            pltpu.VMEM((3, 3 * HZ * CY, 128), F32),
            pltpu.VMEM((2, HZ * CY, 128), F32),
            pltpu.SemaphoreType.DMA((18,)),
        ],
        name="warp_sum",
    )(info, assign, *tables, *planes, *fields, below, above)


def relax_kernel(info, chunks, out, flat, pair, flat2, pair2, even, odd, ready, sems):
    level, me, zone = info[0], info[1], info[2]
    size = flat.shape[1] - 16
    for held in (flat, pair, flat2, pair2):
        held[:, :8] = jnp.zeros((held.shape[0], 8, 128), F32)
        held[:, size + 8 :] = jnp.zeros((held.shape[0], 8, 128), F32)
    for held in (flat, flat2):
        for z in (0, held.shape[0] - 1):
            held[z, 8 : 8 + size] = jnp.zeros((size, 128), F32)
    narrow = lax.broadcasted_iota(jnp.int32, (CY, 128), 1)
    tail = HZ * 3 // 2
    for peer in range(8):
        rows = slice(8 + CY * peer, 8 + CY * (peer + 1))

        def block(half, index):
            return chunks[half ^ level, peer ^ me, CY * index : CY * (index + 1)]

        for half in range(2):
            for z in range(HZ):
                flat[3 + 14 * half + z, rows] = block(half, z)
            for z in range(2):
                flat[1 + 28 * half + z, rows] = block(half, tail + z)
        packed = [HZ + z % (HZ // 2) for z in range(HZ)]
        sides = [z // (HZ // 2) for z in range(HZ)]
        lows = [(tail + 2, 0), (tail + 2, 1)] + list(zip(packed, sides))
        highs = list(zip(packed, sides)) + [(tail + 2, 0), (tail + 2, 1)]
        for index in range(14):
            low, high = block(0, lows[index][0]), block(1, highs[index][0])
            if lows[index][1] == 1:
                low = pltpu.roll(low, 64, 1)
            if highs[index][1] == 0:
                high = pltpu.roll(high, 64, 1)
            pair[1 + index, rows] = jnp.where(narrow < 64, low, high)

    def mirror(planes, both):
        body = slice(8, 8 + size)
        both[0, body] = pltpu.roll(both[14, body], 64, 1)
        both[15, body] = pltpu.roll(both[1, body], 64, 1)
        planes[16, body] = pltpu.roll(planes[14, body], 64, 1)
        planes[15, body] = pltpu.roll(planes[17, body], 64, 1)

    mirror(flat, pair)
    count = 2 * CY
    lane = lax.broadcasted_iota(jnp.int32, (count, 128), 1)

    def shift(planes, index, sums):
        for start in range(8, 8 + size, count):
            refs = [(planes[0], index), (planes[0], index + 16), (planes[1], index)]
            part = [held[z, start : start + count] for held, z in refs]
            left = [pltpu.roll(p, 1, 1) for p in part]
            right = [pltpu.roll(p, 127, 1) for p in part]
            left[2] = jnp.where(lane == 0, left[0], jnp.where(lane == 64, left[1], left[2]))
            left[0] = jnp.where(lane == 0, 0.0, left[0])
            left[1] = jnp.where(lane == 64, 0.0, left[1])
            right[0] = jnp.where(lane == 127, right[2], right[0])
            right[1] = jnp.where(lane == 63, right[2], right[1])
            right[2] = jnp.where(lane % 64 == 63, 0.0, right[2])
            for b in range(3):
                sums[b, start - 8 : start - 8 + count] = left[b] + right[b]

    def swept(planes, index, sums, start, scale):
        refs = [(planes[0], index), (planes[0], index + 16), (planes[1], index)]
        done = []
        for b, (held, z) in enumerate(refs):
            around = held[z - 1, start : start + count] + held[z + 1, start : start + count]
            around += held[z, start - 1 : start - 1 + count] + held[z, start + 1 : start + 1 + count]
            around += sums[b, start - 8 : start - 8 + count]
            value = around + (2.0 / 3.0) * held[z, start : start + count]
            done.append(value if scale is None else scale * value)
        return done

    def sweep(planes, store, scale, after):
        shift(planes, 1, even)

        def turn(step, carry):
            index = 2 * step + 1
            shift(planes, index + 1, odd)
            for start in range(8, 8 + size, count):
                store(index, start, swept(planes, index, even, start, scale))
            shift(planes, jnp.minimum(index + 2, 14), even)
            for start in range(8, 8 + size, count):
                store(index + 1, start, swept(planes, index + 1, odd, start, scale))
            after(index)
            after(index + 1)
            return carry

        lax.fori_loop(0, 7, turn, 0)

    def first(index, start, done):
        flat2[index, start : start + count] = done[0]
        flat2[index + 16, start : start + count] = done[1]
        pair2[index, start : start + count] = done[2]

    sweep((flat, pair), first, None, lambda index: None)
    whole = lax.broadcasted_iota(jnp.int32, (size, 128), 1)

    @pl.when(zone == 0)
    def _():
        flat2[2, 8 : 8 + size] = jnp.zeros((size, 128), F32)
        pair2[2, 8 : 8 + size] = jnp.where(whole < 64, 0.0, pair2[2, 8 : 8 + size])

    @pl.when(zone == 7)
    def _():
        flat2[29, 8 : 8 + size] = jnp.zeros((size, 128), F32)
        pair2[13, 8 : 8 + size] = jnp.where(whole < 64, pair2[13, 8 : 8 + size], 0.0)

    mirror(flat2, pair2)

    def emit(z):
        return pltpu.make_async_copy(ready.at[z + 2], out.at[z], sems.at[z])

    def second(index, start, done):
        rows = slice(start - 8, start - 8 + count)
        ready[index - 1, rows, :128] = done[0]
        ready[index - 1, rows, 128:] = done[2][:, :64]
        ready[index + 13, rows, :128] = pltpu.roll(done[1], 64, 1)
        ready[index + 13, rows, 128:] = pltpu.roll(done[2], 64, 1)[:, :64]

    def depart(index):
        @pl.when(index >= 3)
        def _():
            emit(index - 3).start()

        @pl.when(index <= 12)
        def _():
            emit(index + 11).start()

    sweep((flat2, pair2), second, 0.15 * 0.15 / SCALE, depart)

    def finish(z, carry):
        emit(z).wait()
        return carry

    lax.fori_loop(0, 24, finish, 0)


def relax(info, chunks):
    vmem = pl.BlockSpec(memory_space=pltpu.VMEM)
    return pl.pallas_call(
        relax_kernel,
        grid=(),
        in_specs=[pl.BlockSpec(memory_space=pltpu.SMEM), vmem],
        out_specs=pl.BlockSpec(memory_space=pl.ANY),
        out_shape=jax.ShapeDtypeStruct((24, 192, 192), F32),
        scratch_shapes=[
            pltpu.VMEM((32, 208, 128), F32),
            pltpu.VMEM((16, 208, 128), F32),
            pltpu.VMEM((32, 208, 128), F32),
            pltpu.VMEM((16, 208, 128), F32),
            pltpu.VMEM((3, 192, 128), F32),
            pltpu.VMEM((3, 192, 128), F32),
            pltpu.VMEM((28, 192, 192), F32),
            pltpu.SemaphoreType.DMA((24,)),
        ],
        name="relax",
    )(info, chunks)


def update(images, momenta, assign):
    level = lax.axis_index("level")
    me = lax.axis_index("subj")
    zone = lax.axis_index("gz")
    info = jnp.stack([level, me, zone]).astype(jnp.int32)
    zones = lax.axis_size("gz")
    outward = [(g, g + 1) for g in range(zones - 1)]
    outward += [(zones + g + 1, zones + g) for g in range(zones - 1)]
    nearest = ("level", "gz")
    cross = [(zones + g, g + 1) for g in range(zones - 1)]
    cross += [(g + 1, zones + g) for g in range(zones - 1)]
    climb = [(g, zones + g) for g in range(zones)]
    climb += [(zones + g, g + 1) for g in range(zones - 1)]
    part = (1, 3) + momenta.shape[2:]
    rim = lax.dynamic_slice(momenta, (0, 9 * (1 - level), 0, 0, 0), part)
    other = lax.dynamic_slice(momenta, (1, 9 * level, 0, 0, 0), part)
    rim = lax.ppermute(rim, nearest, outward)
    other = lax.ppermute(other, nearest, cross)

    def spread(parts):
        arrived = {0: parts[0]}
        for step in SPREAD:
            perm = [(i, i ^ (2 * step)) for i in range(8)]
            arrived[step] = lax.ppermute(parts[step], "subj", perm)
        result = []
        for step in range(4):
            other = lax.ppermute(arrived[step], "subj", [(i, i ^ 1) for i in range(8)])
            result += [arrived[step], other]
        return result

    packed = pack_images(info, images)
    planes = spread(packed)
    blurred = blur(info, momenta, rim, other)
    fields = spread(blurred)
    low, high = edges(planes)
    below = lax.ppermute(high, nearest, climb)
    above = lax.ppermute(low, nearest, [(b, a) for a, b in climb])
    chunk, edge = warp(info, assign, planes, fields, below, above)
    edge = lax.ppermute(edge.astype(jnp.float16), nearest, cross)
    chunk = jnp.concatenate([chunk.astype(jnp.float16), edge], axis=0)
    gathered = []
    for far in range(2):
        for step in range(4):
            part = chunk
            if far or step:
                perm = [
                    (8 * a + i, 8 * (a ^ far) + (i ^ (2 * step))) for a in range(2) for i in range(8)
                ]
                part = lax.ppermute(chunk, ("level", "subj"), perm)
            gathered += [part, lax.ppermute(part, "subj", [(i, i ^ 1) for i in range(8)])]
    chunks = jnp.stack(gathered).astype(F32)
    return relax(info, chunks.reshape(2, 8, -1, 128))


def solution(mesh):
    return jax.shard_map(
        update,
        mesh=mesh,
        in_specs=(P("subj", "gz", None, None), P("subj", "gz", None, None, None), P()),
        out_specs=P("gz", None, None),
        check_vma=False,
    )
```

```python
import jax
import jax.numpy as jnp
import numpy as np
from jax import lax
from jax.experimental import pallas as pl
from jax.experimental.pallas import tpu as pltpu
from jax.sharding import PartitionSpec as P


F32 = jnp.float32
BF16 = jnp.bfloat16
HZ = 12
CY = 24
CZ = HZ // 2 + 2
CW = CY // 2 + 2
VR = CZ * CW
VROWS = 5 * VR
PROWS = 80
SPREAD = (1, 3, 7, 5, 2, 6, 4)
SCALE = 128.0


def lerp_table(fine):
    table = np.zeros((fine, fine // 2 + 2), np.float32)
    for row in range(fine):
        near = row // 2 + 1
        table[row, near] += 0.75
        table[row, near + 2 * (row % 2) - 1] += 0.25
    return table


def zy_table():
    return np.kron(lerp_table(HZ), lerp_table(CY))


def x_table(fine, slot):
    inner = lerp_table(fine)[:, 1:-1].T
    coarse = fine // 2
    table = np.zeros((256, 256), np.float32)
    for base in (0, 128):
        table[base : base + coarse, :128] = inner[:, :128]
        table[base : base + coarse, 128 + 64 * slot : 192 + 64 * slot] = inner[:, 128:]
    return table


def pack_plane(plane, put):
    count = plane.shape[1] // CY
    low = [plane[0][:, :128], plane[1][:, :128]]
    both = jnp.concatenate([plane[0][:, 128:], plane[1][:, 128:]], axis=1)
    parts = low + [both]
    row = lax.broadcasted_iota(jnp.int32, (8, 128), 0)
    for peer in range(count):
        start = CY * peer
        halo = jnp.zeros((8, 128), F32)
        for index, part in enumerate(parts):
            if peer > 0:
                halo = jnp.where(row == 2 * index, part[start - 1 : start], halo)
            if peer < count - 1:
                halo = jnp.where(row == 2 * index + 1, part[start + CY : start + CY + 1], halo)
        blocks = [part[start : start + CY] for part in parts] + [halo]
        put(peer, jnp.concatenate(blocks, axis=0))


GROUPS = ((0, 3), (3, 3), (6, 3), (9, 3))


def pack_kernel(info, images, *rest):
    outs = rest[:8]
    held, stage, sems, gone = rest[8:]
    level, me = info[0], info[1]
    loads = []
    for index, (first, count) in enumerate(GROUPS):
        rows = pl.ds(HZ * level + first, count)
        loads.append(
            pltpu.make_async_copy(
                images.at[:, rows], held.at[:, pl.ds(first, count)], sems.at[index]
            )
        )
    for copy in loads:
        copy.start()
    sent = []
    for index, (first, count) in enumerate(GROUPS):
        loads[index].wait()

        def step(z, carry):
            def put(peer, value):
                stage[peer, z] = value.astype(BF16)

            pack_plane(held[:, z].astype(F32), put)
            return carry

        lax.fori_loop(first, first + count, step, 0)
        for k, out in enumerate(outs):
            rows = pl.ds(first, count)
            copy = pltpu.make_async_copy(
                stage.at[me ^ k, rows], out.at[rows], gone.at[8 * index + k]
            )
            copy.start()
            sent.append(copy)
    for copy in sent:
        copy.wait()


def pack_images(info, images):
    hbm = pl.BlockSpec(memory_space=pl.ANY)
    return pl.pallas_call(
        pack_kernel,
        grid=(),
        in_specs=[pl.BlockSpec(memory_space=pltpu.SMEM), hbm],
        out_specs=[hbm] * 8,
        out_shape=[jax.ShapeDtypeStruct((HZ, PROWS, 128), BF16)] * 8,
        scratch_shapes=[
            pltpu.VMEM((2, HZ, 192, 192), BF16),
            pltpu.VMEM((8, HZ, PROWS, 128), BF16),
            pltpu.SemaphoreType.DMA((len(GROUPS),)),
            pltpu.SemaphoreType.DMA((8 * len(GROUPS),)),
        ],
        name="pack_images",
    )(info, images)


def blur_kernel(info, momenta, halo, *rest):
    outs = rest[:8]
    held, stage, tall, wide, third, piece, sems, gone = rest[8:]
    level, me = info[0], info[1]
    half = info[2] * 2 + level
    own = pltpu.make_async_copy(
        momenta.at[:, pl.ds(3 * level, 9)], held.at[:, pl.ds(3 - 3 * level, 9)], sems.at[0]
    )
    side = pltpu.make_async_copy(halo, held.at[:, pl.ds(9 * level, 3)], sems.at[1])
    own.start()
    side.start()
    for held_rows in (tall, wide):
        held_rows[:, :8] = jnp.zeros((CZ, 8, 128), F32)
        held_rows[:, 104:] = jnp.zeros((CZ, 8, 128), F32)
    own.wait()
    side.wait()
    first = (half > 0).astype(F32)
    last = (half < 15).astype(F32)
    spare = jnp.zeros((96, 32), F32)
    plane_lane = lax.broadcasted_iota(jnp.int32, (96, 128), 1)
    for subject, component in ((1, 0), (0, 0), (0, 1), (0, 2), (1, 1), (1, 2)):

        def row(r, carry, subject=subject, component=component):
            def m(t):
                return held[subject, r + t, component]

            z = (m(0) + m(4)) * 0.0625 + (m(1) + m(3)) * 0.25 + m(2) * 0.375
            z = z * jnp.where(r == 0, first, jnp.where(r == CZ - 1, last, 1.0))
            z = jnp.concatenate([z, spare], axis=1)

            def lane(k):
                return pltpu.roll(z, k % 128, 1)

            x = (lane(2) + lane(-2)) * 0.0625 + (lane(1) + lane(-1)) * 0.25 + z * 0.375
            tall[r, 8:104] = x
            y = (tall[r, 6:102] + tall[r, 10:106]) * 0.0625
            y += (tall[r, 7:103] + tall[r, 9:105]) * 0.25
            y += x * 0.375
            if (subject, component) == (1, 0):
                third[r] = y
            elif subject == 0:
                extra = pltpu.roll(third[r], 96 - 32 * component, 1)
                wide[r, 8:104] = jnp.where(plane_lane < 96, y, extra)
            else:
                wide[r, 8:104] = y
            return carry

        lax.fori_loop(0, CZ, row, 0, unroll=2)
        if (subject, component) == (1, 0):
            continue
        block = 2 * subject + component
        for peer in range(8):
            start = 8 + (CY // 2) * peer - 1
            for r in range(CZ):
                piece[CW * r : CW * (r + 1)] = wide[r, start : start + CW]
            stage[peer, VR * block : VR * (block + 1)] = piece[...].astype(BF16)
    sent = [
        pltpu.make_async_copy(stage.at[me ^ k], out, gone.at[k]) for k, out in enumerate(outs)
    ]
    for copy in sent:
        copy.start()
    for copy in sent:
        copy.wait()


def blur(info, momenta, halo):
    rows = VROWS
    return pl.pallas_call(
        blur_kernel,
        grid=(),
        in_specs=[
            pl.BlockSpec(memory_space=pltpu.SMEM),
            pl.BlockSpec(memory_space=pl.ANY),
            pl.BlockSpec(memory_space=pl.ANY),
        ],
        out_specs=[pl.BlockSpec(memory_space=pl.ANY)] * 8,
        out_shape=[jax.ShapeDtypeStruct((rows, 128), BF16)] * 8,
        scratch_shapes=[
            pltpu.VMEM((2, 12, 3, 96, 96), F32),
            pltpu.VMEM((8, rows, 128), BF16),
            pltpu.VMEM((CZ, 112, 128), F32),
            pltpu.VMEM((CZ, 112, 128), F32),
            pltpu.VMEM((CZ, 96, 128), F32),
            pltpu.VMEM((VR, 128), F32),
            pltpu.SemaphoreType.DMA((2,)),
            pltpu.SemaphoreType.DMA((8,)),
        ],
        name="blur_momenta",
    )(info, momenta, halo)


def edge_kernel(*refs):
    planes, below, above = refs[:8], refs[8], refs[9]
    low, high, sems, gone = refs[10:]
    copies = []
    for k, plane in enumerate(planes):
        copies.append(pltpu.make_async_copy(plane.at[0], low.at[k], sems.at[k]))
        copies.append(pltpu.make_async_copy(plane.at[HZ - 1], high.at[k], sems.at[8 + k]))
    for copy in copies:
        copy.start()
    for copy in copies:
        copy.wait()
    leaving = [
        pltpu.make_async_copy(low, below, gone.at[0]),
        pltpu.make_async_copy(high, above, gone.at[1]),
    ]
    for copy in leaving:
        copy.start()
    for copy in leaving:
        copy.wait()


def edges(planes):
    hbm = pl.BlockSpec(memory_space=pl.ANY)
    shape = (8, PROWS, 128)
    return pl.pallas_call(
        edge_kernel,
        grid=(),
        in_specs=[hbm] * 8,
        out_specs=[hbm] * 2,
        out_shape=[jax.ShapeDtypeStruct(shape, BF16)] * 2,
        scratch_shapes=[
            pltpu.VMEM(shape, BF16),
            pltpu.VMEM(shape, BF16),
            pltpu.SemaphoreType.DMA((16,)),
            pltpu.SemaphoreType.DMA((2,)),
        ],
        name="cut_edges",
    )(*planes)


def warp_kernel(info, assign, zy, x0, x1, *rest):
    planes, fields, below, above = rest[:8], rest[8:16], rest[16], rest[17]
    chunk, edge = rest[18:20]
    image, field, even, odd, acc, sems = rest[20:]
    level, me = info[0], info[1]
    copies = [
        pltpu.make_async_copy(below, image.at[:, 0], sems.at[16]),
        pltpu.make_async_copy(above, image.at[:, HZ + 1], sems.at[17]),
    ]
    for k in range(8):
        copies.append(
            pltpu.make_async_copy(planes[k], image.at[k, 1 : HZ + 1], sems.at[k])
        )
    first = [pltpu.make_async_copy(fields[k], field.at[k], sems.at[8 + k]) for k in range(8)]
    for copy in first + copies:
        copy.start()
    acc[...] = jnp.zeros_like(acc)
    for copy in first:
        copy.wait()
    lane = lax.broadcasted_iota(jnp.int32, (CY, 128), 1)
    sub = lax.broadcasted_iota(jnp.int32, (CY, 128), 0)
    coarse_lane = lax.broadcasted_iota(jnp.int32, (VR, 128), 1)

    def neighbours(part):
        left0, left1, left2 = (pltpu.roll(p, 1, 1) for p in part)
        right0, right1, right2 = (pltpu.roll(p, 127, 1) for p in part)
        left2 = jnp.where(lane == 0, left0, jnp.where(lane == 64, pltpu.roll(part[1], 65, 1), left2))
        left0 = jnp.where(lane == 0, 0.0, left0)
        left1 = jnp.where(lane == 0, 0.0, left1)
        right0 = jnp.where(lane == 127, right2, right0)
        right1 = jnp.where(lane == 127, pltpu.roll(part[2], 63, 1), right1)
        right2 = jnp.where(lane % 64 == 63, 0.0, right2)
        return (left0, left1, left2), (right0, right1, right2)

    def interpolate(k, velocity):
        base = 2 * (me ^ k)
        slots = [(assign[base + j] // 2) ^ me for j in range(2)]
        stacked = [[], []]
        for c in range(3):
            parts = [field[slots[0], VR * c : VR * (c + 1)]]
            if c > 0:
                parts.append(field[slots[1], VR * (c + 2) : VR * (c + 3)])
            else:
                spread = [
                    pltpu.roll(
                        field[slots[1], VR * t : VR * (t + 1)].astype(F32), 32 * t + 32, 1
                    )
                    for t in range(3)
                ]
                third = jnp.where(
                    coarse_lane < 32, spread[0], jnp.where(coarse_lane < 64, spread[1], spread[2])
                )
                parts.append(third.astype(BF16))
            rough = jnp.dot(
                zy[...], jnp.concatenate(parts, axis=1), preferred_element_type=F32
            )
            high = rough.astype(BF16)
            low = (rough - high.astype(F32)).astype(BF16)
            for j in range(2):
                own = slice(128 * j, 128 * j + 128)
                stacked[j].append(jnp.concatenate([high[:, own], low[:, own]], axis=1))
        fine = [
            jnp.dot(jnp.concatenate(stacked[j], axis=0), table[...], preferred_element_type=F32)
            for j, table in enumerate((x0, x1))
        ]
        velocity[0] = fine[0][:, :128]
        velocity[1] = fine[1][:, :128]
        velocity[2] = fine[0][:, 128:] + fine[1][:, 128:]

    def apply(k, velocity):
        for z in range(HZ):
            before = image[k, z].astype(F32)
            centre = image[k, z + 1].astype(F32)
            after = image[k, z + 2].astype(F32)
            part = [centre[CY * b : CY * (b + 1)] for b in range(3)]
            halo = centre[3 * CY :]
            left, right = neighbours(part)
            warped = []
            for b in range(3):
                own = slice(CY * b, CY * (b + 1))
                up = jnp.where(sub == 0, halo[2 * b : 2 * b + 1], pltpu.roll(part[b], 1, 0))
                down = jnp.where(
                    sub == CY - 1, halo[2 * b + 1 : 2 * b + 2], pltpu.roll(part[b], CY - 1, 0)
                )

                def v(c):
                    start = HZ * CY * c + CY * z
                    return velocity[b, start : start + CY]

                push = v(0) * (right[b] - left[b]) + v(1) * (down - up)
                push += v(2) * (after[own] - before[own])
                warped.append(part[b] - 0.5 * push)
            rows = slice(CY * z, CY * (z + 1))
            acc[0, rows] += warped[0] + warped[1]
            acc[1, rows] += warped[2]

    interpolate(0, even)
    for copy in copies:
        copy.wait()

    def turn(step, carry):
        interpolate(2 * step + 1, odd)
        apply(2 * step, even)
        interpolate(jnp.minimum(2 * step + 2, 7), even)
        apply(2 * step + 1, odd)
        return carry

    lax.fori_loop(0, 4, turn, 0)
    weight = SCALE / 16.0
    chunk[: HZ * CY] = pltpu.roll(acc[0] * weight, 64 * level, 1)
    wide = lax.broadcasted_iota(jnp.int32, (CY, 128), 1)

    def joined(z, other):
        one, two = (acc[1, pl.ds(pl.multiple_of(r * CY, 8), CY)] for r in (z, other))
        one = one + pltpu.roll(one, 64, 1)
        two = two + pltpu.roll(two, 64, 1)
        return jnp.where(wide < 64, one, two) * weight

    for z in range(HZ // 2):
        chunk[(HZ + z) * CY : (HZ + z + 1) * CY] = joined(z, z + HZ // 2)
    outer = (HZ - 2) * level
    rim = acc[0, pl.ds(pl.multiple_of(outer * CY, 8), 2 * CY)] * weight
    edge[: 2 * CY] = pltpu.roll(rim, 64 - 64 * level, 1)
    edge[2 * CY :] = joined(outer, outer + 1)


def warp(info, assign, planes, fields, below, above):
    tables = [
        jnp.asarray(t, BF16) for t in (zy_table(), x_table(192, 0), x_table(192, 1))
    ]
    vmem = pl.BlockSpec(memory_space=pltpu.VMEM)
    smem = pl.BlockSpec(memory_space=pltpu.SMEM)
    hbm = pl.BlockSpec(memory_space=pl.ANY)
    return pl.pallas_call(
        warp_kernel,
        grid=(),
        in_specs=[smem, smem, vmem, vmem, vmem] + [hbm] * 18,
        out_specs=[vmem] * 2,
        out_shape=[
            jax.ShapeDtypeStruct((HZ * CY * 3 // 2, 128), F32),
            jax.ShapeDtypeStruct((3 * CY, 128), F32),
        ],
        scratch_shapes=[
            pltpu.VMEM((8, HZ + 2, PROWS, 128), BF16),
            pltpu.VMEM((8, VROWS, 128), BF16),
            pltpu.VMEM((3, 3 * HZ * CY, 128), F32),
            pltpu.VMEM((3, 3 * HZ * CY, 128), F32),
            pltpu.VMEM((2, HZ * CY, 128), F32),
            pltpu.SemaphoreType.DMA((18,)),
        ],
        name="warp_sum",
    )(info, assign, *tables, *planes, *fields, below, above)


def relax_kernel(info, *rest):
    parts = rest[:16]
    out, chunks, arriving, flat, pair, flat2, pair2, even, odd, ready, sems = rest[16:]
    copies = [
        pltpu.make_async_copy(part, chunks.at[k], arriving.at[k]) for k, part in enumerate(parts)
    ]
    for copy in copies:
        copy.start()
    level, me, zone = info[0], info[1], info[2]
    size = flat.shape[1] - 16
    for held in (flat, pair, flat2, pair2):
        held[:, :8] = jnp.zeros((held.shape[0], 8, 128), F32)
        held[:, size + 8 :] = jnp.zeros((held.shape[0], 8, 128), F32)
    for held in (flat, flat2):
        for z in (0, held.shape[0] - 1):
            held[z, 8 : 8 + size] = jnp.zeros((size, 128), F32)
    for copy in copies:
        copy.wait()
    narrow = lax.broadcasted_iota(jnp.int32, (CY, 128), 1)
    tail = HZ * 3 // 2
    for peer in range(8):
        rows = slice(8 + CY * peer, 8 + CY * (peer + 1))

        def block(half, index):
            slot = (half ^ level) * 8 + (peer ^ me)
            return chunks[slot, CY * index : CY * (index + 1)]

        for half in range(2):
            for z in range(HZ):
                flat[3 + 14 * half + z, rows] = block(half, z)
            for z in range(2):
                flat[1 + 28 * half + z, rows] = block(half, tail + z)
        packed = [HZ + z % (HZ // 2) for z in range(HZ)]
        sides = [z // (HZ // 2) for z in range(HZ)]
        lows = [(tail + 2, 0), (tail + 2, 1)] + list(zip(packed, sides))
        highs = list(zip(packed, sides)) + [(tail + 2, 0), (tail + 2, 1)]
        for index in range(14):
            low, high = block(0, lows[index][0]), block(1, highs[index][0])
            if lows[index][1] == 1:
                low = pltpu.roll(low, 64, 1)
            if highs[index][1] == 0:
                high = pltpu.roll(high, 64, 1)
            pair[1 + index, rows] = jnp.where(narrow < 64, low, high)

    def mirror(planes, both):
        body = slice(8, 8 + size)
        both[0, body] = pltpu.roll(both[14, body], 64, 1)
        both[15, body] = pltpu.roll(both[1, body], 64, 1)
        planes[16, body] = pltpu.roll(planes[14, body], 64, 1)
        planes[15, body] = pltpu.roll(planes[17, body], 64, 1)

    mirror(flat, pair)
    count = 2 * CY
    lane = lax.broadcasted_iota(jnp.int32, (count, 128), 1)

    def shift(planes, index, sums):
        for start in range(8, 8 + size, count):
            refs = [(planes[0], index), (planes[0], index + 16), (planes[1], index)]
            part = [held[z, start : start + count] for held, z in refs]
            left = [pltpu.roll(p, 1, 1) for p in part]
            right = [pltpu.roll(p, 127, 1) for p in part]
            left[2] = jnp.where(lane == 0, left[0], jnp.where(lane == 64, left[1], left[2]))
            left[0] = jnp.where(lane == 0, 0.0, left[0])
            left[1] = jnp.where(lane == 64, 0.0, left[1])
            right[0] = jnp.where(lane == 127, right[2], right[0])
            right[1] = jnp.where(lane == 63, right[2], right[1])
            right[2] = jnp.where(lane % 64 == 63, 0.0, right[2])
            for b in range(3):
                sums[b, start - 8 : start - 8 + count] = left[b] + right[b]

    def swept(planes, index, sums, start, scale):
        refs = [(planes[0], index), (planes[0], index + 16), (planes[1], index)]
        done = []
        for b, (held, z) in enumerate(refs):
            around = held[z - 1, start : start + count] + held[z + 1, start : start + count]
            around += held[z, start - 1 : start - 1 + count] + held[z, start + 1 : start + 1 + count]
            around += sums[b, start - 8 : start - 8 + count]
            value = around + (2.0 / 3.0) * held[z, start : start + count]
            done.append(value if scale is None else scale * value)
        return done

    def sweep(planes, store, scale, after):
        shift(planes, 1, even)

        def turn(step, carry):
            index = 2 * step + 1
            shift(planes, index + 1, odd)
            for start in range(8, 8 + size, count):
                store(index, start, swept(planes, index, even, start, scale))
            shift(planes, jnp.minimum(index + 2, 14), even)
            for start in range(8, 8 + size, count):
                store(index + 1, start, swept(planes, index + 1, odd, start, scale))
            after(index)
            after(index + 1)
            return carry

        lax.fori_loop(0, 7, turn, 0)

    def first(index, start, done):
        flat2[index, start : start + count] = done[0]
        flat2[index + 16, start : start + count] = done[1]
        pair2[index, start : start + count] = done[2]

    sweep((flat, pair), first, None, lambda index: None)
    whole = lax.broadcasted_iota(jnp.int32, (size, 128), 1)

    @pl.when(zone == 0)
    def _():
        flat2[2, 8 : 8 + size] = jnp.zeros((size, 128), F32)
        pair2[2, 8 : 8 + size] = jnp.where(whole < 64, 0.0, pair2[2, 8 : 8 + size])

    @pl.when(zone == 7)
    def _():
        flat2[29, 8 : 8 + size] = jnp.zeros((size, 128), F32)
        pair2[13, 8 : 8 + size] = jnp.where(whole < 64, pair2[13, 8 : 8 + size], 0.0)

    mirror(flat2, pair2)

    def emit(z):
        return pltpu.make_async_copy(ready.at[z + 2], out.at[z], sems.at[z])

    def second(index, start, done):
        rows = slice(start - 8, start - 8 + count)
        ready[index - 1, rows, :128] = done[0]
        ready[index - 1, rows, 128:] = done[2][:, :64]
        ready[index + 13, rows, :128] = pltpu.roll(done[1], 64, 1)
        ready[index + 13, rows, 128:] = pltpu.roll(done[2], 64, 1)[:, :64]

    def depart(index):
        @pl.when(index >= 3)
        def _():
            emit(index - 3).start()

        @pl.when(index <= 12)
        def _():
            emit(index + 11).start()

    sweep((flat2, pair2), second, 0.15 * 0.15 / SCALE, depart)

    def finish(z, carry):
        emit(z).wait()
        return carry

    lax.fori_loop(0, 24, finish, 0)


def relax(info, parts):
    hbm = pl.BlockSpec(memory_space=pl.ANY)
    return pl.pallas_call(
        relax_kernel,
        grid=(),
        in_specs=[pl.BlockSpec(memory_space=pltpu.SMEM)] + [hbm] * 16,
        out_specs=hbm,
        out_shape=jax.ShapeDtypeStruct((24, 192, 192), F32),
        scratch_shapes=[
            pltpu.VMEM((16,) + parts[0].shape, F32),
            pltpu.SemaphoreType.DMA((16,)),
            pltpu.VMEM((32, 208, 128), F32),
            pltpu.VMEM((16, 208, 128), F32),
            pltpu.VMEM((32, 208, 128), F32),
            pltpu.VMEM((16, 208, 128), F32),
            pltpu.VMEM((3, 192, 128), F32),
            pltpu.VMEM((3, 192, 128), F32),
            pltpu.VMEM((28, 192, 192), F32),
            pltpu.SemaphoreType.DMA((24,)),
        ],
        name="relax",
    )(info, *parts)


def update(images, momenta, assign):
    level = lax.axis_index("level")
    me = lax.axis_index("subj")
    zone = lax.axis_index("gz")
    info = jnp.stack([level, me, zone]).astype(jnp.int32)
    zones = lax.axis_size("gz")
    outward = [(g, g + 1) for g in range(zones - 1)]
    outward += [(zones + g + 1, zones + g) for g in range(zones - 1)]
    nearest = ("level", "gz")
    cross = [(zones + g, g + 1) for g in range(zones - 1)]
    cross += [(g + 1, zones + g) for g in range(zones - 1)]
    climb = [(g, zones + g) for g in range(zones)]
    climb += [(zones + g, g + 1) for g in range(zones - 1)]
    rim = lax.dynamic_slice_in_dim(momenta, 9 * (1 - level), 3, axis=1)
    rim = lax.ppermute(rim, nearest, outward)

    def spread(parts):
        arrived = {0: parts[0]}
        for k in SPREAD:
            arrived[k] = lax.ppermute(parts[k], "subj", [(i, i ^ k) for i in range(8)])
        return [arrived[k] for k in range(8)]

    packed = pack_images(info, images)
    planes = spread(packed)
    blurred = blur(info, momenta, rim)
    fields = spread(blurred)
    low, high = edges(planes)
    below = lax.ppermute(high, nearest, climb)
    above = lax.ppermute(low, nearest, [(b, a) for a, b in climb])
    chunk, edge = warp(info, assign, planes, fields, below, above)
    edge = lax.ppermute(edge.astype(jnp.float16), nearest, cross)
    chunk = jnp.concatenate([chunk.astype(jnp.float16), edge], axis=0)
    gathered = []
    for far in range(2):
        for step in range(4):
            part = chunk
            if far or step:
                perm = [
                    (8 * a + i, 8 * (a ^ far) + (i ^ (2 * step))) for a in range(2) for i in range(8)
                ]
                part = lax.ppermute(chunk, ("level", "subj"), perm)
            gathered += [part, lax.ppermute(part, "subj", [(i, i ^ 1) for i in range(8)])]
    return relax(info, [part.astype(F32) for part in gathered])


def solution(mesh):
    return jax.shard_map(
        update,
        mesh=mesh,
        in_specs=(P("subj", "gz", None, None), P("subj", "gz", None, None, None), P()),
        out_specs=P("gz", None, None),
        check_vma=False,
    )
```

```python
import jax
import jax.numpy as jnp
import numpy as np
from jax import lax
from jax.experimental import pallas as pl
from jax.experimental.pallas import tpu as pltpu
from jax.sharding import PartitionSpec as P


F32 = jnp.float32
BF16 = jnp.bfloat16
HZ = 12
CY = 24
CZ = HZ // 2 + 2
CW = CY // 2 + 2
VR = CZ * CW
VROWS = 5 * VR
PROWS = 80
SPREAD = (1, 3, 7, 5, 2, 6, 4)
SCALE = 128.0


def lerp_table(fine):
    table = np.zeros((fine, fine // 2 + 2), np.float32)
    for row in range(fine):
        near = row // 2 + 1
        table[row, near] += 0.75
        table[row, near + 2 * (row % 2) - 1] += 0.25
    return table


def zy_table():
    return np.kron(lerp_table(HZ), lerp_table(CY))


def x_table(fine, slot):
    inner = lerp_table(fine)[:, 1:-1].T
    coarse = fine // 2
    table = np.zeros((256, 256), np.float32)
    for base in (0, 128):
        table[base : base + coarse, :128] = inner[:, :128]
        table[base : base + coarse, 128 + 64 * slot : 192 + 64 * slot] = inner[:, 128:]
    return table


def pack_plane(plane, put):
    count = plane.shape[1] // CY
    low = [plane[0][:, :128], plane[1][:, :128]]
    both = jnp.concatenate([plane[0][:, 128:], plane[1][:, 128:]], axis=1)
    parts = low + [both]
    row = lax.broadcasted_iota(jnp.int32, (8, 128), 0)
    for peer in range(count):
        start = CY * peer
        halo = jnp.zeros((8, 128), F32)
        for index, part in enumerate(parts):
            if peer > 0:
                halo = jnp.where(row == 2 * index, part[start - 1 : start], halo)
            if peer < count - 1:
                halo = jnp.where(row == 2 * index + 1, part[start + CY : start + CY + 1], halo)
        blocks = [part[start : start + CY] for part in parts] + [halo]
        put(peer, jnp.concatenate(blocks, axis=0))


GROUPS = ((0, 3), (3, 3), (6, 3), (9, 3))


def pack_kernel(info, images, *rest):
    outs = rest[:8]
    held, stage, sems, gone = rest[8:]
    level, me = info[0], info[1]
    loads = []
    for index, (first, count) in enumerate(GROUPS):
        rows = pl.ds(HZ * level + first, count)
        loads.append(
            pltpu.make_async_copy(
                images.at[:, rows], held.at[:, pl.ds(first, count)], sems.at[index]
            )
        )
    for copy in loads:
        copy.start()
    sent = []
    for index, (first, count) in enumerate(GROUPS):
        loads[index].wait()

        def step(z, carry):
            def put(peer, value):
                stage[peer, z] = value.astype(BF16)

            pack_plane(held[:, z].astype(F32), put)
            return carry

        lax.fori_loop(first, first + count, step, 0)
        for k, out in enumerate(outs):
            rows = pl.ds(first, count)
            copy = pltpu.make_async_copy(
                stage.at[me ^ k, rows], out.at[rows], gone.at[8 * index + k]
            )
            copy.start()
            sent.append(copy)
    for copy in sent:
        copy.wait()


def pack_images(info, images):
    hbm = pl.BlockSpec(memory_space=pl.ANY)
    return pl.pallas_call(
        pack_kernel,
        grid=(),
        in_specs=[pl.BlockSpec(memory_space=pltpu.SMEM), hbm],
        out_specs=[hbm] * 8,
        out_shape=[jax.ShapeDtypeStruct((HZ, PROWS, 128), BF16)] * 8,
        scratch_shapes=[
            pltpu.VMEM((2, HZ, 192, 192), BF16),
            pltpu.VMEM((8, HZ, PROWS, 128), BF16),
            pltpu.SemaphoreType.DMA((len(GROUPS),)),
            pltpu.SemaphoreType.DMA((8 * len(GROUPS),)),
        ],
        name="pack_images",
    )(info, images)


def blur_kernel(info, momenta, halo, other, *rest):
    outs = rest[:8]
    held, stage, tall, wide, third, piece, sems, gone = rest[8:]
    level, me = info[0], info[1]
    half = info[2] * 2 + level
    own = pltpu.make_async_copy(
        momenta.at[:, pl.ds(3 * level, 9)], held.at[:, pl.ds(3 - 3 * level, 9)], sems.at[0]
    )
    sides = [
        pltpu.make_async_copy(rows.at[0], held.at[j, pl.ds(9 * level, 3)], sems.at[1 + j])
        for j, rows in enumerate((halo, other))
    ]
    for copy in [own] + sides:
        copy.start()
    for held_rows in (tall, wide):
        held_rows[:, :8] = jnp.zeros((CZ, 8, 128), F32)
        held_rows[:, 104:] = jnp.zeros((CZ, 8, 128), F32)
    for copy in [own] + sides:
        copy.wait()
    first = (half > 0).astype(F32)
    last = (half < 15).astype(F32)
    spare = jnp.zeros((96, 32), F32)
    plane_lane = lax.broadcasted_iota(jnp.int32, (96, 128), 1)
    for subject, component in ((1, 0), (0, 0), (0, 1), (0, 2), (1, 1), (1, 2)):

        def row(r, carry, subject=subject, component=component):
            def m(t):
                return held[subject, r + t, component]

            z = (m(0) + m(4)) * 0.0625 + (m(1) + m(3)) * 0.25 + m(2) * 0.375
            z = z * jnp.where(r == 0, first, jnp.where(r == CZ - 1, last, 1.0))
            z = jnp.concatenate([z, spare], axis=1)

            def lane(k):
                return pltpu.roll(z, k % 128, 1)

            x = (lane(2) + lane(-2)) * 0.0625 + (lane(1) + lane(-1)) * 0.25 + z * 0.375
            tall[r, 8:104] = x
            y = (tall[r, 6:102] + tall[r, 10:106]) * 0.0625
            y += (tall[r, 7:103] + tall[r, 9:105]) * 0.25
            y += x * 0.375
            if (subject, component) == (1, 0):
                third[r] = y
            elif subject == 0:
                extra = pltpu.roll(third[r], 96 - 32 * component, 1)
                wide[r, 8:104] = jnp.where(plane_lane < 96, y, extra)
            else:
                wide[r, 8:104] = y
            return carry

        lax.fori_loop(0, CZ, row, 0, unroll=2)
        if (subject, component) == (1, 0):
            continue
        block = 2 * subject + component
        for peer in range(8):
            start = 8 + (CY // 2) * peer - 1
            for r in range(CZ):
                piece[CW * r : CW * (r + 1)] = wide[r, start : start + CW]
            stage[peer, VR * block : VR * (block + 1)] = piece[...].astype(BF16)
    sent = [
        pltpu.make_async_copy(stage.at[me ^ k], out, gone.at[k]) for k, out in enumerate(outs)
    ]
    for copy in sent:
        copy.start()
    for copy in sent:
        copy.wait()


def blur(info, momenta, halo, other):
    rows = VROWS
    return pl.pallas_call(
        blur_kernel,
        grid=(),
        in_specs=[
            pl.BlockSpec(memory_space=pltpu.SMEM),
            pl.BlockSpec(memory_space=pl.ANY),
            pl.BlockSpec(memory_space=pl.ANY),
            pl.BlockSpec(memory_space=pl.ANY),
        ],
        out_specs=[pl.BlockSpec(memory_space=pl.ANY)] * 8,
        out_shape=[jax.ShapeDtypeStruct((rows, 128), BF16)] * 8,
        scratch_shapes=[
            pltpu.VMEM((2, 12, 3, 96, 96), F32),
            pltpu.VMEM((8, rows, 128), BF16),
            pltpu.VMEM((CZ, 112, 128), F32),
            pltpu.VMEM((CZ, 112, 128), F32),
            pltpu.VMEM((CZ, 96, 128), F32),
            pltpu.VMEM((VR, 128), F32),
            pltpu.SemaphoreType.DMA((3,)),
            pltpu.SemaphoreType.DMA((8,)),
        ],
        name="blur_momenta",
    )(info, momenta, halo, other)


def edge_kernel(*refs):
    planes, below, above = refs[:8], refs[8], refs[9]
    low, high, sems, gone = refs[10:]
    copies = []
    for k, plane in enumerate(planes):
        copies.append(pltpu.make_async_copy(plane.at[0], low.at[k], sems.at[k]))
        copies.append(pltpu.make_async_copy(plane.at[HZ - 1], high.at[k], sems.at[8 + k]))
    for copy in copies:
        copy.start()
    for copy in copies:
        copy.wait()
    leaving = [
        pltpu.make_async_copy(low, below, gone.at[0]),
        pltpu.make_async_copy(high, above, gone.at[1]),
    ]
    for copy in leaving:
        copy.start()
    for copy in leaving:
        copy.wait()


def edges(planes):
    hbm = pl.BlockSpec(memory_space=pl.ANY)
    shape = (8, PROWS, 128)
    return pl.pallas_call(
        edge_kernel,
        grid=(),
        in_specs=[hbm] * 8,
        out_specs=[hbm] * 2,
        out_shape=[jax.ShapeDtypeStruct(shape, BF16)] * 2,
        scratch_shapes=[
            pltpu.VMEM(shape, BF16),
            pltpu.VMEM(shape, BF16),
            pltpu.SemaphoreType.DMA((16,)),
            pltpu.SemaphoreType.DMA((2,)),
        ],
        name="cut_edges",
    )(*planes)


def warp_kernel(info, assign, zy, x0, x1, *rest):
    planes, fields, below, above = rest[:8], rest[8:16], rest[16], rest[17]
    chunk, edge = rest[18:20]
    image, field, even, odd, acc, sems = rest[20:]
    level, me = info[0], info[1]
    copies = [
        pltpu.make_async_copy(below, image.at[:, 0], sems.at[16]),
        pltpu.make_async_copy(above, image.at[:, HZ + 1], sems.at[17]),
    ]
    for k in range(8):
        copies.append(
            pltpu.make_async_copy(planes[k], image.at[k, 1 : HZ + 1], sems.at[k])
        )
    first = [pltpu.make_async_copy(fields[k], field.at[k], sems.at[8 + k]) for k in range(8)]
    for copy in first + copies:
        copy.start()
    acc[...] = jnp.zeros_like(acc)
    for copy in first:
        copy.wait()
    lane = lax.broadcasted_iota(jnp.int32, (CY, 128), 1)
    sub = lax.broadcasted_iota(jnp.int32, (CY, 128), 0)
    coarse_lane = lax.broadcasted_iota(jnp.int32, (VR, 128), 1)

    def neighbours(part):
        left0, left1, left2 = (pltpu.roll(p, 1, 1) for p in part)
        right0, right1, right2 = (pltpu.roll(p, 127, 1) for p in part)
        left2 = jnp.where(lane == 0, left0, jnp.where(lane == 64, pltpu.roll(part[1], 65, 1), left2))
        left0 = jnp.where(lane == 0, 0.0, left0)
        left1 = jnp.where(lane == 0, 0.0, left1)
        right0 = jnp.where(lane == 127, right2, right0)
        right1 = jnp.where(lane == 127, pltpu.roll(part[2], 63, 1), right1)
        right2 = jnp.where(lane % 64 == 63, 0.0, right2)
        return (left0, left1, left2), (right0, right1, right2)

    def interpolate(k, velocity):
        base = 2 * (me ^ k)
        slots = [(assign[base + j] // 2) ^ me for j in range(2)]
        stacked = [[], []]
        for c in range(3):
            parts = [field[slots[0], VR * c : VR * (c + 1)]]
            if c > 0:
                parts.append(field[slots[1], VR * (c + 2) : VR * (c + 3)])
            else:
                spread = [
                    pltpu.roll(
                        field[slots[1], VR * t : VR * (t + 1)].astype(F32), 32 * t + 32, 1
                    )
                    for t in range(3)
                ]
                third = jnp.where(
                    coarse_lane < 32, spread[0], jnp.where(coarse_lane < 64, spread[1], spread[2])
                )
                parts.append(third.astype(BF16))
            rough = jnp.dot(
                zy[...], jnp.concatenate(parts, axis=1), preferred_element_type=F32
            )
            high = rough.astype(BF16)
            low = (rough - high.astype(F32)).astype(BF16)
            for j in range(2):
                own = slice(128 * j, 128 * j + 128)
                stacked[j].append(jnp.concatenate([high[:, own], low[:, own]], axis=1))
        fine = [
            jnp.dot(jnp.concatenate(stacked[j], axis=0), table[...], preferred_element_type=F32)
            for j, table in enumerate((x0, x1))
        ]
        velocity[0] = fine[0][:, :128]
        velocity[1] = fine[1][:, :128]
        velocity[2] = fine[0][:, 128:] + fine[1][:, 128:]

    def apply(k, velocity):
        for z in range(HZ):
            before = image[k, z].astype(F32)
            centre = image[k, z + 1].astype(F32)
            after = image[k, z + 2].astype(F32)
            part = [centre[CY * b : CY * (b + 1)] for b in range(3)]
            halo = centre[3 * CY :]
            left, right = neighbours(part)
            warped = []
            for b in range(3):
                own = slice(CY * b, CY * (b + 1))
                up = jnp.where(sub == 0, halo[2 * b : 2 * b + 1], pltpu.roll(part[b], 1, 0))
                down = jnp.where(
                    sub == CY - 1, halo[2 * b + 1 : 2 * b + 2], pltpu.roll(part[b], CY - 1, 0)
                )

                def v(c):
                    start = HZ * CY * c + CY * z
                    return velocity[b, start : start + CY]

                push = v(0) * (right[b] - left[b]) + v(1) * (down - up)
                push += v(2) * (after[own] - before[own])
                warped.append(part[b] - 0.5 * push)
            rows = slice(CY * z, CY * (z + 1))
            acc[0, rows] += warped[0] + warped[1]
            acc[1, rows] += warped[2]

    interpolate(0, even)
    for copy in copies:
        copy.wait()

    def turn(step, carry):
        interpolate(2 * step + 1, odd)
        apply(2 * step, even)
        interpolate(jnp.minimum(2 * step + 2, 7), even)
        apply(2 * step + 1, odd)
        return carry

    lax.fori_loop(0, 4, turn, 0)
    weight = SCALE / 16.0
    chunk[: HZ * CY] = pltpu.roll(acc[0] * weight, 64 * level, 1)
    wide = lax.broadcasted_iota(jnp.int32, (CY, 128), 1)

    def joined(z, other):
        one, two = (acc[1, pl.ds(pl.multiple_of(r * CY, 8), CY)] for r in (z, other))
        one = one + pltpu.roll(one, 64, 1)
        two = two + pltpu.roll(two, 64, 1)
        return jnp.where(wide < 64, one, two) * weight

    for z in range(HZ // 2):
        chunk[(HZ + z) * CY : (HZ + z + 1) * CY] = joined(z, z + HZ // 2)
    outer = (HZ - 2) * level
    rim = acc[0, pl.ds(pl.multiple_of(outer * CY, 8), 2 * CY)] * weight
    edge[: 2 * CY] = pltpu.roll(rim, 64 - 64 * level, 1)
    edge[2 * CY :] = joined(outer, outer + 1)


def warp(info, assign, planes, fields, below, above):
    tables = [
        jnp.asarray(t, BF16) for t in (zy_table(), x_table(192, 0), x_table(192, 1))
    ]
    vmem = pl.BlockSpec(memory_space=pltpu.VMEM)
    smem = pl.BlockSpec(memory_space=pltpu.SMEM)
    hbm = pl.BlockSpec(memory_space=pl.ANY)
    return pl.pallas_call(
        warp_kernel,
        grid=(),
        in_specs=[smem, smem, vmem, vmem, vmem] + [hbm] * 18,
        out_specs=[vmem] * 2,
        out_shape=[
            jax.ShapeDtypeStruct((HZ * CY * 3 // 2, 128), F32),
            jax.ShapeDtypeStruct((3 * CY, 128), F32),
        ],
        scratch_shapes=[
            pltpu.VMEM((8, HZ + 2, PROWS, 128), BF16),
            pltpu.VMEM((8, VROWS, 128), BF16),
            pltpu.VMEM((3, 3 * HZ * CY, 128), F32),
            pltpu.VMEM((3, 3 * HZ * CY, 128), F32),
            pltpu.VMEM((2, HZ * CY, 128), F32),
            pltpu.SemaphoreType.DMA((18,)),
        ],
        name="warp_sum",
    )(info, assign, *tables, *planes, *fields, below, above)


def relax_kernel(info, chunks, out, flat, pair, flat2, pair2, even, odd, ready, sems):
    level, me, zone = info[0], info[1], info[2]
    size = flat.shape[1] - 16
    for held in (flat, pair, flat2, pair2):
        held[:, :8] = jnp.zeros((held.shape[0], 8, 128), F32)
        held[:, size + 8 :] = jnp.zeros((held.shape[0], 8, 128), F32)
    for held in (flat, flat2):
        for z in (0, held.shape[0] - 1):
            held[z, 8 : 8 + size] = jnp.zeros((size, 128), F32)
    narrow = lax.broadcasted_iota(jnp.int32, (CY, 128), 1)
    tail = HZ * 3 // 2
    for peer in range(8):
        rows = slice(8 + CY * peer, 8 + CY * (peer + 1))

        def block(half, index):
            slot = (half ^ level) * 8 + (peer ^ me)
            return chunks[slot, CY * index : CY * (index + 1)]

        for half in range(2):
            for z in range(HZ):
                flat[3 + 14 * half + z, rows] = block(half, z)
            for z in range(2):
                flat[1 + 28 * half + z, rows] = block(half, tail + z)
        packed = [HZ + z % (HZ // 2) for z in range(HZ)]
        sides = [z // (HZ // 2) for z in range(HZ)]
        lows = [(tail + 2, 0), (tail + 2, 1)] + list(zip(packed, sides))
        highs = list(zip(packed, sides)) + [(tail + 2, 0), (tail + 2, 1)]
        for index in range(14):
            low, high = block(0, lows[index][0]), block(1, highs[index][0])
            if lows[index][1] == 1:
                low = pltpu.roll(low, 64, 1)
            if highs[index][1] == 0:
                high = pltpu.roll(high, 64, 1)
            pair[1 + index, rows] = jnp.where(narrow < 64, low, high)

    def mirror(planes, both):
        body = slice(8, 8 + size)
        both[0, body] = pltpu.roll(both[14, body], 64, 1)
        both[15, body] = pltpu.roll(both[1, body], 64, 1)
        planes[16, body] = pltpu.roll(planes[14, body], 64, 1)
        planes[15, body] = pltpu.roll(planes[17, body], 64, 1)

    mirror(flat, pair)
    count = 2 * CY
    lane = lax.broadcasted_iota(jnp.int32, (count, 128), 1)

    def shift(planes, index, sums):
        for start in range(8, 8 + size, count):
            refs = [(planes[0], index), (planes[0], index + 16), (planes[1], index)]
            part = [held[z, start : start + count] for held, z in refs]
            left = [pltpu.roll(p, 1, 1) for p in part]
            right = [pltpu.roll(p, 127, 1) for p in part]
            left[2] = jnp.where(lane == 0, left[0], jnp.where(lane == 64, left[1], left[2]))
            left[0] = jnp.where(lane == 0, 0.0, left[0])
            left[1] = jnp.where(lane == 64, 0.0, left[1])
            right[0] = jnp.where(lane == 127, right[2], right[0])
            right[1] = jnp.where(lane == 63, right[2], right[1])
            right[2] = jnp.where(lane % 64 == 63, 0.0, right[2])
            for b in range(3):
                sums[b, start - 8 : start - 8 + count] = left[b] + right[b]

    def swept(planes, index, sums, start, scale):
        refs = [(planes[0], index), (planes[0], index + 16), (planes[1], index)]
        done = []
        for b, (held, z) in enumerate(refs):
            around = held[z - 1, start : start + count] + held[z + 1, start : start + count]
            around += held[z, start - 1 : start - 1 + count] + held[z, start + 1 : start + 1 + count]
            around += sums[b, start - 8 : start - 8 + count]
            value = around + (2.0 / 3.0) * held[z, start : start + count]
            done.append(value if scale is None else scale * value)
        return done

    def sweep(planes, store, scale, after):
        shift(planes, 1, even)

        def turn(step, carry):
            index = 2 * step + 1
            shift(planes, index + 1, odd)
            for start in range(8, 8 + size, count):
                store(index, start, swept(planes, index, even, start, scale))
            shift(planes, jnp.minimum(index + 2, 14), even)
            for start in range(8, 8 + size, count):
                store(index + 1, start, swept(planes, index + 1, odd, start, scale))
            after(index)
            after(index + 1)
            return carry

        lax.fori_loop(0, 7, turn, 0)

    def first(index, start, done):
        flat2[index, start : start + count] = done[0]
        flat2[index + 16, start : start + count] = done[1]
        pair2[index, start : start + count] = done[2]

    sweep((flat, pair), first, None, lambda index: None)
    whole = lax.broadcasted_iota(jnp.int32, (size, 128), 1)

    @pl.when(zone == 0)
    def _():
        flat2[2, 8 : 8 + size] = jnp.zeros((size, 128), F32)
        pair2[2, 8 : 8 + size] = jnp.where(whole < 64, 0.0, pair2[2, 8 : 8 + size])

    @pl.when(zone == 7)
    def _():
        flat2[29, 8 : 8 + size] = jnp.zeros((size, 128), F32)
        pair2[13, 8 : 8 + size] = jnp.where(whole < 64, pair2[13, 8 : 8 + size], 0.0)

    mirror(flat2, pair2)

    def emit(z):
        return pltpu.make_async_copy(ready.at[z + 2], out.at[z], sems.at[z])

    def second(index, start, done):
        rows = slice(start - 8, start - 8 + count)
        ready[index - 1, rows, :128] = done[0]
        ready[index - 1, rows, 128:] = done[2][:, :64]
        ready[index + 13, rows, :128] = pltpu.roll(done[1], 64, 1)
        ready[index + 13, rows, 128:] = pltpu.roll(done[2], 64, 1)[:, :64]

    def depart(index):
        @pl.when(index >= 3)
        def _():
            emit(index - 3).start()

        @pl.when(index <= 12)
        def _():
            emit(index + 11).start()

    sweep((flat2, pair2), second, 0.15 * 0.15 / SCALE, depart)

    def finish(z, carry):
        emit(z).wait()
        return carry

    lax.fori_loop(0, 24, finish, 0)


def relax(info, chunks):
    vmem = pl.BlockSpec(memory_space=pltpu.VMEM)
    return pl.pallas_call(
        relax_kernel,
        grid=(),
        in_specs=[pl.BlockSpec(memory_space=pltpu.SMEM), vmem],
        out_specs=pl.BlockSpec(memory_space=pl.ANY),
        out_shape=jax.ShapeDtypeStruct((24, 192, 192), F32),
        scratch_shapes=[
            pltpu.VMEM((32, 208, 128), F32),
            pltpu.VMEM((16, 208, 128), F32),
            pltpu.VMEM((32, 208, 128), F32),
            pltpu.VMEM((16, 208, 128), F32),
            pltpu.VMEM((3, 192, 128), F32),
            pltpu.VMEM((3, 192, 128), F32),
            pltpu.VMEM((28, 192, 192), F32),
            pltpu.SemaphoreType.DMA((24,)),
        ],
        name="relax",
    )(info, chunks)


def update(images, momenta, assign):
    level = lax.axis_index("level")
    me = lax.axis_index("subj")
    zone = lax.axis_index("gz")
    info = jnp.stack([level, me, zone]).astype(jnp.int32)
    zones = lax.axis_size("gz")
    outward = [(g, g + 1) for g in range(zones - 1)]
    outward += [(zones + g + 1, zones + g) for g in range(zones - 1)]
    nearest = ("level", "gz")
    cross = [(zones + g, g + 1) for g in range(zones - 1)]
    cross += [(g + 1, zones + g) for g in range(zones - 1)]
    climb = [(g, zones + g) for g in range(zones)]
    climb += [(zones + g, g + 1) for g in range(zones - 1)]
    part = (1, 3) + momenta.shape[2:]
    rim = lax.dynamic_slice(momenta, (0, 9 * (1 - level), 0, 0, 0), part)
    other = lax.dynamic_slice(momenta, (1, 9 * level, 0, 0, 0), part)
    rim = lax.ppermute(rim, nearest, outward)
    other = lax.ppermute(other, nearest, cross)

    def spread(parts):
        arrived = {0: parts[0]}
        for k in SPREAD:
            arrived[k] = lax.ppermute(parts[k], "subj", [(i, i ^ k) for i in range(8)])
        return [arrived[k] for k in range(8)]

    packed = pack_images(info, images)
    planes = spread(packed)
    blurred = blur(info, momenta, rim, other)
    fields = spread(blurred)
    low, high = edges(planes)
    below = lax.ppermute(high, nearest, climb)
    above = lax.ppermute(low, nearest, [(b, a) for a, b in climb])
    chunk, edge = warp(info, assign, planes, fields, below, above)
    edge = lax.ppermute(edge.astype(jnp.float16), nearest, cross)
    chunk = jnp.concatenate([chunk.astype(jnp.float16), edge], axis=0)
    gathered = []
    for far in range(2):
        for step in range(4):
            part = chunk
            if far or step:
                perm = [
                    (8 * a + i, 8 * (a ^ far) + (i ^ (2 * step))) for a in range(2) for i in range(8)
                ]
                part = lax.ppermute(chunk, ("level", "subj"), perm)
            gathered += [part, lax.ppermute(part, "subj", [(i, i ^ 1) for i in range(8)])]
    chunks = jnp.stack(gathered).astype(F32)
    return relax(info, chunks)


def solution(mesh):
    return jax.shard_map(
        update,
        mesh=mesh,
        in_specs=(P("subj", "gz", None, None), P("subj", "gz", None, None, None), P()),
        out_specs=P("gz", None, None),
        check_vma=False,
    )
```

```python
import jax
import jax.numpy as jnp
import numpy as np
from jax import lax
from jax.experimental import pallas as pl
from jax.experimental.pallas import tpu as pltpu
from jax.sharding import PartitionSpec as P


F32 = jnp.float32
BF16 = jnp.bfloat16
HZ = 12
CY = 24
CZ = HZ // 2 + 2
CW = CY // 2 + 2
VR = CZ * CW
VROWS = 5 * VR
PROWS = 80
SPREAD = (1, 3, 7, 5, 2, 6, 4)
SCALE = 128.0


def lerp_table(fine):
    table = np.zeros((fine, fine // 2 + 2), np.float32)
    for row in range(fine):
        near = row // 2 + 1
        table[row, near] += 0.75
        table[row, near + 2 * (row % 2) - 1] += 0.25
    return table


def zy_table():
    return np.kron(lerp_table(HZ), lerp_table(CY))


def x_table(fine, slot):
    inner = lerp_table(fine)[:, 1:-1].T
    coarse = fine // 2
    table = np.zeros((256, 256), np.float32)
    for base in (0, 128):
        table[base : base + coarse, :128] = inner[:, :128]
        table[base : base + coarse, 128 + 64 * slot : 192 + 64 * slot] = inner[:, 128:]
    return table


def pack_plane(plane, put):
    count = plane.shape[1] // CY
    low = [plane[0][:, :128], plane[1][:, :128]]
    both = jnp.concatenate([plane[0][:, 128:], plane[1][:, 128:]], axis=1)
    parts = low + [both]
    row = lax.broadcasted_iota(jnp.int32, (8, 128), 0)
    for peer in range(count):
        start = CY * peer
        halo = jnp.zeros((8, 128), F32)
        for index, part in enumerate(parts):
            if peer > 0:
                halo = jnp.where(row == 2 * index, part[start - 1 : start], halo)
            if peer < count - 1:
                halo = jnp.where(row == 2 * index + 1, part[start + CY : start + CY + 1], halo)
        blocks = [part[start : start + CY] for part in parts] + [halo]
        put(peer, jnp.concatenate(blocks, axis=0))


GROUPS = ((0, 3), (3, 3), (6, 3), (9, 3))


def pack_kernel(info, images, *rest):
    outs = rest[:8]
    held, stage, sems, gone = rest[8:]
    level, me = info[0], info[1]
    loads = []
    for index, (first, count) in enumerate(GROUPS):
        rows = pl.ds(HZ * level + first, count)
        loads.append(
            pltpu.make_async_copy(
                images.at[:, rows], held.at[:, pl.ds(first, count)], sems.at[index]
            )
        )
    for copy in loads:
        copy.start()
    sent = []
    for index, (first, count) in enumerate(GROUPS):
        loads[index].wait()

        def step(z, carry):
            def put(peer, value):
                stage[peer, z] = value.astype(BF16)

            pack_plane(held[:, z].astype(F32), put)
            return carry

        lax.fori_loop(first, first + count, step, 0)
        for k, out in enumerate(outs):
            rows = pl.ds(first, count)
            copy = pltpu.make_async_copy(
                stage.at[me ^ k, rows], out.at[rows], gone.at[8 * index + k]
            )
            copy.start()
            sent.append(copy)
    for copy in sent:
        copy.wait()


def pack_images(info, images):
    hbm = pl.BlockSpec(memory_space=pl.ANY)
    return pl.pallas_call(
        pack_kernel,
        grid=(),
        in_specs=[pl.BlockSpec(memory_space=pltpu.SMEM), hbm],
        out_specs=[hbm] * 8,
        out_shape=[jax.ShapeDtypeStruct((HZ, PROWS, 128), BF16)] * 8,
        scratch_shapes=[
            pltpu.VMEM((2, HZ, 192, 192), BF16),
            pltpu.VMEM((8, HZ, PROWS, 128), BF16),
            pltpu.SemaphoreType.DMA((len(GROUPS),)),
            pltpu.SemaphoreType.DMA((8 * len(GROUPS),)),
        ],
        name="pack_images",
    )(info, images)


def blur_kernel(info, momenta, halo, other, *rest):
    outs = rest[:8]
    held, stage, tall, wide, third, piece, sems, gone = rest[8:]
    level, me = info[0], info[1]
    half = info[2] * 2 + level
    own = pltpu.make_async_copy(
        momenta.at[:, pl.ds(3 * level, 9)], held.at[:, pl.ds(3 - 3 * level, 9)], sems.at[0]
    )
    sides = [
        pltpu.make_async_copy(rows.at[0], held.at[j, pl.ds(9 * level, 3)], sems.at[1 + j])
        for j, rows in enumerate((halo, other))
    ]
    for copy in [own] + sides:
        copy.start()
    for held_rows in (tall, wide):
        held_rows[:, :8] = jnp.zeros((CZ, 8, 128), F32)
        held_rows[:, 104:] = jnp.zeros((CZ, 8, 128), F32)
    for copy in [own] + sides:
        copy.wait()
    first = (half > 0).astype(F32)
    last = (half < 15).astype(F32)
    spare = jnp.zeros((96, 32), F32)
    plane_lane = lax.broadcasted_iota(jnp.int32, (96, 128), 1)
    for subject, component in ((1, 0), (0, 0), (0, 1), (0, 2), (1, 1), (1, 2)):

        def row(r, carry, subject=subject, component=component):
            def m(t):
                return held[subject, r + t, component]

            z = (m(0) + m(4)) * 0.0625 + (m(1) + m(3)) * 0.25 + m(2) * 0.375
            z = z * jnp.where(r == 0, first, jnp.where(r == CZ - 1, last, 1.0))
            z = jnp.concatenate([z, spare], axis=1)

            def lane(k):
                return pltpu.roll(z, k % 128, 1)

            x = (lane(2) + lane(-2)) * 0.0625 + (lane(1) + lane(-1)) * 0.25 + z * 0.375
            tall[r, 8:104] = x
            y = (tall[r, 6:102] + tall[r, 10:106]) * 0.0625
            y += (tall[r, 7:103] + tall[r, 9:105]) * 0.25
            y += x * 0.375
            if (subject, component) == (1, 0):
                third[r] = y
            elif subject == 0:
                extra = pltpu.roll(third[r], 96 - 32 * component, 1)
                wide[r, 8:104] = jnp.where(plane_lane < 96, y, extra)
            else:
                wide[r, 8:104] = y
            return carry

        lax.fori_loop(0, CZ, row, 0, unroll=2)
        if (subject, component) == (1, 0):
            continue
        block = 2 * subject + component
        for peer in range(8):
            start = 8 + (CY // 2) * peer - 1
            for r in range(CZ):
                piece[CW * r : CW * (r + 1)] = wide[r, start : start + CW]
            stage[peer, VR * block : VR * (block + 1)] = piece[...].astype(BF16)
    sent = [
        pltpu.make_async_copy(stage.at[me ^ k], out, gone.at[k]) for k, out in enumerate(outs)
    ]
    for copy in sent:
        copy.start()
    for copy in sent:
        copy.wait()


def blur(info, momenta, halo, other):
    rows = VROWS
    return pl.pallas_call(
        blur_kernel,
        grid=(),
        in_specs=[
            pl.BlockSpec(memory_space=pltpu.SMEM),
            pl.BlockSpec(memory_space=pl.ANY),
            pl.BlockSpec(memory_space=pl.ANY),
            pl.BlockSpec(memory_space=pl.ANY),
        ],
        out_specs=[pl.BlockSpec(memory_space=pl.ANY)] * 8,
        out_shape=[jax.ShapeDtypeStruct((rows, 128), BF16)] * 8,
        scratch_shapes=[
            pltpu.VMEM((2, 12, 3, 96, 96), F32),
            pltpu.VMEM((8, rows, 128), BF16),
            pltpu.VMEM((CZ, 112, 128), F32),
            pltpu.VMEM((CZ, 112, 128), F32),
            pltpu.VMEM((CZ, 96, 128), F32),
            pltpu.VMEM((VR, 128), F32),
            pltpu.SemaphoreType.DMA((3,)),
            pltpu.SemaphoreType.DMA((8,)),
        ],
        name="blur_momenta",
    )(info, momenta, halo, other)


def edge_kernel(*refs):
    planes, below, above = refs[:8], refs[8], refs[9]
    low, high, sems, gone = refs[10:]
    copies = []
    for k, plane in enumerate(planes):
        copies.append(pltpu.make_async_copy(plane.at[0], low.at[k], sems.at[k]))
        copies.append(pltpu.make_async_copy(plane.at[HZ - 1], high.at[k], sems.at[8 + k]))
    for copy in copies:
        copy.start()
    for copy in copies:
        copy.wait()
    leaving = [
        pltpu.make_async_copy(low, below, gone.at[0]),
        pltpu.make_async_copy(high, above, gone.at[1]),
    ]
    for copy in leaving:
        copy.start()
    for copy in leaving:
        copy.wait()


def edges(planes):
    hbm = pl.BlockSpec(memory_space=pl.ANY)
    shape = (8, PROWS, 128)
    return pl.pallas_call(
        edge_kernel,
        grid=(),
        in_specs=[hbm] * 8,
        out_specs=[hbm] * 2,
        out_shape=[jax.ShapeDtypeStruct(shape, BF16)] * 2,
        scratch_shapes=[
            pltpu.VMEM(shape, BF16),
            pltpu.VMEM(shape, BF16),
            pltpu.SemaphoreType.DMA((16,)),
            pltpu.SemaphoreType.DMA((2,)),
        ],
        name="cut_edges",
    )(*planes)


def warp_kernel(info, assign, zy, x0, x1, *rest):
    planes, fields, below, above = rest[:8], rest[8:16], rest[16], rest[17]
    chunk, edge = rest[18:20]
    image, field, even, odd, acc, sems = rest[20:]
    level, me = info[0], info[1]
    copies = [
        pltpu.make_async_copy(below, image.at[:, 0], sems.at[16]),
        pltpu.make_async_copy(above, image.at[:, HZ + 1], sems.at[17]),
    ]
    for k in range(8):
        copies.append(
            pltpu.make_async_copy(planes[k], image.at[k, 1 : HZ + 1], sems.at[k])
        )
    first = [pltpu.make_async_copy(fields[k], field.at[k], sems.at[8 + k]) for k in range(8)]
    for copy in first + copies:
        copy.start()
    acc[...] = jnp.zeros_like(acc)
    for copy in first:
        copy.wait()
    lane = lax.broadcasted_iota(jnp.int32, (CY, 128), 1)
    sub = lax.broadcasted_iota(jnp.int32, (CY, 128), 0)
    coarse_lane = lax.broadcasted_iota(jnp.int32, (VR, 128), 1)

    def neighbours(part):
        left0, left1, left2 = (pltpu.roll(p, 1, 1) for p in part)
        right0, right1, right2 = (pltpu.roll(p, 127, 1) for p in part)
        left2 = jnp.where(lane == 0, left0, jnp.where(lane == 64, pltpu.roll(part[1], 65, 1), left2))
        left0 = jnp.where(lane == 0, 0.0, left0)
        left1 = jnp.where(lane == 0, 0.0, left1)
        right0 = jnp.where(lane == 127, right2, right0)
        right1 = jnp.where(lane == 127, pltpu.roll(part[2], 63, 1), right1)
        right2 = jnp.where(lane % 64 == 63, 0.0, right2)
        return (left0, left1, left2), (right0, right1, right2)

    def interpolate(k, velocity):
        base = 2 * (me ^ k)
        slots = [(assign[base + j] // 2) ^ me for j in range(2)]
        stacked = [[], []]
        for c in range(3):
            parts = [field[slots[0], VR * c : VR * (c + 1)]]
            if c > 0:
                parts.append(field[slots[1], VR * (c + 2) : VR * (c + 3)])
            else:
                spread = [
                    pltpu.roll(
                        field[slots[1], VR * t : VR * (t + 1)].astype(F32), 32 * t + 32, 1
                    )
                    for t in range(3)
                ]
                third = jnp.where(
                    coarse_lane < 32, spread[0], jnp.where(coarse_lane < 64, spread[1], spread[2])
                )
                parts.append(third.astype(BF16))
            rough = jnp.dot(
                zy[...], jnp.concatenate(parts, axis=1), preferred_element_type=F32
            )
            high = rough.astype(BF16)
            low = (rough - high.astype(F32)).astype(BF16)
            for j in range(2):
                own = slice(128 * j, 128 * j + 128)
                stacked[j].append(jnp.concatenate([high[:, own], low[:, own]], axis=1))
        fine = [
            jnp.dot(jnp.concatenate(stacked[j], axis=0), table[...], preferred_element_type=F32)
            for j, table in enumerate((x0, x1))
        ]
        velocity[0] = fine[0][:, :128]
        velocity[1] = fine[1][:, :128]
        velocity[2] = fine[0][:, 128:] + fine[1][:, 128:]

    def apply(k, velocity):
        for z in range(HZ):
            before = image[k, z].astype(F32)
            centre = image[k, z + 1].astype(F32)
            after = image[k, z + 2].astype(F32)
            part = [centre[CY * b : CY * (b + 1)] for b in range(3)]
            halo = centre[3 * CY :]
            left, right = neighbours(part)
            warped = []
            for b in range(3):
                own = slice(CY * b, CY * (b + 1))
                up = jnp.where(sub == 0, halo[2 * b : 2 * b + 1], pltpu.roll(part[b], 1, 0))
                down = jnp.where(
                    sub == CY - 1, halo[2 * b + 1 : 2 * b + 2], pltpu.roll(part[b], CY - 1, 0)
                )

                def v(c):
                    start = HZ * CY * c + CY * z
                    return velocity[b, start : start + CY]

                push = v(0) * (right[b] - left[b]) + v(1) * (down - up)
                push += v(2) * (after[own] - before[own])
                warped.append(part[b] - 0.5 * push)
            rows = slice(CY * z, CY * (z + 1))
            acc[0, rows] += warped[0] + warped[1]
            acc[1, rows] += warped[2]

    interpolate(0, even)
    for copy in copies:
        copy.wait()

    def turn(step, carry):
        interpolate(2 * step + 1, odd)
        apply(2 * step, even)
        interpolate(jnp.minimum(2 * step + 2, 7), even)
        apply(2 * step + 1, odd)
        return carry

    lax.fori_loop(0, 4, turn, 0)
    weight = SCALE / 16.0
    chunk[: HZ * CY] = pltpu.roll(acc[0] * weight, 64 * level, 1)
    wide = lax.broadcasted_iota(jnp.int32, (CY, 128), 1)

    def joined(z, other):
        one, two = (acc[1, pl.ds(pl.multiple_of(r * CY, 8), CY)] for r in (z, other))
        one = one + pltpu.roll(one, 64, 1)
        two = two + pltpu.roll(two, 64, 1)
        return jnp.where(wide < 64, one, two) * weight

    for z in range(HZ // 2):
        chunk[(HZ + z) * CY : (HZ + z + 1) * CY] = joined(z, z + HZ // 2)
    outer = (HZ - 2) * level
    rim = acc[0, pl.ds(pl.multiple_of(outer * CY, 8), 2 * CY)] * weight
    edge[: 2 * CY] = pltpu.roll(rim, 64 - 64 * level, 1)
    edge[2 * CY :] = joined(outer, outer + 1)


def warp(info, assign, planes, fields, below, above):
    tables = [
        jnp.asarray(t, BF16) for t in (zy_table(), x_table(192, 0), x_table(192, 1))
    ]
    vmem = pl.BlockSpec(memory_space=pltpu.VMEM)
    smem = pl.BlockSpec(memory_space=pltpu.SMEM)
    hbm = pl.BlockSpec(memory_space=pl.ANY)
    return pl.pallas_call(
        warp_kernel,
        grid=(),
        in_specs=[smem, smem, vmem, vmem, vmem] + [hbm] * 18,
        out_specs=[vmem] * 2,
        out_shape=[
            jax.ShapeDtypeStruct((HZ * CY * 3 // 2, 128), F32),
            jax.ShapeDtypeStruct((3 * CY, 128), F32),
        ],
        scratch_shapes=[
            pltpu.VMEM((8, HZ + 2, PROWS, 128), BF16),
            pltpu.VMEM((8, VROWS, 128), BF16),
            pltpu.VMEM((3, 3 * HZ * CY, 128), F32),
            pltpu.VMEM((3, 3 * HZ * CY, 128), F32),
            pltpu.VMEM((2, HZ * CY, 128), F32),
            pltpu.SemaphoreType.DMA((18,)),
        ],
        name="warp_sum",
    )(info, assign, *tables, *planes, *fields, below, above)


def relax_kernel(
    info, source, out, chunks, flat, pair, flat2, pair2, even, odd, ready, sems, arriving
):
    level, me, zone = info[0], info[1], info[2]
    size = flat.shape[1] - 16
    copies = []
    for peer in range(8):
        for half in range(2):
            slot = (half ^ level) * 8 + (peer ^ me)
            copies.append(
                pltpu.make_async_copy(source.at[slot], chunks.at[slot], arriving.at[slot])
            )
    for copy in copies:
        copy.start()
    for held in (flat, pair, flat2, pair2):
        held[:, :8] = jnp.zeros((held.shape[0], 8, 128), F32)
        held[:, size + 8 :] = jnp.zeros((held.shape[0], 8, 128), F32)
    for held in (flat, flat2):
        for z in (0, held.shape[0] - 1):
            held[z, 8 : 8 + size] = jnp.zeros((size, 128), F32)
    narrow = lax.broadcasted_iota(jnp.int32, (CY, 128), 1)
    tail = HZ * 3 // 2
    for peer in range(8):
        rows = slice(8 + CY * peer, 8 + CY * (peer + 1))
        for copy in copies[2 * peer : 2 * peer + 2]:
            copy.wait()

        def block(half, index):
            slot = (half ^ level) * 8 + (peer ^ me)
            return chunks[slot, CY * index : CY * (index + 1)]

        for half in range(2):
            for z in range(HZ):
                flat[3 + 14 * half + z, rows] = block(half, z)
            for z in range(2):
                flat[1 + 28 * half + z, rows] = block(half, tail + z)
        packed = [HZ + z % (HZ // 2) for z in range(HZ)]
        sides = [z // (HZ // 2) for z in range(HZ)]
        lows = [(tail + 2, 0), (tail + 2, 1)] + list(zip(packed, sides))
        highs = list(zip(packed, sides)) + [(tail + 2, 0), (tail + 2, 1)]
        for index in range(14):
            low, high = block(0, lows[index][0]), block(1, highs[index][0])
            if lows[index][1] == 1:
                low = pltpu.roll(low, 64, 1)
            if highs[index][1] == 0:
                high = pltpu.roll(high, 64, 1)
            pair[1 + index, rows] = jnp.where(narrow < 64, low, high)

    def mirror(planes, both):
        body = slice(8, 8 + size)
        both[0, body] = pltpu.roll(both[14, body], 64, 1)
        both[15, body] = pltpu.roll(both[1, body], 64, 1)
        planes[16, body] = pltpu.roll(planes[14, body], 64, 1)
        planes[15, body] = pltpu.roll(planes[17, body], 64, 1)

    mirror(flat, pair)
    count = 2 * CY
    lane = lax.broadcasted_iota(jnp.int32, (count, 128), 1)

    def shift(planes, index, sums):
        for start in range(8, 8 + size, count):
            refs = [(planes[0], index), (planes[0], index + 16), (planes[1], index)]
            part = [held[z, start : start + count] for held, z in refs]
            left = [pltpu.roll(p, 1, 1) for p in part]
            right = [pltpu.roll(p, 127, 1) for p in part]
            left[2] = jnp.where(lane == 0, left[0], jnp.where(lane == 64, left[1], left[2]))
            left[0] = jnp.where(lane == 0, 0.0, left[0])
            left[1] = jnp.where(lane == 64, 0.0, left[1])
            right[0] = jnp.where(lane == 127, right[2], right[0])
            right[1] = jnp.where(lane == 63, right[2], right[1])
            right[2] = jnp.where(lane % 64 == 63, 0.0, right[2])
            for b in range(3):
                sums[b, start - 8 : start - 8 + count] = left[b] + right[b]

    def swept(planes, index, sums, start, scale):
        refs = [(planes[0], index), (planes[0], index + 16), (planes[1], index)]
        done = []
        for b, (held, z) in enumerate(refs):
            around = held[z - 1, start : start + count] + held[z + 1, start : start + count]
            around += held[z, start - 1 : start - 1 + count] + held[z, start + 1 : start + 1 + count]
            around += sums[b, start - 8 : start - 8 + count]
            value = around + (2.0 / 3.0) * held[z, start : start + count]
            done.append(value if scale is None else scale * value)
        return done

    def sweep(planes, store, scale, after):
        shift(planes, 1, even)

        def turn(step, carry):
            index = 2 * step + 1
            shift(planes, index + 1, odd)
            for start in range(8, 8 + size, count):
                store(index, start, swept(planes, index, even, start, scale))
            shift(planes, jnp.minimum(index + 2, 14), even)
            for start in range(8, 8 + size, count):
                store(index + 1, start, swept(planes, index + 1, odd, start, scale))
            after(index)
            after(index + 1)
            return carry

        lax.fori_loop(0, 7, turn, 0)

    def first(index, start, done):
        flat2[index, start : start + count] = done[0]
        flat2[index + 16, start : start + count] = done[1]
        pair2[index, start : start + count] = done[2]

    sweep((flat, pair), first, None, lambda index: None)
    whole = lax.broadcasted_iota(jnp.int32, (size, 128), 1)

    @pl.when(zone == 0)
    def _():
        flat2[2, 8 : 8 + size] = jnp.zeros((size, 128), F32)
        pair2[2, 8 : 8 + size] = jnp.where(whole < 64, 0.0, pair2[2, 8 : 8 + size])

    @pl.when(zone == 7)
    def _():
        flat2[29, 8 : 8 + size] = jnp.zeros((size, 128), F32)
        pair2[13, 8 : 8 + size] = jnp.where(whole < 64, pair2[13, 8 : 8 + size], 0.0)

    mirror(flat2, pair2)

    def emit(z):
        return pltpu.make_async_copy(ready.at[z + 2], out.at[z], sems.at[z])

    def second(index, start, done):
        rows = slice(start - 8, start - 8 + count)
        ready[index - 1, rows, :128] = done[0]
        ready[index - 1, rows, 128:] = done[2][:, :64]
        ready[index + 13, rows, :128] = pltpu.roll(done[1], 64, 1)
        ready[index + 13, rows, 128:] = pltpu.roll(done[2], 64, 1)[:, :64]

    def depart(index):
        @pl.when(index >= 3)
        def _():
            emit(index - 3).start()

        @pl.when(index <= 12)
        def _():
            emit(index + 11).start()

    sweep((flat2, pair2), second, 0.15 * 0.15 / SCALE, depart)

    def finish(z, carry):
        emit(z).wait()
        return carry

    lax.fori_loop(0, 24, finish, 0)


def relax(info, chunks):
    hbm = pl.BlockSpec(memory_space=pl.ANY)
    return pl.pallas_call(
        relax_kernel,
        grid=(),
        in_specs=[pl.BlockSpec(memory_space=pltpu.SMEM), hbm],
        out_specs=pl.BlockSpec(memory_space=pl.ANY),
        out_shape=jax.ShapeDtypeStruct((24, 192, 192), F32),
        scratch_shapes=[
            pltpu.VMEM(chunks.shape, F32),
            pltpu.VMEM((32, 208, 128), F32),
            pltpu.VMEM((16, 208, 128), F32),
            pltpu.VMEM((32, 208, 128), F32),
            pltpu.VMEM((16, 208, 128), F32),
            pltpu.VMEM((3, 192, 128), F32),
            pltpu.VMEM((3, 192, 128), F32),
            pltpu.VMEM((28, 192, 192), F32),
            pltpu.SemaphoreType.DMA((24,)),
            pltpu.SemaphoreType.DMA((16,)),
        ],
        name="relax",
    )(info, chunks)


def update(images, momenta, assign):
    level = lax.axis_index("level")
    me = lax.axis_index("subj")
    zone = lax.axis_index("gz")
    info = jnp.stack([level, me, zone]).astype(jnp.int32)
    zones = lax.axis_size("gz")
    outward = [(g, g + 1) for g in range(zones - 1)]
    outward += [(zones + g + 1, zones + g) for g in range(zones - 1)]
    nearest = ("level", "gz")
    cross = [(zones + g, g + 1) for g in range(zones - 1)]
    cross += [(g + 1, zones + g) for g in range(zones - 1)]
    climb = [(g, zones + g) for g in range(zones)]
    climb += [(zones + g, g + 1) for g in range(zones - 1)]
    part = (1, 3) + momenta.shape[2:]
    rim = lax.dynamic_slice(momenta, (0, 9 * (1 - level), 0, 0, 0), part)
    other = lax.dynamic_slice(momenta, (1, 9 * level, 0, 0, 0), part)
    rim = lax.ppermute(rim, nearest, outward)
    other = lax.ppermute(other, nearest, cross)

    def spread(parts):
        arrived = {0: parts[0]}
        for k in SPREAD:
            arrived[k] = lax.ppermute(parts[k], "subj", [(i, i ^ k) for i in range(8)])
        return [arrived[k] for k in range(8)]

    packed = pack_images(info, images)
    planes = spread(packed)
    blurred = blur(info, momenta, rim, other)
    fields = spread(blurred)
    low, high = edges(planes)
    below = lax.ppermute(high, nearest, climb)
    above = lax.ppermute(low, nearest, [(b, a) for a, b in climb])
    chunk, edge = warp(info, assign, planes, fields, below, above)
    edge = lax.ppermute(edge.astype(jnp.float16), nearest, cross)
    chunk = jnp.concatenate([chunk.astype(jnp.float16), edge], axis=0)
    gathered = []
    for far in range(2):
        for step in range(4):
            part = chunk
            if far or step:
                perm = [
                    (8 * a + i, 8 * (a ^ far) + (i ^ (2 * step))) for a in range(2) for i in range(8)
                ]
                part = lax.ppermute(chunk, ("level", "subj"), perm)
            gathered += [part, lax.ppermute(part, "subj", [(i, i ^ 1) for i in range(8)])]
    chunks = jnp.stack(gathered).astype(F32)
    return relax(info, chunks)


def solution(mesh):
    return jax.shard_map(
        update,
        mesh=mesh,
        in_specs=(P("subj", "gz", None, None), P("subj", "gz", None, None, None), P()),
        out_specs=P("gz", None, None),
        check_vma=False,
    )
```
